32 devices in a mesh: seq: 8 (over y, x, core), head: 4 (over z).
Axes of the slice: x: 2, y: 2, z: 4, core: 2. Of those that a mesh axis runs over, the one named last changes fastest.
Arguments:
- out_grad: bfloat16 [2048, 4096], P('seq', 'head'), may hold values from -7.2 to 7.2
- x_in: bfloat16 [2048, 4096], P('seq', 'head'), may hold values from -6 to 6
- b_in: bfloat16 [2048, 128], P('seq'), may hold values from -2.5 to 2.5
- c_in: bfloat16 [2048, 128], P('seq'), may hold values from -2.5 to 2.5
- dt_raw: float32 [64, 2048], P('head', 'seq'), may hold values from -5.1 to -0.7
- dt_bias: float32 [64], P('head'), may hold values from -0.5 to 0.5
- a_log: float32 [64], P('head'), may hold values from -7.5 to 2.2
- d_skip: float32 [64], P('head'), may hold values from 0.5 to 1.5
- states: bfloat16 [8, 4096, 128], P('seq', 'head'), may hold values from -6 to 6
- w_out: bfloat16 [4096, 4096], P('head'), may hold values from -0.09375 to 0.09375
- w_in: bfloat16 [4096, 4096], P(None, 'head'), may hold values from -0.125 to 0.125
Outputs:
- in_grad: bfloat16 [4096, 2048], P('head', 'seq')
- bc_grad: bfloat16 [256, 2048], P('head', 'seq')
- dt_grad: float32 [64, 2048], P('head', 'seq')
- param_grad: float32 [3, 64], P(None, 'head')
The draws below stay inside these ranges and needn't reach their ends.
All inputs are finite; a program needn't handle non-finite values.
Results may differ from the reference program's by a relative error of at most 0.015.
Values may be sent and summed in bfloat16 or wider, within the bound.
A program may use at most 64 MiB of HBM per device.

```python
import jax
import jax.numpy as jnp
from jax import lax

D = 4096
HEADS = 64
HDIM = 64
STATE = 128
SPAN = 256
TOKENS = 2048
INNER = 4096
GROUP_HEADS = 16
N_HEAD = 4


def draw_out_grad(key, part):
    position = jnp.arange(TOKENS, dtype=jnp.float32) / max(TOKENS - 1, 1)
    base_draw = jnp.clip(jax.random.normal(key, (TOKENS, D), jnp.float32), -4.0, 4.0)
    growth = 0.6 * 3.0 ** position
    return (base_draw * growth[:, None]).astype(jnp.bfloat16)


def draw_a_log(key, part):
    key_order, key_slow, key_fast = jax.random.split(jax.random.fold_in(key, 11), 3)
    ranking = jax.random.permutation(key_order, HEADS)
    slow_head = ranking < HEADS // 2
    slow_rate = jax.random.uniform(key_slow, (HEADS,), jnp.float32, 0.3, 1.5) / (TOKENS * 0.06)
    fast_rate = jax.random.uniform(key_fast, (HEADS,), jnp.float32, 0.7, 1.4) * 6.0 / (SPAN * 0.06)
    return jnp.log(jnp.where(slow_head, slow_rate, fast_rate))


def draw_dt_raw(key, part):
    key_jitter, key_block = jax.random.split(jax.random.fold_in(key, 23))
    blocks = TOKENS // SPAN
    offset = jax.random.uniform(key_block, (HEADS, blocks, 1), jnp.float32, -0.7, 0.7)
    jitter = jnp.clip(0.5 * jax.random.normal(key_jitter, (HEADS, blocks, SPAN), jnp.float32), -1.5, 1.5)
    return (-2.9 + offset + jitter).reshape(HEADS, TOKENS)


def strengthened(values, key, source, target, parts, factor):
    def block_of(axis_at):
        return (jnp.arange(values.shape[axis_at]) // (values.shape[axis_at] // parts)).reshape((-1,) + (1,) * (values.ndim - 1 - axis_at))

    near = jax.random.permutation(key, parts)[block_of(target)]
    second = (block_of(target) + parts // 2) % parts
    return jnp.where((block_of(source) == near) | (block_of(source) == second), factor * values, values)


def steps_of(stream_key, extent, cuts, smallest, largest):
    gain, own = 1.0, jax.random.fold_in(stream_key, 6)
    for dim, shards_of in cuts:
        heights = jnp.exp(jax.random.uniform(jax.random.fold_in(own, dim), (shards_of,), jnp.float32, smallest / len(cuts), largest / len(cuts)))
        gain = gain * jnp.repeat(heights, extent[dim] // shards_of).reshape([-1 if axis == dim else 1 for axis in range(len(extent))])
    return gain


def gaussian(stream_key, extent, width, limit, pieces=(), held_as=jnp.bfloat16):
    array = width * jax.random.normal(stream_key, extent, jnp.float32)
    if pieces:
        array = array * steps_of(stream_key, extent, pieces, -0.22, 0.18)
    return jnp.clip(array, -limit, limit).astype(held_as)


def bell_draw_with(stream_key, dims, spread, most, shards, heavy, kind=jnp.bfloat16):
    entries = spread * jax.random.normal(stream_key, dims, jnp.float32)
    if shards:
        entries = entries * steps_of(stream_key, dims, shards, -0.22, 0.18)
    return jnp.clip(strengthened(entries, jax.random.fold_in(stream_key, 3), *heavy), -most, most).astype(kind)


def setup_inputs(seed: int = 0) -> dict:
    key_list = jax.random.split(jax.random.key(seed), 12)
    out_grad = draw_out_grad(jax.random.fold_in(key_list[11], 71), 0)
    x_in = gaussian(key_list[1], (TOKENS, INNER), 1.0, 6.0, ((0, 8), (1, 4)))
    b_in = gaussian(key_list[2], (TOKENS, STATE), 0.3, 2.5, ((0, 8),))
    c_in = gaussian(key_list[3], (TOKENS, STATE), 0.3, 2.5, ((0, 8),))
    dt_raw = draw_dt_raw(jax.random.fold_in(key_list[11], 71), 0)
    dt_bias = jnp.clip(jax.random.uniform(key_list[5], (HEADS,), jnp.float32, -0.5, 0.5) * steps_of(key_list[5], (HEADS,), ((0, 4),), -0.4, 0.0), -0.5, 0.5)
    a_log = draw_a_log(jax.random.fold_in(key_list[11], 71), 0)
    d_skip = jnp.clip(0.5 + 1.0 * jax.random.uniform(key_list[7], (HEADS,), jnp.float32) ** steps_of(key_list[7], (HEADS,), ((0, 4),), -0.2, 0.2), 0.5, 1.5)
    states = gaussian(key_list[8], (TOKENS // SPAN, INNER, STATE), 1.0, 6.0, ((0, 8), (1, 4)))
    w_out = gaussian(key_list[9], (INNER, D), INNER ** -0.5, 0.09375, ((0, 4),))
    w_in = bell_draw_with(key_list[10], (D, INNER), D ** -0.5, 0.125, ((1, 4),), (1, 0, 4, 2.0))
    return dict(out_grad=out_grad, x_in=x_in, b_in=b_in, c_in=c_in, dt_raw=dt_raw, dt_bias=dt_bias, a_log=a_log, d_skip=d_skip, states=states, w_out=w_out, w_in=w_in)


def rounded(values):
    return lax.optimization_barrier(values.astype(jnp.bfloat16)).astype(jnp.float32)


def reference(out_grad, x_in, b_in, c_in, dt_raw, dt_bias, a_log, d_skip, states, w_out, w_in):
    blocks = TOKENS // SPAN
    head_grad = jnp.dot(out_grad, w_out.T, preferred_element_type=jnp.float32).astype(jnp.bfloat16)
    decay_rate = jnp.exp(a_log)
    step_size = jax.nn.softplus(dt_raw + dt_bias[:, None])
    x_blocks = x_in.astype(jnp.float32).reshape(blocks, SPAN, HEADS, HDIM)
    dy_blocks = head_grad.astype(jnp.float32).reshape(blocks, SPAN, HEADS, HDIM)
    b_blocks = b_in.reshape(blocks, SPAN, STATE)
    c_blocks = c_in.reshape(blocks, SPAN, STATE)
    step_blocks = step_size.reshape(HEADS, blocks, SPAN).transpose(1, 0, 2)
    raw_blocks = dt_raw.reshape(HEADS, blocks, SPAN).transpose(1, 0, 2)
    entry_blocks = states.astype(jnp.float32).reshape(blocks, HEADS, HDIM, STATE)
    causal = jnp.arange(SPAN)[:, None] >= jnp.arange(SPAN)[None, :]

    def front(items):
        dy_heads, c_block, step_block = items
        cumlog = jnp.cumsum(-decay_rate[:, None] * step_block, axis=1)
        dy_decay = rounded(dy_heads * jnp.exp(cumlog).T[:, :, None])
        local_state = jnp.einsum('ihp,in->hpn', dy_decay, c_block.astype(jnp.float32))
        return local_state, jnp.exp(cumlog[:, -1])

    local_states, end_totals = lax.map(front, (dy_blocks, c_blocks, step_blocks))

    def carry_step(held_state, items):
        local_state, end_total = items
        return end_total[:, None, None] * held_state + local_state, held_state

    final_state, carried = lax.scan(carry_step, jnp.zeros((HEADS, HDIM, STATE), jnp.float32), (local_states, end_totals), reverse=True)

    def back(items):
        x_heads, dy_heads, b_block, c_block, step_block, raw_block, entry_state, held_state = items
        b_wide = b_block.astype(jnp.float32)
        c_wide = c_block.astype(jnp.float32)
        log_step = -decay_rate[:, None] * step_block
        cumlog = jnp.cumsum(log_step, axis=1)
        log_gaps = cumlog[:, :, None] - cumlog[:, None, :]
        decay_mask = jnp.where(causal[None], jnp.exp(jnp.minimum(log_gaps, 0.0)), 0.0)
        scores = jnp.dot(c_block, b_block.T, preferred_element_type=jnp.float32)
        step_rows = step_block.T
        x_scaled = rounded(x_heads * step_rows[:, :, None])
        pair_dots = jnp.einsum('ihp,jhp->hij', dy_heads, x_scaled)
        kernel = rounded(scores[None] * decay_mask)
        intra_back = jnp.einsum('hij,ihp->jhp', kernel, dy_heads)
        masked_dots = rounded(pair_dots * decay_mask)
        start_decay = jnp.exp(cumlog)
        dy_decay = rounded(dy_heads * start_decay.T[:, :, None])
        carried_bf = rounded(held_state)
        state_back = jnp.einsum('jn,hpn->jhp', b_wide, carried_bf)
        end_decay = jnp.exp(cumlog[:, -1:] - cumlog)
        end_weight = (step_block * end_decay).T
        x_grad = (step_rows[:, :, None] * intra_back + end_weight[:, :, None] * state_back + d_skip[None, :, None] * dy_heads).astype(jnp.bfloat16)
        x_end = rounded(x_heads * end_weight[:, :, None])
        db_heads = jnp.einsum('hij,in->hjn', masked_dots, c_wide) + jnp.einsum('jhp,hpn->hjn', x_end, carried_bf)
        dc_heads = jnp.einsum('hij,jn->hin', masked_dots, b_wide) + jnp.einsum('ihp,hpn->hin', dy_decay, entry_state)
        db_groups = rounded(db_heads.reshape(N_HEAD, GROUP_HEADS, SPAN, STATE).sum(axis=1)).sum(axis=0)
        dc_groups = rounded(dc_heads.reshape(N_HEAD, GROUP_HEADS, SPAN, STATE).sum(axis=1)).sum(axis=0)
        bc_block = jnp.concatenate([db_groups.T, dc_groups.T], axis=0)
        ystate = jnp.einsum('in,hpn->ihp', c_wide, entry_state)
        pair_weight = pair_dots * scores[None] * decay_mask
        state_terms = start_decay * jnp.sum(dy_heads * ystate, axis=2).T
        end_terms = end_weight.T * jnp.sum(x_heads * state_back, axis=2).T
        cum_grad = pair_weight.sum(axis=2) - pair_weight.sum(axis=1) + state_terms - end_terms
        tail_grad = end_terms.sum(axis=1) + jnp.exp(cumlog[:, -1]) * jnp.sum(entry_state * held_state, axis=(1, 2))
        cum_grad = cum_grad.at[:, -1].add(tail_grad)
        step_grad = jnp.cumsum(cum_grad[:, ::-1], axis=1)[:, ::-1]
        dt_sum = -decay_rate[:, None] * step_grad + jnp.sum(x_heads * (intra_back + end_decay.T[:, :, None] * state_back), axis=2).T
        dt_grad = dt_sum * jax.nn.sigmoid(raw_block + dt_bias[:, None])
        param_terms = jnp.stack([jnp.sum(step_grad * log_step, axis=1), jnp.sum(dy_heads * x_heads, axis=(0, 2)), jnp.sum(dt_grad, axis=1)])
        return x_grad, bc_block, dt_grad, param_terms

    x_grads, bc_blocks, dt_blocks, param_blocks = lax.map(back, (x_blocks, dy_blocks, b_blocks, c_blocks, step_blocks, raw_blocks, entry_blocks, carried))
    x_grad = x_grads.reshape(TOKENS, HEADS * HDIM)
    bc_grad = bc_blocks.transpose(1, 0, 2).reshape(2 * STATE, TOKENS).astype(jnp.bfloat16)
    dt_grad = dt_blocks.transpose(1, 0, 2).reshape(HEADS, TOKENS)
    param_grad = param_blocks.sum(axis=0) * (TOKENS * HDIM) ** -0.5
    group_width = GROUP_HEADS * HDIM
    running = jnp.zeros((D, TOKENS), jnp.float32)
    for group_index in range(N_HEAD):
        w_cols = w_in[:, group_index * group_width:(group_index + 1) * group_width]
        x_cols = x_grad[:, group_index * group_width:(group_index + 1) * group_width]
        running = running + rounded(jnp.dot(w_cols, x_cols.T, preferred_element_type=jnp.float32))
    return running.astype(jnp.bfloat16), bc_grad, dt_grad, param_grad
```

```python
import functools

import jax
import jax.numpy as jnp
from jax import lax
from jax.experimental import pallas as pl
from jax.experimental.pallas import tpu as pltpu
from jax.sharding import PartitionSpec as P


def partners(count, distance):
    return [(place, place ^ distance) for place in range(count)]


def entering(decay, state, axis, beside):
    count, mine = (lax.axis_size(axis), lax.axis_index(axis))
    carried = jnp.zeros_like(state)
    reach = jnp.ones_like(decay)
    distance = 1
    while distance < count:
        pairs = partners(count, distance)
        other_decay = lax.ppermute(decay, axis, pairs)
        other_state = lax.ppermute(state.astype(jnp.bfloat16), axis, pairs)
        if distance == 1:
            other_state, beside = lax.optimization_barrier((other_state, beside))
        other_state = other_state.astype(jnp.float32)
        earlier = (mine // distance) % 2 == 0
        carried = jnp.where(earlier, carried + reach[:, None, None] * other_state, carried)
        reach = jnp.where(earlier, reach * other_decay, reach)
        state = jnp.where(
            earlier,
            state + decay[:, None, None] * other_state,
            other_state + other_decay[:, None, None] * state,
        )
        decay = decay * other_decay
        distance *= 2
    return carried, beside


LAST = (((1,), (1,)), ((), ()))
MESH = pl.DeviceIdType.MESH
CHUNKS = 2


def tile_of(extent):
    return 256 if extent % 256 == 0 else extent


def ring_copy(src, dst, sems, way, step, target):
    return pltpu.make_async_remote_copy(
        src_ref=src,
        dst_ref=dst,
        send_sem=sems[0].at[way, step],
        recv_sem=sems[1].at[way, step],
        device_id={"head": target},
        device_id_type=MESH,
    )


def gather_matmul_kernel(n, x_ref, w_hbm, o_ref, held, w_ref, total, send_sem, recv_sem, w_sem):
    me = lax.axis_index("head")
    right, left = (lax.rem(me + 1, n), lax.rem(me + n - 1, n))
    tokens, depth = x_ref.shape
    half = tokens // 2
    width = o_ref.shape[1]
    tile = tile_of(width)

    def columns(offset):
        owner = lax.rem(me + offset, n)
        return pl.ds(pl.multiple_of(owner * depth, depth), depth)

    def w_copy(offset):
        where = columns(offset)
        return pltpu.make_async_copy(w_hbm.at[:, where], w_ref.at[:, where], w_sem.at[offset])

    barrier = pltpu.get_barrier_semaphore()
    for neighbour in (left, right):
        pl.semaphore_signal(barrier, inc=1, device_id={"head": neighbour}, device_id_type=MESH)
    pl.semaphore_wait(barrier, 2)
    sems = (send_sem, recv_sem)
    order = []
    for step in range(n):
        for offset in ((n - step) % n, step):
            if offset not in order:
                order.append(offset)
    loaded = set()
    sent = {}
    for step in range(n):
        for chunk in range(CHUNKS):
            for way, target in ((0, right), (1, left)):
                lane = way * CHUNKS + chunk
                rows = pl.ds(lane * (half // CHUNKS), half // CHUNKS)
                if step > 0:
                    sent[step - 1, lane].wait_recv()
                if step < n - 1:
                    source = x_ref.at[rows] if step == 0 else held.at[step - 1, rows]
                    copy = ring_copy(source, held.at[step, rows], sems, lane, step, target)
                    copy.start()
                    sent[step, lane] = copy
        if step == 0:
            for offset in order:
                w_copy(offset).start()
        for way in (0, 1):
            offset = (n - step) % n if way == 0 else step
            if offset not in loaded:
                w_copy(offset).wait()
                loaded.add(offset)
            where = columns(offset)
            rows = pl.ds(way * half, half)
            source = x_ref.at[rows] if step == 0 else held.at[step - 1, rows]

            def multiply(index, carry):
                outs = pl.ds(pl.multiple_of(index * tile, tile), tile)
                part = lax.dot_general(
                    source[...], w_ref[outs, where], LAST, preferred_element_type=jnp.float32
                )
                if step > 0:
                    part = part + total[rows, outs]
                if step < n - 1:
                    total[rows, outs] = part
                else:
                    o_ref[rows, outs] = part.astype(o_ref.dtype)
                return carry

            lax.fori_loop(0, width // tile, multiply, 0)
    for copy in sent.values():
        copy.wait_send()


def gather_matmul(x, w):
    n = lax.axis_size("head")
    tokens, depth = x.shape
    width = w.shape[0]
    vmem = pl.BlockSpec(memory_space=pltpu.VMEM)
    return pl.pallas_call(
        functools.partial(gather_matmul_kernel, n),
        out_shape=jax.ShapeDtypeStruct((tokens, width), jnp.bfloat16),
        in_specs=[vmem, pl.BlockSpec(memory_space=pltpu.HBM)],
        out_specs=vmem,
        scratch_shapes=[
            pltpu.VMEM((n - 1, tokens, depth), jnp.bfloat16),
            pltpu.VMEM(w.shape, jnp.bfloat16),
            pltpu.VMEM((tokens, width), jnp.float32),
            pltpu.SemaphoreType.DMA((2 * CHUNKS, n - 1)),
            pltpu.SemaphoreType.DMA((2 * CHUNKS, n - 1)),
            pltpu.SemaphoreType.DMA((n,)),
        ],
        compiler_params=pltpu.CompilerParams(
            collective_id=0, has_side_effects=True, vmem_limit_bytes=52 * 2**20
        ),
        name="gather_matmul",
    )(x, w)


def matmul_scatter_kernel(
    n, s, w_hbm, x_ref, bc_ref, p_ref, o_ref, obc_ref, op_ref,
    w_ref, going, coming, p_in, send_sem, recv_sem, w_sem, p_send, p_recv,
):
    me = lax.axis_index("head")
    mine = lax.axis_index("seq")
    right, left = (lax.rem(me + 1, n), lax.rem(me + n - 1, n))
    rows_here = o_ref.shape[0]
    half = rows_here // 2
    bc_half = obc_ref.shape[0] // 2
    piece = half // CHUNKS
    tile = tile_of(piece)

    def owner_of(way, step):
        return lax.rem(me + 2 * n - 1 - step, n) if way == 0 else lax.rem(me + 1 + step, n)

    def w_copy(way, step):
        start = pl.multiple_of(owner_of(way, step) * rows_here + way * half, half)
        rows = pl.ds(start, half)
        return pltpu.make_async_copy(w_hbm.at[rows], w_ref.at[rows], w_sem.at[way, step])

    for step in range(n):
        for way in (0, 1):
            w_copy(way, step).start()
    barrier = pltpu.get_barrier_semaphore()
    for neighbour in (left, right):
        pl.semaphore_signal(barrier, inc=1, device_id={"head": neighbour}, device_id_type=MESH)
    for away in range(1, s):
        pl.semaphore_signal(
            barrier, inc=1, device_id={"seq": lax.rem(mine + away, s)}, device_id_type=MESH
        )
    pl.semaphore_wait(barrier, 2 + s - 1)
    sems = (send_sem, recv_sem)
    p_copies = []
    for away in range(1, s):
        copy = pltpu.make_async_remote_copy(
            src_ref=p_ref,
            dst_ref=p_in.at[away - 1],
            send_sem=p_send.at[away - 1],
            recv_sem=p_recv.at[away - 1],
            device_id={"seq": lax.rem(mine + away, s)},
            device_id_type=MESH,
        )
        p_copies.append(copy)
    sent = {}
    for step in range(n):
        for chunk, way in ((c, w) for c in range(CHUNKS) for w in (0, 1)):
            target = left if way else right
            lane = way * CHUNKS + chunk
            owner = owner_of(way, step)
            if chunk == 0:
                w_copy(way, step).wait()
            if step > 0:
                sent[step - 1, lane].wait_recv()
            first = pl.multiple_of(owner * rows_here + way * half, half)

            def finish(start, count, part, target_ref, base):
                if step > 0:
                    old = coming[way, step - 1, pl.ds(start, count), :]
                    part = part.astype(jnp.bfloat16).astype(jnp.float32) + old.astype(jnp.float32)
                if step < n - 1:
                    going[way, step, pl.ds(start, count), :] = part.astype(jnp.bfloat16)
                else:
                    target_ref[pl.ds(base, count), :] = part.astype(jnp.bfloat16)

            def multiply(index, carry):
                start = pl.multiple_of(chunk * piece + index * tile, tile)
                part = lax.dot_general(
                    w_ref[pl.ds(first + start, tile), :],
                    x_ref[...],
                    LAST,
                    preferred_element_type=jnp.float32,
                )
                base = pl.multiple_of(way * half + start, tile)
                finish(start, tile, part, o_ref, base)
                return carry

            lax.fori_loop(0, piece // tile, multiply, 0)
            span = piece
            if chunk == CHUNKS - 1:
                span = piece + bc_half
                bc_start = pl.multiple_of(owner * 2 * bc_half + way * bc_half, bc_half)
                finish(half, bc_half, bc_ref[pl.ds(bc_start, bc_half), :], obc_ref, way * bc_half)
            if step < n - 1:
                rows = pl.ds(chunk * piece, span)
                copy = ring_copy(
                    going.at[way, step, rows], coming.at[way, step, rows], sems, lane, step, target
                )
                copy.start()
                sent[step, lane] = copy
        if step == 0:
            for copy in p_copies:
                copy.start()
    value = p_ref[...]
    for index, copy in enumerate(p_copies):
        copy.wait_recv()
        value = value + p_in[index]
    op_ref[...] = value
    for copy in p_copies + list(sent.values()):
        copy.wait_send()


def matmul_scatter(w, x, bc, params):
    n, s = (lax.axis_size("head"), lax.axis_size("seq"))
    tokens = x.shape[0]
    rows_here, bc_here = (w.shape[0] // n, bc.shape[0] // n)
    padded = jnp.zeros((8, 128), jnp.float32).at[: params.shape[0], : params.shape[1]].set(params)
    vmem = pl.BlockSpec(memory_space=pltpu.VMEM)
    packet = (2, n - 1, (rows_here + bc_here) // 2, tokens)
    in_sum, bc_sum, param_sum = pl.pallas_call(
        functools.partial(matmul_scatter_kernel, n, s),
        out_shape=(
            jax.ShapeDtypeStruct((rows_here, tokens), jnp.bfloat16),
            jax.ShapeDtypeStruct((bc_here, tokens), jnp.bfloat16),
            jax.ShapeDtypeStruct((8, 128), jnp.float32),
        ),
        in_specs=[pl.BlockSpec(memory_space=pltpu.HBM), vmem, vmem, vmem],
        out_specs=(vmem, vmem, vmem),
        scratch_shapes=[
            pltpu.VMEM(w.shape, jnp.bfloat16),
            pltpu.VMEM(packet, jnp.bfloat16),
            pltpu.VMEM(packet, jnp.bfloat16),
            pltpu.VMEM((s - 1, 8, 128), jnp.float32),
            pltpu.SemaphoreType.DMA((2 * CHUNKS, n - 1)),
            pltpu.SemaphoreType.DMA((2 * CHUNKS, n - 1)),
            pltpu.SemaphoreType.DMA((2, n)),
            pltpu.SemaphoreType.DMA((s - 1,)),
            pltpu.SemaphoreType.DMA((s - 1,)),
        ],
        compiler_params=pltpu.CompilerParams(
            collective_id=1, has_side_effects=True, vmem_limit_bytes=52 * 2**20
        ),
        name="matmul_scatter",
    )(w, x, bc, padded)
    return in_sum, bc_sum, param_sum[: params.shape[0], : params.shape[1]]


def shards(out_grad, x_in, b_in, c_in, dt_raw, dt_bias, a_log, d_skip, states, w_out, w_in):
    tokens_here, inner_here = x_in.shape
    group_heads = dt_raw.shape[0]
    head_dim = inner_here // group_heads
    state_dim = b_in.shape[1]
    contract_last = (((1,), (1,)), ((), ()))
    head_grad = gather_matmul(out_grad, w_out)
    dy_heads = head_grad.reshape(tokens_here, group_heads, head_dim)
    x_heads = x_in.reshape(tokens_here, group_heads, head_dim)
    x_wide = x_heads.astype(jnp.float32)
    decay_rate = jnp.exp(a_log)
    step_size = jax.nn.softplus(dt_raw + dt_bias[:, None])
    log_step = -decay_rate[:, None] * step_size
    positions = jnp.arange(tokens_here)
    causal = positions[:, None] >= positions[None, :]
    upto = causal.astype(jnp.float32)
    cumlog = lax.dot_general(log_step, upto, contract_last, precision=lax.Precision.HIGHEST)
    log_gaps = cumlog[:, :, None] - cumlog[:, None, :]
    decay_mask = jnp.where(causal[None], jnp.exp(jnp.minimum(log_gaps, 0.0)), 0.0)
    start_decay = jnp.exp(cumlog)
    dy_decay = (dy_heads.astype(jnp.float32) * start_decay.T[:, :, None]).astype(jnp.bfloat16)
    local_state = jnp.einsum("ihp,in->hpn", dy_decay, c_in, preferred_element_type=jnp.float32)
    end_total = jnp.exp(cumlog[:, -1])
    carried, dy_heads = entering(end_total, local_state, "seq", dy_heads)
    dy_wide = dy_heads.astype(jnp.float32)
    scores = lax.dot_general(c_in, b_in, contract_last, preferred_element_type=jnp.float32)
    step_rows = step_size.T
    x_scaled = (x_wide * step_rows[:, :, None]).astype(jnp.bfloat16)
    pair_dots = jnp.einsum("ihp,jhp->hij", dy_heads, x_scaled, preferred_element_type=jnp.float32)
    kernel = (scores[None] * decay_mask).astype(jnp.bfloat16)
    intra_back = jnp.einsum("hij,ihp->jhp", kernel, dy_heads, preferred_element_type=jnp.float32)
    masked_dots = (pair_dots * decay_mask).astype(jnp.bfloat16)
    entry_state = states.reshape(group_heads, head_dim, state_dim)
    db_intra = jnp.einsum("hij,in->nj", masked_dots, c_in, preferred_element_type=jnp.float32)
    dc_intra = jnp.einsum("hij,jn->ni", masked_dots, b_in, preferred_element_type=jnp.float32)
    dc_entry = jnp.einsum("ihp,hpn->ni", dy_decay, entry_state, preferred_element_type=jnp.float32)
    ystate = jnp.einsum("in,hpn->ihp", c_in, entry_state, preferred_element_type=jnp.float32)
    pair_weight = pair_dots * scores[None] * decay_mask
    state_terms = start_decay * jnp.sum(dy_wide * ystate, axis=2).T
    skip_terms = jnp.sum(dy_wide * x_wide, axis=(0, 2))

    carried_bf = carried.astype(jnp.bfloat16)
    state_back = jnp.einsum("jn,hpn->jhp", b_in, carried_bf, preferred_element_type=jnp.float32)
    end_decay = jnp.exp(cumlog[:, -1:] - cumlog)
    end_weight = (step_size * end_decay).T
    x_grad = (
        (
            step_rows[:, :, None] * intra_back
            + end_weight[:, :, None] * state_back
            + d_skip[None, :, None] * dy_wide
        )
        .astype(jnp.bfloat16)
        .reshape(tokens_here, inner_here)
    )
    x_end = (x_wide * end_weight[:, :, None]).astype(jnp.bfloat16)
    db_entry = jnp.einsum("jhp,hpn->nj", x_end, carried_bf, preferred_element_type=jnp.float32)
    bc_part = jnp.concatenate([db_intra + db_entry, dc_intra + dc_entry], axis=0)
    end_terms = end_weight.T * jnp.sum(x_wide * state_back, axis=2).T
    cum_grad = pair_weight.sum(axis=2) - pair_weight.sum(axis=1) + state_terms - end_terms
    tail_grad = end_terms.sum(axis=1) + end_total * jnp.sum(
        entry_state.astype(jnp.float32) * carried, axis=(1, 2)
    )
    cum_grad = cum_grad.at[:, -1].add(tail_grad)
    step_grad = jnp.dot(cum_grad, upto, precision=lax.Precision.HIGHEST)
    dt_sum = (
        -decay_rate[:, None] * step_grad
        + jnp.sum(x_wide * (intra_back + end_decay.T[:, :, None] * state_back), axis=2).T
    )
    dt_grad = dt_sum * jax.nn.sigmoid(dt_raw + dt_bias[:, None])
    param_terms = jnp.stack(
        [jnp.sum(step_grad * log_step, axis=1), skip_terms, jnp.sum(dt_grad, axis=1)]
    )
    in_part, bc_sum, param_sum = matmul_scatter(w_in, x_grad, bc_part, param_terms)
    norm_scale = (lax.axis_size("seq") * tokens_here * head_dim) ** (-0.5)
    param_grad = param_sum * norm_scale
    return (in_part, bc_sum, dt_grad, param_grad)


def solution(mesh):
    return jax.shard_map(
        shards,
        mesh=mesh,
        in_specs=(
            P("seq", "head"),
            P("seq", "head"),
            P("seq", None),
            P("seq", None),
            P("head", "seq"),
            P("head"),
            P("head"),
            P("head"),
            P("seq", "head", None),
            P("head", None),
            P(None, "head"),
        ),
        out_specs=(P("head", "seq"), P("head", "seq"), P("head", "seq"), P(None, "head")),
        check_vma=False,
    )
```

```python
import functools

import jax
import jax.numpy as jnp
from jax import lax
from jax.experimental import pallas as pl
from jax.experimental.pallas import tpu as pltpu
from jax.sharding import PartitionSpec as P

LAST = (((1,), (1,)), ((), ()))
FIRST = (((0,), (0,)), ((), ()))
PLAIN = (((1,), (0,)), ((), ()))
MESH = pl.DeviceIdType.MESH
EXACT = lax.Precision.HIGHEST
F32, BF16 = jnp.float32, jnp.bfloat16
LANES = 128


def dot(a, b, dims=PLAIN, precision=None):
    return lax.dot_general(a, b, dims, precision=precision, preferred_element_type=F32)


def pieces_of(extent, unit, most):
    count = most
    while extent % (count * unit):
        count //= 2
    return count


def remote(src, dst, send, recv, axis, target):
    return pltpu.make_async_remote_copy(
        src_ref=src, dst_ref=dst, send_sem=send, recv_sem=recv,
        device_id={axis: target}, device_id_type=MESH,
    )


def layer_kernel(
    n, s, scale,
    og, x_ref, b_ref, c_ref, raw_ref, bias_ref, alog_ref, skip_ref, states, w_out, w_in,
    o_ref, obc_ref, odt_ref, opar_ref,
    wo, wi, held, acc, dy, dyd, xt, mask, km, intra, ysta, back, xend, xg,
    going, coming, own_bc, lf, lb, lin, sb, sin, tf, tb, tin, carried,
    et_own, et_in, reach, rows_step, rows_cum, rows_r, rows_xi, rows_st, rows_dx, rows_xs, rows_tail,
    cols, shared, par, par_in,
    g_send, g_recv, wo_sem, wi_sem, s_send, s_recv, et_send, et_recv,
    l_send, l_recv, st_send, st_recv, t_send, t_recv, p_send, p_recv,
):
    me = lax.axis_index("head")
    mine = lax.axis_index("seq")
    tokens, depth = og.shape
    heads = raw_ref.shape[0]
    inner = x_ref.shape[1]
    hdim = inner // heads
    state = b_ref.shape[1]
    per = LANES // hdim
    chips = s // 2
    chip = mine // 2
    odd = lax.rem(mine, 2) == 1
    even = jnp.logical_not(odd)
    right, left = lax.rem(me + 1, n), lax.rem(me + n - 1, n)
    has_right, has_left = me < n - 1, me > 0
    tile = min(256, inner)

    def w_copy(offset):
        where = pl.ds(pl.multiple_of(lax.rem(me + offset, n) * depth, depth), depth)
        return pltpu.make_async_copy(w_out.at[:, where], wo.at[:, where], wo_sem.at[offset])

    wi_copy = pltpu.make_async_copy(w_in, wi, wi_sem)
    w_order = [0]
    for d in range(n - 1):
        for offset in (n - 1 - d, d + 1):
            if offset not in w_order:
                w_order.append(offset)
    for offset in w_order:
        w_copy(offset).start()
    wi_copy.start()

    barrier = pltpu.get_barrier_semaphore()
    for neighbour in (left, right):
        pl.semaphore_signal(barrier, inc=1, device_id={"head": neighbour}, device_id_type=MESH)
    for away in range(1, s):
        pl.semaphore_signal(
            barrier, inc=1, device_id={"seq": lax.rem(mine + away, s)}, device_id_type=MESH
        )
    pl.semaphore_wait(barrier, 2 + s - 1)

    parts = pieces_of(depth, LANES, 4)
    width = depth // parts

    def g_copy(side, d, q):
        where = pl.ds(q * width, width)
        src = og.at[:, where] if d == 0 else held.at[side, d - 1, :, where]
        return remote(
            src, held.at[side, d, :, where], g_send.at[side, d, q], g_recv.at[side, d, q],
            "head", right if side == 0 else left,
        )

    def g_sends(side, d):
        return (has_right & (me >= d)) if side == 0 else (has_left & (me + d <= n - 1))

    def g_gets(side, d):
        return (me > d) if side == 0 else (me + 1 + d <= n - 1)

    for side in (0, 1):
        @pl.when(g_sends(side, 0))
        def _():
            for q in range(parts):
                g_copy(side, 0, q).start()

    def column_of(row):
        at = lax.broadcasted_iota(jnp.int32, (heads, heads), 0)
        along = lax.broadcasted_iota(jnp.int32, (heads, heads), 1)
        return jnp.sum(jnp.where(at == along, row, 0.0), axis=1, keepdims=True)

    bias = column_of(bias_ref[...])
    rate = jnp.exp(column_of(alog_ref[...]))
    skip = column_of(skip_ref[...])
    first = lax.broadcasted_iota(jnp.int32, (tokens, tokens), 0)
    second = lax.broadcasted_iota(jnp.int32, (tokens, tokens), 1)
    upto = (first <= second).astype(F32)
    raw = raw_ref[...] + bias
    step = jnp.maximum(raw, 0.0) + jnp.log1p(jnp.exp(-jnp.abs(raw)))
    log_step = -rate * step
    cum = dot(log_step, upto, precision=EXACT)
    total = cum[:, tokens - 1 : tokens]
    end_decay = jnp.exp(total - cum)
    start_decay = jnp.exp(cum)
    end_total = jnp.exp(total)
    end_weight = step * end_decay
    rows_step[...] = step
    rows_cum[...] = cum
    et_own[...] = jnp.broadcast_to(end_total, et_own.shape)

    def et_copy(away):
        return remote(
            et_own, et_in.at[away - 1], et_send.at[away - 1], et_recv.at[away - 1],
            "seq", lax.rem(mine + s - away, s),
        )

    for away in range(1, s):
        et_copy(away).start()

    eye = (first == second).astype(F32)
    cols[0] = dot(eye, cum, LAST, precision=EXACT)
    cols[1] = dot(eye, step, LAST, precision=EXACT)
    shared[0] = dot(b_ref[...], c_ref[...], LAST)
    shared[1] = jnp.zeros((tokens, tokens), F32)
    lane = lax.broadcasted_iota(jnp.int32, (tokens, heads), 1)

    def masks(h, carry):
        col = jnp.sum(jnp.where(lane == h, cols[0], 0.0), axis=1, keepdims=True)
        col_step = jnp.sum(jnp.where(lane == h, cols[1], 0.0), axis=1, keepdims=True)
        gap = rows_cum[pl.ds(h, 1), :] - col
        value = jnp.where(first <= second, jnp.exp(jnp.minimum(gap, 0.0)) * col_step, 0.0)
        mask[h] = value
        km[h] = (shared[0] * value).astype(BF16)
        return carry

    lax.fori_loop(0, heads, masks, 0)
    eye_bf = eye[:tile, :tile].astype(BF16)
    for k in range(inner // tile):
        where = pl.ds(k * tile, tile)
        xt[where, :] = dot(eye_bf, x_ref[:, where], LAST).astype(BF16)
        ysta[where, :] = dot(states[0, where, :], c_ref[...], LAST)
    ct = dot(eye_bf[:state, :state], c_ref[...], LAST).astype(BF16)
    bt = dot(eye_bf[:state, :state], b_ref[...], LAST).astype(BF16)
    sbt = dot(eye_bf[:state, :state], states[0], LAST).astype(BF16)

    def multiply(source, offset, fresh):
        w_copy(offset).wait()
        where = pl.ds(pl.multiple_of(lax.rem(me + offset, n) * depth, depth), depth)

        def body(k, carry):
            outs = pl.ds(pl.multiple_of(k * tile, tile), tile)
            part = dot(wo[outs, where], source[...], LAST)
            acc[outs, :] = part if fresh else acc[outs, :] + part
            return carry

        lax.fori_loop(0, inner // tile, body, 0)

    multiply(og, 0, True)
    for d in range(n - 1):
        for q in range(parts):
            for side in (0, 1):
                @pl.when(g_gets(side, d))
                def _():
                    g_copy(side, d, q).wait_recv()
                if d + 1 < n - 1:
                    @pl.when(g_gets(side, d) & g_sends(side, d + 1))
                    def _():
                        g_copy(side, d + 1, q).start()
        for side in (0, 1):
            @pl.when(g_gets(side, d))
            def _():
                multiply(held.at[side, d], n - 1 - d if side == 0 else d + 1, False)

    for h in range(heads):
        rows = pl.ds(h * hdim, hdim)
        rounded = acc[rows, :].astype(BF16)
        dy[rows, :] = rounded
        dyd[rows, :] = (rounded.astype(F32) * start_decay[h : h + 1, :]).astype(BF16)
    for k in range(inner // tile):
        rows = pl.ds(k * tile, tile)
        lf[rows, :] = dot(dyd[rows, :], c_ref[...])
        lb[rows, :] = lf[rows, :].astype(BF16)

    sibling = mine + 1 - 2 * lax.rem(mine, 2)
    l_copy = remote(lb, lin, l_send, l_recv, "seq", sibling)
    t_copy = remote(tb, tin, t_send, t_recv, "seq", sibling)

    @pl.when(odd)
    def _():
        l_copy.start()

    for away in range(1, s):
        et_copy(away).wait_recv()
    weight = jnp.ones((heads, LANES), F32)
    for a in range(1, chips):
        reach[a - 1] = weight
        weight = weight * et_in[2 * a - 1] * et_in[2 * a]

    half_lane = lax.broadcasted_iota(jnp.int32, (tokens, LANES), 1) // hdim

    def intra_heads(pair, carry):
        block = pl.ds(pl.multiple_of(pair * LANES, LANES), LANES)
        x_pair = x_ref[:, block]
        dy_pair = dy[block, :]
        for sub in range(per):
            h = pair * per + sub
            rows = pl.ds(pl.multiple_of(h * hdim, hdim), hdim)
            dots = dot(jnp.where(half_lane == sub, x_pair, jnp.zeros_like(x_pair)), dy_pair)
            shared[1] += dots * mask[h]
            rows_r[pl.ds(h, 1), :] = jnp.sum(dots * km[h].astype(F32), axis=0, keepdims=True)
            dy_h = dy[rows, :]
            x_h = xt[rows, :].astype(F32)
            inside = dot(dy_h, km[h], LAST)
            intra[rows, :] = inside
            wide = dy_h.astype(F32)
            rows_xi[pl.ds(h, 1), :] = jnp.sum(x_h * inside, axis=0, keepdims=True)
            rows_st[pl.ds(h, 1), :] = jnp.sum(wide * ysta[rows, :], axis=0, keepdims=True)
            rows_dx[pl.ds(h, 1), :] = jnp.sum(wide * x_h, axis=0, keepdims=True)
        return carry

    pairs = heads // per
    early = pairs // 4
    lax.fori_loop(0, early, intra_heads, 0)

    def st_copy(a):
        return remote(
            sb, sin.at[a - 1], st_send.at[a - 1], st_recv.at[a - 1],
            "seq", jnp.maximum(mine - 2 * a, 0),
        )

    @pl.when(even)
    def _():
        l_copy.wait_recv()

        def join(h, carry):
            rows = pl.ds(pl.multiple_of(h * hdim, hdim), hdim)
            value = lf[rows, :] + et_own[pl.ds(h, 1), :] * lin[rows, :].astype(F32)
            sb[rows, :] = value.astype(BF16)
            return carry

        lax.fori_loop(0, heads, join, 0)

    for a in range(1, chips):
        @pl.when(even & (chip >= a))
        def _():
            st_copy(a).start()

    lax.fori_loop(early, pairs, intra_heads, 0)

    @pl.when(even)
    def _():
        tf[...] = jnp.zeros_like(tf)

    for a in range(1, chips):
        @pl.when(even & (chip + a < chips))
        def _():
            st_copy(a).wait_recv()

            def add(h, carry):
                rows = pl.ds(pl.multiple_of(h * hdim, hdim), hdim)
                tf[rows, :] += reach[a - 1, pl.ds(h, 1), :] * sin[a - 1, rows, :].astype(F32)
                return carry

            lax.fori_loop(0, heads, add, 0)

    @pl.when(even)
    def _():
        tb[...] = tf[...].astype(BF16)
        t_copy.start()

        def enter(h, carry):
            rows = pl.ds(pl.multiple_of(h * hdim, hdim), hdim)
            carried[rows, :] = lin[rows, :].astype(F32) + et_in[0, pl.ds(h, 1), :] * tf[rows, :]
            return carry

        lax.fori_loop(0, heads, enter, 0)

    @pl.when(odd)
    def _():
        t_copy.wait_recv()
        carried[...] = tin[...].astype(F32)

    for k in range(inner // tile):
        rows = pl.ds(k * tile, tile)
        back[rows, :] = dot(carried[rows, :].astype(BF16), b_ref[...], LAST)
    for h in range(heads):
        rows = pl.ds(h * hdim, hdim)
        xg[rows, :] = (
            intra[rows, :]
            + end_weight[h : h + 1, :] * back[rows, :]
            + skip[h : h + 1, :] * dy[rows, :].astype(F32)
        ).astype(BF16)

    wi_copy.wait()
    out_rows = o_ref.shape[0]
    bc_rows = obc_ref.shape[0]
    splits = pieces_of(out_rows, 16, 4)
    piece = out_rows // splits

    def s_copy(side, e, q):
        rows = pl.ds(q * piece, piece + (bc_rows if q == splits - 1 else 0))
        return remote(
            going.at[side, e, rows], coming.at[side, e, rows],
            s_send.at[side, e, q], s_recv.at[side, e, q], "head", right if side == 0 else left,
        )

    def owner_of(side, e):
        return n - 1 - e if side == 0 else e

    def s_sends(side, e):
        return (me < owner_of(side, e)) if side == 0 else (me > owner_of(side, e))

    def s_gets(side, e):
        return (s_sends(side, e) | (me == owner_of(side, e))) & (has_left if side == 0 else has_right)

    def term(owner, q):
        start = pl.multiple_of(owner * out_rows + q * piece, piece)
        return dot(wi[pl.ds(start, piece), :], xg[...])

    def pass_on(side, e, q):
        @pl.when(s_sends(side, e))
        def _():
            owner = owner_of(side, e)
            rows = pl.ds(q * piece, piece)
            going[side, e, rows, :] = term(owner, q).astype(BF16)
            bc_to = pl.ds(out_rows, bc_rows)
            if q == splits - 1:
                going[side, e, bc_to, :] = own_bc[pl.ds(owner * bc_rows, bc_rows), :]

            @pl.when(s_gets(side, e))
            def _():
                s_copy(side, e, q).wait_recv()
                for where in (rows, bc_to) if q == splits - 1 else (rows,):
                    going[side, e, where, :] = (
                        going[side, e, where, :].astype(F32) + coming[side, e, where, :].astype(F32)
                    ).astype(BF16)

            s_copy(side, e, q).start()

    for side in (0, 1):
        pass_on(side, 0, 0)

    for h in range(heads):
        rows = pl.ds(h * hdim, hdim)
        x_h = xt[rows, :].astype(F32)
        xend[rows, :] = (x_h * end_weight[h : h + 1, :]).astype(BF16)
        rows_xs[h : h + 1, :] = jnp.sum(x_h * back[rows, :], axis=0, keepdims=True)
        rows_tail[h : h + 1, :] = jnp.sum(
            states[0, rows, :].astype(F32) * carried[rows, :], axis=0, keepdims=True
        )
    sums = shared[1].astype(BF16)
    carried_t = dot(eye_bf[:state, :state], carried[...].astype(BF16), LAST).astype(BF16)
    own_bc[:state, :] = (dot(ct, sums, LAST) + dot(carried_t, xend[...])).astype(BF16)
    own_bc[state:, :] = (dot(bt, sums) + dot(sbt, dyd[...])).astype(BF16)

    for q in range(1, splits):
        for side in (0, 1):
            pass_on(side, 0, q)

    end_terms = end_weight * rows_xs[...]
    cum_grad = rows_r[...] - rows_xi[...] + start_decay * rows_st[...] - end_terms
    tail = jnp.sum(end_terms, axis=1, keepdims=True) + end_total * jnp.sum(
        rows_tail[...], axis=1, keepdims=True
    )
    token = lax.broadcasted_iota(jnp.int32, (heads, tokens), 1)
    cum_grad = cum_grad + jnp.where(token == tokens - 1, tail, 0.0)
    step_grad = dot(cum_grad, upto, LAST, precision=EXACT)
    dt_sum = -rate * step_grad + (rows_xi[...] + end_terms) / step
    dt_grad = dt_sum / (1.0 + jnp.exp(-raw))
    odt_ref[...] = dt_grad

    def row_of(column):
        at = lax.broadcasted_iota(jnp.int32, (heads, LANES), 0)
        along = lax.broadcasted_iota(jnp.int32, (heads, LANES), 1)
        return jnp.sum(jnp.where(at == along, column, 0.0), axis=0, keepdims=True)

    line = lax.broadcasted_iota(jnp.int32, (8, LANES), 0)
    packet = jnp.zeros((8, LANES), F32)
    for index, terms in enumerate((step_grad * log_step, rows_dx[...], dt_grad)):
        packet = jnp.where(line == index, row_of(jnp.sum(terms, axis=1, keepdims=True)), packet)
    par[...] = packet

    def p_copy(away):
        return remote(
            par, par_in.at[away - 1], p_send.at[away - 1], p_recv.at[away - 1],
            "seq", lax.rem(mine + s - away, s),
        )

    for away in range(1, s):
        p_copy(away).start()

    for e in range(1, n - 1):
        for q in range(splits):
            for side in (0, 1):
                pass_on(side, e, q)

    for q in range(splits):
        rows = pl.ds(q * piece, piece)
        acc[rows, :] = term(me, q)
    acc_bc = own_bc[pl.ds(pl.multiple_of(me * bc_rows, bc_rows), bc_rows), :].astype(F32)
    lf_bc = acc_bc
    value = packet
    for away in range(1, s):
        p_copy(away).wait_recv()
        value = value + par_in[away - 1]
    opar_ref[...] = value[: opar_ref.shape[0], :heads] * scale
    o_bc = pl.ds(out_rows, bc_rows)
    back[:bc_rows, :] = lf_bc
    for q in range(splits):
        rows = pl.ds(q * piece, piece)
        for side in (0, 1):
            for e in range(n - 1):
                @pl.when((me == owner_of(side, e)) & s_gets(side, e))
                def _():
                    s_copy(side, e, q).wait_recv()
                    acc[rows, :] += coming[side, e, rows, :].astype(F32)
                    if q == splits - 1:
                        back[:bc_rows, :] += coming[side, e, o_bc, :].astype(F32)
        o_ref[rows, :] = acc[rows, :].astype(BF16)
    obc_ref[...] = back[:bc_rows, :].astype(BF16)

    for side in (0, 1):
        for d in range(n - 1):
            @pl.when(g_sends(side, d))
            def _():
                for q in range(parts):
                    g_copy(side, d, q).wait_send()

            @pl.when(s_sends(side, d))
            def _():
                for q in range(splits):
                    s_copy(side, d, q).wait_send()
    for away in range(1, s):
        et_copy(away).wait_send()
        p_copy(away).wait_send()

    @pl.when(odd)
    def _():
        l_copy.wait_send()

    for a in range(1, chips):
        @pl.when(even & (chip >= a))
        def _():
            st_copy(a).wait_send()

    @pl.when(even)
    def _():
        t_copy.wait_send()


def layer(og, x, b, c, raw, bias, alog, skip, states, w_out, w_in):
    n, s = lax.axis_size("head"), lax.axis_size("seq")
    tokens, depth = og.shape
    inner = x.shape[1]
    heads = raw.shape[0]
    hdim = inner // heads
    state = b.shape[1]
    out_rows = w_in.shape[0] // n
    bc_rows = 2 * state // n
    chips = s // 2
    scale = (s * tokens * hdim) ** (-0.5)
    vmem = pl.BlockSpec(memory_space=pltpu.VMEM)
    hbm = pl.BlockSpec(memory_space=pltpu.HBM)
    dma = pltpu.SemaphoreType.DMA
    parts = pieces_of(depth, LANES, 4)
    splits = pieces_of(out_rows, 16, 4)

    def wide(dtype):
        return pltpu.VMEM((inner, tokens), dtype)

    def slim(dtype, *lead):
        return pltpu.VMEM((*lead, inner, state), dtype)

    rows = pltpu.VMEM((heads, tokens), F32)
    packet = pltpu.VMEM((2, n - 1, out_rows + bc_rows, tokens), BF16)
    scratch = [
        pltpu.VMEM(w_out.shape, BF16),
        pltpu.VMEM(w_in.shape, BF16),
        pltpu.VMEM((2, n - 1, tokens, depth), BF16),
        wide(F32), wide(BF16), wide(BF16), wide(BF16),
        pltpu.VMEM((heads, tokens, tokens), F32),
        pltpu.VMEM((heads, tokens, tokens), BF16),
        wide(F32), wide(F32), wide(F32), wide(BF16), wide(BF16),
        packet, packet,
        pltpu.VMEM((2 * state, tokens), BF16),
        slim(F32), slim(BF16), slim(BF16), slim(BF16), slim(BF16, chips - 1),
        slim(F32), slim(BF16), slim(BF16), slim(F32),
        pltpu.VMEM((heads, LANES), F32),
        pltpu.VMEM((s - 1, heads, LANES), F32),
        pltpu.VMEM((chips - 1, heads, LANES), F32),
        rows, rows, rows, rows, rows, rows, rows, pltpu.VMEM((heads, state), F32),
        pltpu.VMEM((2, tokens, heads), F32),
        pltpu.VMEM((2, tokens, tokens), F32),
        pltpu.VMEM((8, LANES), F32),
        pltpu.VMEM((s - 1, 8, LANES), F32),
        dma((2, n - 1, parts)), dma((2, n - 1, parts)), dma((n,)), dma,
        dma((2, n - 1, splits)), dma((2, n - 1, splits)),
        dma((s - 1,)), dma((s - 1,)),
        dma, dma, dma((chips - 1,)), dma((chips - 1,)), dma, dma,
        dma((s - 1,)), dma((s - 1,)),
    ]
    return pl.pallas_call(
        functools.partial(layer_kernel, n, s, scale),
        out_shape=(
            jax.ShapeDtypeStruct((out_rows, tokens), BF16),
            jax.ShapeDtypeStruct((bc_rows, tokens), BF16),
            jax.ShapeDtypeStruct((heads, tokens), F32),
            jax.ShapeDtypeStruct((3, heads), F32),
        ),
        in_specs=[vmem] * 9 + [hbm] * 2,
        out_specs=(vmem,) * 4,
        scratch_shapes=scratch,
        compiler_params=pltpu.CompilerParams(
            collective_id=0, has_side_effects=True, vmem_limit_bytes=58 * 2**20
        ),
        name="layer",
    )(og, x, b, c, raw, bias[None], alog[None], skip[None], states, w_out, w_in)


def solution(mesh):
    return jax.shard_map(
        layer,
        mesh=mesh,
        in_specs=(
            P("seq", "head"),
            P("seq", "head"),
            P("seq", None),
            P("seq", None),
            P("head", "seq"),
            P("head"),
            P("head"),
            P("head"),
            P("seq", "head", None),
            P("head", None),
            P(None, "head"),
        ),
        out_specs=(P("head", "seq"), P("head", "seq"), P("head", "seq"), P(None, "head")),
        check_vma=False,
    )
```

```python
import functools

import jax
import jax.numpy as jnp
from jax import lax
from jax.experimental import pallas as pl
from jax.experimental.pallas import tpu as pltpu
from jax.sharding import PartitionSpec as P

LAST = (((1,), (1,)), ((), ()))
FIRST = (((0,), (0,)), ((), ()))
PLAIN = (((1,), (0,)), ((), ()))
MESH = pl.DeviceIdType.MESH
EXACT = lax.Precision.HIGHEST
F32, BF16 = jnp.float32, jnp.bfloat16
SKEW = 2
LANES = 128


def dot(a, b, dims=PLAIN, precision=None):
    return lax.dot_general(a, b, dims, precision=precision, preferred_element_type=F32)


def pieces_of(extent, unit, most):
    count = most
    while extent % (count * unit):
        count //= 2
    return count


def remote(src, dst, send, recv, axis, target):
    return pltpu.make_async_remote_copy(
        src_ref=src, dst_ref=dst, send_sem=send, recv_sem=recv,
        device_id={axis: target}, device_id_type=MESH,
    )


def layer_kernel(
    n, s, scale,
    og, x_ref, b_ref, c_ref, raw_ref, bias_ref, alog_ref, skip_ref, states, w_out, w_in,
    o_ref, obc_ref, odt_ref, opar_ref,
    wo, wi, held, acc, dy, dyd, xt, mask, km, intra, ysta, back, xend, xg,
    going, coming, own_bc, lf, lb, lin, sb, sin, tf, tb, tin, carried,
    et_own, et_in, reach, rows_step, rows_cum, rows_r, rows_xi, rows_st, rows_dx, rows_xs, rows_tail,
    cols, shared, par, par_in, acc_bc,
    g_send, g_recv, wo_sem, wi_sem, s_send, s_recv, et_send, et_recv,
    l_send, l_recv, st_send, st_recv, t_send, t_recv, p_send, p_recv,
):
    me = lax.axis_index("head")
    mine = lax.axis_index("seq")
    tokens, depth = og.shape
    heads = raw_ref.shape[0]
    inner = x_ref.shape[1]
    hdim = inner // heads
    state = b_ref.shape[1]
    per = LANES // hdim
    chips = s // 2
    chip = mine // 2
    odd = lax.rem(mine, 2) == 1
    even = jnp.logical_not(odd)
    right, left = lax.rem(me + 1, n), lax.rem(me + n - 1, n)
    has_right, has_left = me < n - 1, me > 0
    tile = min(256, inner)

    def w_copy(offset):
        where = pl.ds(pl.multiple_of(lax.rem(me + offset, n) * depth, depth), depth)
        return pltpu.make_async_copy(w_out.at[:, where], wo.at[:, where], wo_sem.at[offset])

    wi_copy = pltpu.make_async_copy(w_in, wi, wi_sem)
    w_order = [0]
    for d in range(n - 1):
        for offset in (n - 1 - d, d + 1):
            if offset not in w_order:
                w_order.append(offset)
    for offset in w_order:
        w_copy(offset).start()
    wi_copy.start()

    barrier = pltpu.get_barrier_semaphore()
    for neighbour in (left, right):
        pl.semaphore_signal(barrier, inc=1, device_id={"head": neighbour}, device_id_type=MESH)
    for away in range(1, s):
        pl.semaphore_signal(
            barrier, inc=1, device_id={"seq": lax.rem(mine + away, s)}, device_id_type=MESH
        )
    pl.semaphore_wait(barrier, 2 + s - 1)

    parts = pieces_of(depth, LANES, 4)
    width = depth // parts

    def g_copy(side, d, q):
        where = pl.ds(q * width, width)
        src = og.at[:, where] if d == 0 else held.at[side, d - 1, :, where]
        return remote(
            src, held.at[side, d, :, where], g_send.at[side, d, q], g_recv.at[side, d, q],
            "head", right if side == 0 else left,
        )

    def g_sends(side, d):
        return (has_right & (me >= d)) if side == 0 else (has_left & (me + d <= n - 1))

    def g_gets(side, d):
        return (me > d) if side == 0 else (me + 1 + d <= n - 1)

    for side in (0, 1):
        @pl.when(g_sends(side, 0))
        def _():
            for q in range(parts):
                g_copy(side, 0, q).start()

    def column_of(row):
        at = lax.broadcasted_iota(jnp.int32, (heads, heads), 0)
        along = lax.broadcasted_iota(jnp.int32, (heads, heads), 1)
        return jnp.sum(jnp.where(at == along, row, 0.0), axis=1, keepdims=True)

    bias = column_of(bias_ref[...])
    rate = jnp.exp(column_of(alog_ref[...]))
    skip = column_of(skip_ref[...])
    first = lax.broadcasted_iota(jnp.int32, (tokens, tokens), 0)
    second = lax.broadcasted_iota(jnp.int32, (tokens, tokens), 1)
    upto = (first <= second).astype(F32)
    raw = raw_ref[...] + bias
    step = jnp.maximum(raw, 0.0) + jnp.log1p(jnp.exp(-jnp.abs(raw)))
    log_step = -rate * step
    cum = dot(log_step, upto, precision=EXACT)
    total = cum[:, tokens - 1 : tokens]
    end_decay = jnp.exp(total - cum)
    start_decay = jnp.exp(cum)
    end_total = jnp.exp(total)
    end_weight = step * end_decay
    rows_step[...] = step
    rows_cum[...] = cum
    et_own[...] = jnp.broadcast_to(end_total, et_own.shape)

    def et_copy(away):
        return remote(
            et_own, et_in.at[away - 1], et_send.at[away - 1], et_recv.at[away - 1],
            "seq", lax.rem(mine + s - away, s),
        )

    for away in range(1, s):
        et_copy(away).start()

    eye = (first == second).astype(F32)
    cols[0] = dot(eye, cum, LAST, precision=EXACT)
    cols[1] = dot(eye, step, LAST, precision=EXACT)
    shared[0] = dot(b_ref[...], c_ref[...], LAST)
    shared[1] = jnp.zeros((tokens, tokens), F32)
    lane = lax.broadcasted_iota(jnp.int32, (tokens, heads), 1)

    def masks(h, carry):
        col = jnp.sum(jnp.where(lane == h, cols[0], 0.0), axis=1, keepdims=True)
        col_step = jnp.sum(jnp.where(lane == h, cols[1], 0.0), axis=1, keepdims=True)
        gap = rows_cum[pl.ds(h, 1), :] - col
        value = jnp.where(first <= second, jnp.exp(jnp.minimum(gap, 0.0)) * col_step, 0.0)
        mask[h] = value
        km[h] = (shared[0] * value).astype(BF16)
        return carry

    lax.fori_loop(0, heads, masks, 0)
    eye_bf = eye[:tile, :tile].astype(BF16)
    for k in range(inner // tile):
        where = pl.ds(k * tile, tile)
        xt[where, :] = dot(eye_bf, x_ref[:, where], LAST).astype(BF16)
        ysta[where, :] = dot(states[0, where, :], c_ref[...], LAST)
    ct = dot(eye_bf[:state, :state], c_ref[...], LAST).astype(BF16)
    bt = dot(eye_bf[:state, :state], b_ref[...], LAST).astype(BF16)
    sbt = dot(eye_bf[:state, :state], states[0], LAST).astype(BF16)

    def multiply(source, offset, fresh):
        w_copy(offset).wait()
        where = pl.ds(pl.multiple_of(lax.rem(me + offset, n) * depth, depth), depth)

        def body(k, carry):
            outs = pl.ds(pl.multiple_of(k * tile, tile), tile)
            part = dot(wo[outs, where], source[...], LAST)
            acc[outs, :] = part if fresh else acc[outs, :] + part
            return carry

        lax.fori_loop(0, inner // tile, body, 0)

    multiply(og, 0, True)
    for d in range(n - 1):
        for q in range(parts):
            for side in (0, 1):
                @pl.when(g_gets(side, d))
                def _():
                    g_copy(side, d, q).wait_recv()
                if d + 1 < n - 1:
                    @pl.when(g_gets(side, d) & g_sends(side, d + 1))
                    def _():
                        g_copy(side, d + 1, q).start()
        for side in (0, 1):
            @pl.when(g_gets(side, d))
            def _():
                multiply(held.at[side, d], n - 1 - d if side == 0 else d + 1, False)

    for h in range(heads):
        rows = pl.ds(h * hdim, hdim)
        rounded = acc[rows, :].astype(BF16)
        dy[rows, :] = rounded
        dyd[rows, :] = (rounded.astype(F32) * start_decay[h : h + 1, :]).astype(BF16)
    for k in range(inner // tile):
        rows = pl.ds(k * tile, tile)
        lf[rows, :] = dot(dyd[rows, :], c_ref[...])
        lb[rows, :] = lf[rows, :].astype(BF16)

    sibling = mine + 1 - 2 * lax.rem(mine, 2)
    l_copy = remote(lb, lin, l_send, l_recv, "seq", sibling)
    t_copy = remote(tb, tin, t_send, t_recv, "seq", sibling)

    @pl.when(odd)
    def _():
        l_copy.start()

    for away in range(1, s):
        et_copy(away).wait_recv()
    weight = jnp.ones((heads, LANES), F32)
    for a in range(1, chips):
        reach[a - 1] = weight
        weight = weight * et_in[2 * a - 1] * et_in[2 * a]

    half_lane = lax.broadcasted_iota(jnp.int32, (tokens, LANES), 1) // hdim

    def intra_heads(pair, carry):
        block = pl.ds(pl.multiple_of(pair * LANES, LANES), LANES)
        x_pair = x_ref[:, block]
        dy_pair = dy[block, :]
        for sub in range(per):
            h = pair * per + sub
            rows = pl.ds(pl.multiple_of(h * hdim, hdim), hdim)
            dots = dot(jnp.where(half_lane == sub, x_pair, jnp.zeros_like(x_pair)), dy_pair)
            shared[1] += dots * mask[h]
            rows_r[pl.ds(h, 1), :] = jnp.sum(dots * km[h].astype(F32), axis=0, keepdims=True)
            dy_h = dy[rows, :]
            x_h = xt[rows, :].astype(F32)
            inside = dot(dy_h, km[h], LAST)
            intra[rows, :] = inside
            wide = dy_h.astype(F32)
            rows_xi[pl.ds(h, 1), :] = jnp.sum(x_h * inside, axis=0, keepdims=True)
            rows_st[pl.ds(h, 1), :] = jnp.sum(wide * ysta[rows, :], axis=0, keepdims=True)
            rows_dx[pl.ds(h, 1), :] = jnp.sum(wide * x_h, axis=0, keepdims=True)
        return carry

    pairs = heads // per
    early = pairs // 4
    lax.fori_loop(0, early, intra_heads, 0)

    def st_copy(a):
        return remote(
            sb, sin.at[a - 1], st_send.at[a - 1], st_recv.at[a - 1],
            "seq", jnp.maximum(mine - 2 * a, 0),
        )

    @pl.when(even)
    def _():
        l_copy.wait_recv()

        def join(h, carry):
            rows = pl.ds(pl.multiple_of(h * hdim, hdim), hdim)
            value = lf[rows, :] + et_own[pl.ds(h, 1), :] * lin[rows, :].astype(F32)
            sb[rows, :] = value.astype(BF16)
            return carry

        lax.fori_loop(0, heads, join, 0)

    for a in range(1, chips):
        @pl.when(even & (chip >= a))
        def _():
            st_copy(a).start()

    lax.fori_loop(early, pairs, intra_heads, 0)

    @pl.when(even)
    def _():
        tf[...] = jnp.zeros_like(tf)

    for a in range(1, chips):
        @pl.when(even & (chip + a < chips))
        def _():
            st_copy(a).wait_recv()

            def add(h, carry):
                rows = pl.ds(pl.multiple_of(h * hdim, hdim), hdim)
                tf[rows, :] += reach[a - 1, pl.ds(h, 1), :] * sin[a - 1, rows, :].astype(F32)
                return carry

            lax.fori_loop(0, heads, add, 0)

    @pl.when(even)
    def _():
        tb[...] = tf[...].astype(BF16)
        t_copy.start()

        def enter(h, carry):
            rows = pl.ds(pl.multiple_of(h * hdim, hdim), hdim)
            carried[rows, :] = lin[rows, :].astype(F32) + et_in[0, pl.ds(h, 1), :] * tf[rows, :]
            return carry

        lax.fori_loop(0, heads, enter, 0)

    @pl.when(odd)
    def _():
        t_copy.wait_recv()
        carried[...] = tin[...].astype(F32)

    for k in range(inner // tile):
        rows = pl.ds(k * tile, tile)
        back[rows, :] = dot(carried[rows, :].astype(BF16), b_ref[...], LAST)
    for h in range(heads):
        rows = pl.ds(h * hdim, hdim)
        xg[rows, :] = (
            intra[rows, :]
            + end_weight[h : h + 1, :] * back[rows, :]
            + skip[h : h + 1, :] * dy[rows, :].astype(F32)
        ).astype(BF16)

    wi_copy.wait()
    out_rows = o_ref.shape[0]
    bc_rows = obc_ref.shape[0]
    splits = pieces_of(out_rows, 16, 4)
    piece = out_rows // splits

    def s_copy(side, e, q, last):
        rows = pl.ds(pl.multiple_of(q * piece, piece), piece + (bc_rows if last else 0))
        return remote(
            going.at[side, e, rows], coming.at[side, e, rows],
            s_send.at[side, e, q], s_recv.at[side, e, q], "head", right if side == 0 else left,
        )

    def owner_of(side, e):
        return n - 1 - e if side == 0 else e

    def s_sends(side, e):
        return (me < owner_of(side, e)) if side == 0 else (me > owner_of(side, e))

    def s_gets(side, e):
        return (s_sends(side, e) | (me == owner_of(side, e))) & (has_left if side == 0 else has_right)

    def term(owner, q):
        start = pl.multiple_of(owner * out_rows + q * piece, piece)
        return dot(wi[pl.ds(start, piece), :], xg[...])

    count = (n - 1) * splits
    bc_to = pl.ds(out_rows, bc_rows)

    def bc_of(owner):
        return own_bc[pl.ds(pl.multiple_of(owner * bc_rows, bc_rows), bc_rows), :]

    def each(q, do):
        @pl.when(q == splits - 1)
        def _():
            do(True)

        if splits > 1:
            @pl.when(q < splits - 1)
            def _():
                do(False)

    def slot(index, carry):
        for side in (0, 1):
            place = index - SKEW * (me if side == 0 else n - 1 - me)
            held_at = jnp.clip(place, 0, count - 1)
            e, q = lax.div(held_at, splits), lax.rem(held_at, splits)
            owner = owner_of(side, e)
            live = (place >= 0) & (place < count)
            rows = pl.ds(pl.multiple_of(q * piece, piece), piece)

            @pl.when(live & s_sends(side, e))
            def _():
                going[side, e, rows, :] = term(owner, q).astype(BF16)

                @pl.when(q == splits - 1)
                def _():
                    going[side, e, bc_to, :] = bc_of(owner)

                @pl.when(s_gets(side, e))
                def _():
                    def add(last):
                        s_copy(side, e, q, last).wait_recv()
                        for where in (rows, bc_to) if last else (rows,):
                            going[side, e, where, :] = (
                                going[side, e, where, :].astype(F32)
                                + coming[side, e, where, :].astype(F32)
                            ).astype(BF16)

                    each(q, add)

                each(q, lambda last: s_copy(side, e, q, last).start())

            @pl.when(live & (me == owner) & s_gets(side, e))
            def _():
                def take(last):
                    s_copy(side, e, q, last).wait_recv()
                    acc[rows, :] += coming[side, e, rows, :].astype(F32)
                    if last:
                        acc_bc[...] += coming[side, e, bc_to, :].astype(F32)

                each(q, take)

        return carry

    lax.fori_loop(0, SKEW, slot, 0)

    for h in range(heads):
        rows = pl.ds(h * hdim, hdim)
        x_h = xt[rows, :].astype(F32)
        xend[rows, :] = (x_h * end_weight[h : h + 1, :]).astype(BF16)
        rows_xs[h : h + 1, :] = jnp.sum(x_h * back[rows, :], axis=0, keepdims=True)
        rows_tail[h : h + 1, :] = jnp.sum(
            states[0, rows, :].astype(F32) * carried[rows, :], axis=0, keepdims=True
        )
    sums = shared[1].astype(BF16)
    carried_t = dot(eye_bf[:state, :state], carried[...].astype(BF16), LAST).astype(BF16)
    own_bc[:state, :] = (dot(ct, sums, LAST) + dot(carried_t, xend[...])).astype(BF16)
    own_bc[state:, :] = (dot(bt, sums) + dot(sbt, dyd[...])).astype(BF16)

    acc_bc[...] = bc_of(me).astype(F32)
    for q in range(splits):
        acc[pl.ds(q * piece, piece), :] = term(me, q)
    slots = max((n - k) * splits + SKEW * k for k in range(1, n))
    first_part = min(slots, SKEW + 3)
    lax.fori_loop(SKEW, first_part, slot, 0)

    end_terms = end_weight * rows_xs[...]
    cum_grad = rows_r[...] - rows_xi[...] + start_decay * rows_st[...] - end_terms
    tail = jnp.sum(end_terms, axis=1, keepdims=True) + end_total * jnp.sum(
        rows_tail[...], axis=1, keepdims=True
    )
    token = lax.broadcasted_iota(jnp.int32, (heads, tokens), 1)
    cum_grad = cum_grad + jnp.where(token == tokens - 1, tail, 0.0)
    step_grad = dot(cum_grad, upto, LAST, precision=EXACT)
    dt_sum = -rate * step_grad + (rows_xi[...] + end_terms) / step
    dt_grad = dt_sum / (1.0 + jnp.exp(-raw))
    odt_ref[...] = dt_grad

    def row_of(column):
        at = lax.broadcasted_iota(jnp.int32, (heads, LANES), 0)
        along = lax.broadcasted_iota(jnp.int32, (heads, LANES), 1)
        return jnp.sum(jnp.where(at == along, column, 0.0), axis=0, keepdims=True)

    line = lax.broadcasted_iota(jnp.int32, (8, LANES), 0)
    packet = jnp.zeros((8, LANES), F32)
    for index, terms in enumerate((step_grad * log_step, rows_dx[...], dt_grad)):
        packet = jnp.where(line == index, row_of(jnp.sum(terms, axis=1, keepdims=True)), packet)
    par[...] = packet

    def p_copy(away):
        return remote(
            par, par_in.at[away - 1], p_send.at[away - 1], p_recv.at[away - 1],
            "seq", lax.rem(mine + s - away, s),
        )

    for away in range(1, s):
        p_copy(away).start()

    lax.fori_loop(first_part, slots, slot, 0)

    value = packet
    for away in range(1, s):
        p_copy(away).wait_recv()
        value = value + par_in[away - 1]
    opar_ref[...] = value[: opar_ref.shape[0], :heads] * scale
    o_ref[...] = acc[:out_rows, :].astype(BF16)
    obc_ref[...] = acc_bc[...].astype(BF16)

    for side in (0, 1):
        for d in range(n - 1):
            @pl.when(g_sends(side, d))
            def _():
                for q in range(parts):
                    g_copy(side, d, q).wait_send()

            @pl.when(s_sends(side, d))
            def _():
                for q in range(splits):
                    s_copy(side, d, q, q == splits - 1).wait_send()
    for away in range(1, s):
        et_copy(away).wait_send()
        p_copy(away).wait_send()

    @pl.when(odd)
    def _():
        l_copy.wait_send()

    for a in range(1, chips):
        @pl.when(even & (chip >= a))
        def _():
            st_copy(a).wait_send()

    @pl.when(even)
    def _():
        t_copy.wait_send()


def hand_on_kernel(*refs):
    count = len(refs) // 2
    for k in range(count):
        refs[count + k][...] = refs[k][...]


def handed_on(arrays):
    vmem = pl.BlockSpec(memory_space=pltpu.VMEM)
    return pl.pallas_call(
        hand_on_kernel,
        out_shape=tuple(jax.ShapeDtypeStruct(a.shape, a.dtype) for a in arrays),
        in_specs=[vmem] * len(arrays),
        out_specs=(vmem,) * len(arrays),
        name="hand_on",
    )(*arrays)


def layer(og, x, b, c, raw, bias, alog, skip, states, w_out, w_in):
    n, s = lax.axis_size("head"), lax.axis_size("seq")
    tokens, depth = og.shape
    inner = x.shape[1]
    heads = raw.shape[0]
    hdim = inner // heads
    state = b.shape[1]
    out_rows = w_in.shape[0] // n
    bc_rows = 2 * state // n
    chips = s // 2
    scale = (s * tokens * hdim) ** (-0.5)
    vmem = pl.BlockSpec(memory_space=pltpu.VMEM)
    hbm = pl.BlockSpec(memory_space=pltpu.HBM)
    dma = pltpu.SemaphoreType.DMA
    parts = pieces_of(depth, LANES, 4)
    splits = pieces_of(out_rows, 16, 4)

    def wide(dtype):
        return pltpu.VMEM((inner, tokens), dtype)

    def slim(dtype, *lead):
        return pltpu.VMEM((*lead, inner, state), dtype)

    rows = pltpu.VMEM((heads, tokens), F32)
    packet = pltpu.VMEM((2, n - 1, out_rows + bc_rows, tokens), BF16)
    scratch = [
        pltpu.VMEM(w_out.shape, BF16),
        pltpu.VMEM(w_in.shape, BF16),
        pltpu.VMEM((2, n - 1, tokens, depth), BF16),
        wide(F32), wide(BF16), wide(BF16), wide(BF16),
        pltpu.VMEM((heads, tokens, tokens), F32),
        pltpu.VMEM((heads, tokens, tokens), BF16),
        wide(F32), wide(F32), wide(F32), wide(BF16), wide(BF16),
        packet, packet,
        pltpu.VMEM((2 * state, tokens), BF16),
        slim(F32), slim(BF16), slim(BF16), slim(BF16), slim(BF16, chips - 1),
        slim(F32), slim(BF16), slim(BF16), slim(F32),
        pltpu.VMEM((heads, LANES), F32),
        pltpu.VMEM((s - 1, heads, LANES), F32),
        pltpu.VMEM((chips - 1, heads, LANES), F32),
        rows, rows, rows, rows, rows, rows, rows, pltpu.VMEM((heads, state), F32),
        pltpu.VMEM((2, tokens, heads), F32),
        pltpu.VMEM((2, tokens, tokens), F32),
        pltpu.VMEM((8, LANES), F32),
        pltpu.VMEM((s - 1, 8, LANES), F32),
        pltpu.VMEM((bc_rows, tokens), F32),
        dma((2, n - 1, parts)), dma((2, n - 1, parts)), dma((n,)), dma,
        dma((2, n - 1, splits)), dma((2, n - 1, splits)),
        dma((s - 1,)), dma((s - 1,)),
        dma, dma, dma((chips - 1,)), dma((chips - 1,)), dma, dma,
        dma((s - 1,)), dma((s - 1,)),
    ]
    outs = pl.pallas_call(
        functools.partial(layer_kernel, n, s, scale),
        out_shape=(
            jax.ShapeDtypeStruct((out_rows, tokens), BF16),
            jax.ShapeDtypeStruct((bc_rows, tokens), BF16),
            jax.ShapeDtypeStruct((heads, tokens), F32),
            jax.ShapeDtypeStruct((3, heads), F32),
        ),
        in_specs=[vmem] * 9 + [hbm] * 2,
        out_specs=(vmem,) * 4,
        scratch_shapes=scratch,
        compiler_params=pltpu.CompilerParams(
            collective_id=0, has_side_effects=True, vmem_limit_bytes=58 * 2**20
        ),
        name="layer",
    )(og, x, b, c, raw, bias[None], alog[None], skip[None], states, w_out, w_in)
    return handed_on(outs)


def solution(mesh):
    return jax.shard_map(
        layer,
        mesh=mesh,
        in_specs=(
            P("seq", "head"),
            P("seq", "head"),
            P("seq", None),
            P("seq", None),
            P("head", "seq"),
            P("head"),
            P("head"),
            P("head"),
            P("seq", "head", None),
            P("head", None),
            P(None, "head"),
        ),
        out_specs=(P("head", "seq"), P("head", "seq"), P("head", "seq"), P(None, "head")),
        check_vma=False,
    )
```

```python
import functools

import jax
import jax.numpy as jnp
from jax import lax
from jax.experimental import pallas as pl
from jax.experimental.pallas import tpu as pltpu
from jax.sharding import PartitionSpec as P

LAST = (((1,), (1,)), ((), ()))
FIRST = (((0,), (0,)), ((), ()))
PLAIN = (((1,), (0,)), ((), ()))
MESH = pl.DeviceIdType.MESH
EXACT = lax.Precision.HIGHEST
F32, BF16 = jnp.float32, jnp.bfloat16
SKEW = 2
LANES = 128


def dot(a, b, dims=PLAIN, precision=None):
    return lax.dot_general(a, b, dims, precision=precision, preferred_element_type=F32)


def pieces_of(extent, unit, most):
    count = most
    while extent % (count * unit):
        count //= 2
    return count


def remote(src, dst, send, recv, axis, target):
    return pltpu.make_async_remote_copy(
        src_ref=src, dst_ref=dst, send_sem=send, recv_sem=recv,
        device_id={axis: target}, device_id_type=MESH,
    )


def layer_kernel(
    n, s, scale,
    og_hbm, x_hbm, b_hbm, c_hbm, raw_hbm, bias_ref, alog_ref, skip_ref, states_hbm, w_out, w_in,
    o_hbm, obc_hbm, odt_hbm, opar_hbm,
    wo, wi, held, acc, dy, dyd, xt, mask, km, intra, ysta, back, xend, xg,
    going, coming, own_bc, lf, lb, lin, sb, sin, tf, tb, tin, carried,
    et_own, et_in, reach, rows_step, rows_cum, rows_r, rows_xi, rows_st, rows_dx, rows_xs, rows_tail,
    cols, shared, par, par_in, acc_bc, o_ref, obc_ref, odt_ref, opar_ref, og, x_ref, b_ref, c_ref, raw_ref, states,
    in_sem, out_sem, g_send, g_recv, wo_sem, wi_sem, s_send, s_recv, et_send, et_recv,
    l_send, l_recv, st_send, st_recv, t_send, t_recv, p_send, p_recv,
):
    me = lax.axis_index("head")
    mine = lax.axis_index("seq")
    tokens, depth = og.shape
    heads = raw_ref.shape[0]
    inner = x_ref.shape[1]
    hdim = inner // heads
    state = b_ref.shape[1]
    per = LANES // hdim
    chips = s // 2
    chip = mine // 2
    odd = lax.rem(mine, 2) == 1
    even = jnp.logical_not(odd)
    right, left = lax.rem(me + 1, n), lax.rem(me + n - 1, n)
    has_right, has_left = me < n - 1, me > 0
    tile = min(256, inner)

    def w_copy(offset):
        where = pl.ds(pl.multiple_of(lax.rem(me + offset, n) * depth, depth), depth)
        return pltpu.make_async_copy(w_out.at[:, where], wo.at[:, where], wo_sem.at[offset])

    wi_copy = pltpu.make_async_copy(w_in, wi, wi_sem)
    w_order = [0]
    for d in range(n - 1):
        for offset in (n - 1 - d, d + 1):
            if offset not in w_order:
                w_order.append(offset)
    barrier = pltpu.get_barrier_semaphore()
    for neighbour in (left, right):
        pl.semaphore_signal(barrier, inc=1, device_id={"head": neighbour}, device_id_type=MESH)
    for away in range(1, s):
        pl.semaphore_signal(
            barrier, inc=1, device_id={"seq": lax.rem(mine + away, s)}, device_id_type=MESH
        )
    loads = [
        pltpu.make_async_copy(src, dst, in_sem.at[k])
        for k, (src, dst) in enumerate((
            (raw_hbm, raw_ref), (b_hbm, b_ref), (c_hbm, c_ref), (x_hbm, x_ref),
            (states_hbm, states), (og_hbm, og),
        ))
    ]
    for load in loads:
        load.start()

    pl.semaphore_wait(barrier, 2 + s - 1)

    parts = pieces_of(depth, LANES, 4)
    width = depth // parts

    def g_copy(side, d, q):
        where = pl.ds(q * width, width)
        src = og_hbm.at[:, where] if d == 0 else held.at[side, d - 1, :, where]
        return remote(
            src, held.at[side, d, :, where], g_send.at[side, d, q], g_recv.at[side, d, q],
            "head", right if side == 0 else left,
        )

    def g_sends(side, d):
        return (has_right & (me >= d)) if side == 0 else (has_left & (me + d <= n - 1))

    def g_gets(side, d):
        return (me > d) if side == 0 else (me + 1 + d <= n - 1)

    for side in (0, 1):
        @pl.when(g_sends(side, 0))
        def _():
            for q in range(parts):
                g_copy(side, 0, q).start()

    for offset in w_order:
        w_copy(offset).start()
    wi_copy.start()
    for load in loads:
        load.wait()

    def column_of(row):
        at = lax.broadcasted_iota(jnp.int32, (heads, heads), 0)
        along = lax.broadcasted_iota(jnp.int32, (heads, heads), 1)
        return jnp.sum(jnp.where(at == along, row, 0.0), axis=1, keepdims=True)

    bias = column_of(bias_ref[...])
    rate = jnp.exp(column_of(alog_ref[...]))
    skip = column_of(skip_ref[...])
    first = lax.broadcasted_iota(jnp.int32, (tokens, tokens), 0)
    second = lax.broadcasted_iota(jnp.int32, (tokens, tokens), 1)
    upto = (first <= second).astype(F32)
    raw = raw_ref[...] + bias
    step = jnp.maximum(raw, 0.0) + jnp.log1p(jnp.exp(-jnp.abs(raw)))
    log_step = -rate * step
    cum = dot(log_step, upto, precision=EXACT)
    total = cum[:, tokens - 1 : tokens]
    end_decay = jnp.exp(total - cum)
    start_decay = jnp.exp(cum)
    end_total = jnp.exp(total)
    end_weight = step * end_decay
    rows_step[...] = step
    rows_cum[...] = cum
    et_own[...] = jnp.broadcast_to(end_total, et_own.shape)

    def et_copy(away):
        return remote(
            et_own, et_in.at[away - 1], et_send.at[away - 1], et_recv.at[away - 1],
            "seq", lax.rem(mine + s - away, s),
        )

    for away in range(1, s):
        et_copy(away).start()

    eye = (first == second).astype(F32)
    cols[0] = dot(eye, cum, LAST, precision=EXACT)
    cols[1] = dot(eye, step, LAST, precision=EXACT)
    shared[0] = dot(b_ref[...], c_ref[...], LAST)
    shared[1] = jnp.zeros((tokens, tokens), F32)
    lane = lax.broadcasted_iota(jnp.int32, (tokens, heads), 1)

    def masks(h, carry):
        col = jnp.sum(jnp.where(lane == h, cols[0], 0.0), axis=1, keepdims=True)
        col_step = jnp.sum(jnp.where(lane == h, cols[1], 0.0), axis=1, keepdims=True)
        gap = rows_cum[pl.ds(h, 1), :] - col
        value = jnp.where(first <= second, jnp.exp(jnp.minimum(gap, 0.0)) * col_step, 0.0)
        mask[h] = value
        km[h] = (shared[0] * value).astype(BF16)
        return carry

    lax.fori_loop(0, heads, masks, 0)
    eye_bf = eye[:tile, :tile].astype(BF16)
    for k in range(inner // tile):
        where = pl.ds(k * tile, tile)
        xt[where, :] = dot(eye_bf, x_ref[:, where], LAST).astype(BF16)
        ysta[where, :] = dot(states[0, where, :], c_ref[...], LAST)
    ct = dot(eye_bf[:state, :state], c_ref[...], LAST).astype(BF16)
    bt = dot(eye_bf[:state, :state], b_ref[...], LAST).astype(BF16)
    sbt = dot(eye_bf[:state, :state], states[0], LAST).astype(BF16)

    def multiply(source, offset, start, extent, fresh):
        if start == 0:
            w_copy(offset).wait()
        base = lax.rem(me + offset, n) * depth + start
        where = pl.ds(pl.multiple_of(base, extent), extent)

        def body(k, carry):
            outs = pl.ds(pl.multiple_of(k * tile, tile), tile)
            part = dot(wo[outs, where], source[:, pl.ds(start, extent)], LAST)
            acc[outs, :] = part if fresh else acc[outs, :] + part
            return carry

        lax.fori_loop(0, inner // tile, body, 0)

    multiply(og, 0, 0, depth, True)
    for d in range(n - 1):
        for q in range(parts):
            for side in (0, 1):
                @pl.when(g_gets(side, d))
                def _():
                    g_copy(side, d, q).wait_recv()
                if d + 1 < n - 1:
                    @pl.when(g_gets(side, d) & g_sends(side, d + 1))
                    def _():
                        g_copy(side, d + 1, q).start()
            for side in (0, 1):
                @pl.when(g_gets(side, d))
                def _():
                    offset = n - 1 - d if side == 0 else d + 1
                    multiply(held.at[side, d], offset, q * width, width, False)

    shares = 2 if heads % 2 == 0 else 1
    group = heads // shares
    sibling = mine + 1 - 2 * lax.rem(mine, 2)

    def share_rows(k):
        return pl.ds(k * group * hdim, group * hdim)

    def l_copy(k):
        return remote(
            lb.at[share_rows(k)], lin.at[share_rows(k)], l_send.at[k], l_recv.at[k],
            "seq", sibling,
        )

    def t_copy(k):
        return remote(
            tb.at[share_rows(k)], tin.at[share_rows(k)], t_send.at[k], t_recv.at[k],
            "seq", sibling,
        )

    for k in range(shares):
        for h in range(k * group, (k + 1) * group):
            rows = pl.ds(h * hdim, hdim)
            rounded = acc[rows, :].astype(BF16)
            dy[rows, :] = rounded
            dyd[rows, :] = (rounded.astype(F32) * start_decay[h : h + 1, :]).astype(BF16)
        where = share_rows(k)
        value = dot(dyd[where, :], c_ref[...])
        lf[where, :] = value
        lb[where, :] = value.astype(BF16)

        @pl.when(odd)
        def _():
            l_copy(k).start()

    for away in range(1, s):
        et_copy(away).wait_recv()
    weight = jnp.ones((heads, LANES), F32)
    for a in range(1, chips):
        reach[a - 1] = weight
        weight = weight * et_in[2 * a - 1] * et_in[2 * a]

    half_lane = lax.broadcasted_iota(jnp.int32, (tokens, LANES), 1) // hdim

    def intra_heads(pair, carry):
        block = pl.ds(pl.multiple_of(pair * LANES, LANES), LANES)
        x_pair = x_ref[:, block]
        dy_pair = dy[block, :]
        for sub in range(per):
            h = pair * per + sub
            rows = pl.ds(pl.multiple_of(h * hdim, hdim), hdim)
            dots = dot(jnp.where(half_lane == sub, x_pair, jnp.zeros_like(x_pair)), dy_pair)
            shared[1] += dots * mask[h]
            rows_r[pl.ds(h, 1), :] = jnp.sum(dots * km[h].astype(F32), axis=0, keepdims=True)
            dy_h = dy[rows, :]
            x_h = xt[rows, :].astype(F32)
            inside = dot(dy_h, km[h], LAST)
            intra[rows, :] = inside
            wide = dy_h.astype(F32)
            rows_xi[pl.ds(h, 1), :] = jnp.sum(x_h * inside, axis=0, keepdims=True)
            rows_st[pl.ds(h, 1), :] = jnp.sum(wide * ysta[rows, :], axis=0, keepdims=True)
            rows_dx[pl.ds(h, 1), :] = jnp.sum(wide * x_h, axis=0, keepdims=True)
        return carry

    pairs = heads // per
    early = pairs // 8
    lax.fori_loop(0, early, intra_heads, 0)

    def st_copy(a, k):
        return remote(
            sb.at[share_rows(k)], sin.at[a - 1, share_rows(k)],
            st_send.at[a - 1, k], st_recv.at[a - 1, k], "seq", jnp.maximum(mine - 2 * a, 0),
        )

    def over_heads(k, do):
        def body(h, carry):
            do(h, pl.ds(pl.multiple_of(h * hdim, hdim), hdim))
            return carry

        lax.fori_loop(k * group, (k + 1) * group, body, 0)

    for k in range(shares):
        @pl.when(even)
        def _():
            l_copy(k).wait_recv()

            def join(h, rows):
                sb[rows, :] = (
                    lf[rows, :] + et_own[pl.ds(h, 1), :] * lin[rows, :].astype(F32)
                ).astype(BF16)
                tf[rows, :] = jnp.zeros((hdim, state), F32)

            over_heads(k, join)

        for a in range(chips - 1, 0, -1):
            @pl.when(even & (chip >= a))
            def _():
                st_copy(a, k).start()

    lax.fori_loop(early, pairs, intra_heads, 0)

    for k in range(shares):
        for a in range(1, chips):
            @pl.when(even & (chip + a < chips))
            def _():
                st_copy(a, k).wait_recv()

                def add(h, rows):
                    tf[rows, :] += (
                        reach[a - 1, pl.ds(h, 1), :] * sin[a - 1, rows, :].astype(F32)
                    )

                over_heads(k, add)

        @pl.when(even)
        def _():
            tb[share_rows(k), :] = tf[share_rows(k), :].astype(BF16)
            t_copy(k).start()

            def enter(h, rows):
                carried[rows, :] = (
                    lin[rows, :].astype(F32) + et_in[0, pl.ds(h, 1), :] * tf[rows, :]
                )

            over_heads(k, enter)

        @pl.when(odd)
        def _():
            t_copy(k).wait_recv()
            carried[share_rows(k), :] = tin[share_rows(k), :].astype(F32)

        back[share_rows(k), :] = dot(carried[share_rows(k), :].astype(BF16), b_ref[...], LAST)

    for h in range(heads):
        rows = pl.ds(h * hdim, hdim)
        xg[rows, :] = (
            intra[rows, :]
            + end_weight[h : h + 1, :] * back[rows, :]
            + skip[h : h + 1, :] * dy[rows, :].astype(F32)
        ).astype(BF16)

    wi_copy.wait()
    out_rows = o_ref.shape[0]
    bc_rows = obc_ref.shape[0]
    splits = pieces_of(out_rows, 16, 4)
    piece = out_rows // splits

    def s_copy(side, e, q, last):
        rows = pl.ds(pl.multiple_of(q * piece, piece), piece + (bc_rows if last else 0))
        return remote(
            going.at[side, e, rows], coming.at[side, e, rows],
            s_send.at[side, e, q], s_recv.at[side, e, q], "head", right if side == 0 else left,
        )

    def owner_of(side, e):
        return n - 1 - e if side == 0 else e

    def s_sends(side, e):
        return (me < owner_of(side, e)) if side == 0 else (me > owner_of(side, e))

    def s_gets(side, e):
        return (s_sends(side, e) | (me == owner_of(side, e))) & (has_left if side == 0 else has_right)

    def term(owner, q):
        start = pl.multiple_of(owner * out_rows + q * piece, piece)
        return dot(wi[pl.ds(start, piece), :], xg[...])

    count = (n - 1) * splits
    bc_to = pl.ds(out_rows, bc_rows)

    def bc_of(owner):
        return own_bc[pl.ds(pl.multiple_of(owner * bc_rows, bc_rows), bc_rows), :]

    def each(q, do):
        @pl.when(q == splits - 1)
        def _():
            do(True)

        if splits > 1:
            @pl.when(q < splits - 1)
            def _():
                do(False)

    def slot(index, carry):
        for side in (0, 1):
            place = index - SKEW * (me if side == 0 else n - 1 - me)
            held_at = jnp.clip(place, 0, count - 1)
            e, q = lax.div(held_at, splits), lax.rem(held_at, splits)
            owner = owner_of(side, e)
            live = (place >= 0) & (place < count)
            rows = pl.ds(pl.multiple_of(q * piece, piece), piece)

            @pl.when(live & s_sends(side, e))
            def _():
                going[side, e, rows, :] = term(owner, q).astype(BF16)

                @pl.when(q == splits - 1)
                def _():
                    going[side, e, bc_to, :] = bc_of(owner)

                @pl.when(s_gets(side, e))
                def _():
                    def add(last):
                        s_copy(side, e, q, last).wait_recv()
                        for where in (rows, bc_to) if last else (rows,):
                            going[side, e, where, :] = (
                                going[side, e, where, :].astype(F32)
                                + coming[side, e, where, :].astype(F32)
                            ).astype(BF16)

                    each(q, add)

                each(q, lambda last: s_copy(side, e, q, last).start())

            @pl.when(live & (me == owner) & s_gets(side, e))
            def _():
                def take(last):
                    s_copy(side, e, q, last).wait_recv()
                    acc[rows, :] += coming[side, e, rows, :].astype(F32)
                    if last:
                        acc_bc[...] += coming[side, e, bc_to, :].astype(F32)

                each(q, take)

        return carry

    lax.fori_loop(0, SKEW, slot, 0)

    for h in range(heads):
        rows = pl.ds(h * hdim, hdim)
        x_h = xt[rows, :].astype(F32)
        xend[rows, :] = (x_h * end_weight[h : h + 1, :]).astype(BF16)
        rows_xs[h : h + 1, :] = jnp.sum(x_h * back[rows, :], axis=0, keepdims=True)
        rows_tail[h : h + 1, :] = jnp.sum(
            states[0, rows, :].astype(F32) * carried[rows, :], axis=0, keepdims=True
        )
    sums = shared[1].astype(BF16)
    carried_t = dot(eye_bf[:state, :state], carried[...].astype(BF16), LAST).astype(BF16)
    own_bc[:state, :] = (dot(ct, sums, LAST) + dot(carried_t, xend[...])).astype(BF16)
    own_bc[state:, :] = (dot(bt, sums) + dot(sbt, dyd[...])).astype(BF16)

    acc_bc[...] = bc_of(me).astype(F32)
    for q in range(splits):
        acc[pl.ds(q * piece, piece), :] = term(me, q)
    slots = max((n - k) * splits + SKEW * k for k in range(1, n))
    first_part = min(slots, SKEW + 3)
    lax.fori_loop(SKEW, first_part, slot, 0)

    end_terms = end_weight * rows_xs[...]
    cum_grad = rows_r[...] - rows_xi[...] + start_decay * rows_st[...] - end_terms
    tail = jnp.sum(end_terms, axis=1, keepdims=True) + end_total * jnp.sum(
        rows_tail[...], axis=1, keepdims=True
    )
    token = lax.broadcasted_iota(jnp.int32, (heads, tokens), 1)
    cum_grad = cum_grad + jnp.where(token == tokens - 1, tail, 0.0)
    step_grad = dot(cum_grad, upto, LAST, precision=EXACT)
    dt_sum = -rate * step_grad + (rows_xi[...] + end_terms) / step
    dt_grad = dt_sum / (1.0 + jnp.exp(-raw))
    odt_ref[...] = dt_grad
    writes = [
        pltpu.make_async_copy(src, dst, out_sem.at[k])
        for k, (src, dst) in enumerate((
            (o_ref, o_hbm), (obc_ref, obc_hbm), (odt_ref, odt_hbm), (opar_ref, opar_hbm),
        ))
    ]
    writes[2].start()

    def row_of(column):
        at = lax.broadcasted_iota(jnp.int32, (heads, LANES), 0)
        along = lax.broadcasted_iota(jnp.int32, (heads, LANES), 1)
        return jnp.sum(jnp.where(at == along, column, 0.0), axis=0, keepdims=True)

    line = lax.broadcasted_iota(jnp.int32, (8, LANES), 0)
    packet = jnp.zeros((8, LANES), F32)
    for index, terms in enumerate((step_grad * log_step, rows_dx[...], dt_grad)):
        packet = jnp.where(line == index, row_of(jnp.sum(terms, axis=1, keepdims=True)), packet)
    par[...] = packet

    def p_copy(away):
        return remote(
            par, par_in.at[away - 1], p_send.at[away - 1], p_recv.at[away - 1],
            "seq", lax.rem(mine + s - away, s),
        )

    for away in range(1, s):
        p_copy(away).start()

    lax.fori_loop(first_part, slots, slot, 0)

    o_ref[...] = acc[:out_rows, :].astype(BF16)
    writes[0].start()
    obc_ref[...] = acc_bc[...].astype(BF16)
    writes[1].start()
    value = packet
    for away in range(1, s):
        p_copy(away).wait_recv()
        value = value + par_in[away - 1]
    opar_ref[...] = value[: opar_ref.shape[0], :heads] * scale
    writes[3].start()

    for side in (0, 1):
        for d in range(n - 1):
            @pl.when(g_sends(side, d))
            def _():
                for q in range(parts):
                    g_copy(side, d, q).wait_send()

            @pl.when(s_sends(side, d))
            def _():
                for q in range(splits):
                    s_copy(side, d, q, q == splits - 1).wait_send()
    for away in range(1, s):
        et_copy(away).wait_send()
        p_copy(away).wait_send()

    for k in range(shares):
        @pl.when(odd)
        def _():
            l_copy(k).wait_send()

        for a in range(1, chips):
            @pl.when(even & (chip >= a))
            def _():
                st_copy(a, k).wait_send()

        @pl.when(even)
        def _():
            t_copy(k).wait_send()
    for write in writes:
        write.wait()


def hand_on_kernel(*refs):
    count = len(refs) // 2
    for k in range(count):
        refs[count + k][...] = refs[k][...]


def handed_on(arrays):
    vmem = pl.BlockSpec(memory_space=pltpu.VMEM)
    return pl.pallas_call(
        hand_on_kernel,
        out_shape=tuple(jax.ShapeDtypeStruct(a.shape, a.dtype) for a in arrays),
        in_specs=[vmem] * len(arrays),
        out_specs=(vmem,) * len(arrays),
        name="hand_on",
    )(*arrays)


def layer(og, x, b, c, raw, bias, alog, skip, states, w_out, w_in):
    n, s = lax.axis_size("head"), lax.axis_size("seq")
    tokens, depth = og.shape
    inner = x.shape[1]
    heads = raw.shape[0]
    hdim = inner // heads
    state = b.shape[1]
    out_rows = w_in.shape[0] // n
    bc_rows = 2 * state // n
    chips = s // 2
    scale = (s * tokens * hdim) ** (-0.5)
    vmem = pl.BlockSpec(memory_space=pltpu.VMEM)
    hbm = pl.BlockSpec(memory_space=pltpu.HBM)
    dma = pltpu.SemaphoreType.DMA
    parts = pieces_of(depth, LANES, 4)
    splits = pieces_of(out_rows, 16, 4)

    def wide(dtype):
        return pltpu.VMEM((inner, tokens), dtype)

    def slim(dtype, *lead):
        return pltpu.VMEM((*lead, inner, state), dtype)

    results = (
        jax.ShapeDtypeStruct((out_rows, tokens), BF16),
        jax.ShapeDtypeStruct((bc_rows, tokens), BF16),
        jax.ShapeDtypeStruct((heads, tokens), F32),
        jax.ShapeDtypeStruct((3, heads), F32),
    )
    rows = pltpu.VMEM((heads, tokens), F32)
    packet = pltpu.VMEM((2, n - 1, out_rows + bc_rows, tokens), BF16)
    scratch = [
        pltpu.VMEM(w_out.shape, BF16),
        pltpu.VMEM(w_in.shape, BF16),
        pltpu.VMEM((2, n - 1, tokens, depth), BF16),
        wide(F32), wide(BF16), wide(BF16), wide(BF16),
        pltpu.VMEM((heads, tokens, tokens), F32),
        pltpu.VMEM((heads, tokens, tokens), BF16),
        wide(F32), wide(F32), wide(F32), wide(BF16), wide(BF16),
        packet, packet,
        pltpu.VMEM((2 * state, tokens), BF16),
        slim(F32), slim(BF16), slim(BF16), slim(BF16), slim(BF16, chips - 1),
        slim(F32), slim(BF16), slim(BF16), slim(F32),
        pltpu.VMEM((heads, LANES), F32),
        pltpu.VMEM((s - 1, heads, LANES), F32),
        pltpu.VMEM((chips - 1, heads, LANES), F32),
        rows, rows, rows, rows, rows, rows, rows, pltpu.VMEM((heads, state), F32),
        pltpu.VMEM((2, tokens, heads), F32),
        pltpu.VMEM((2, tokens, tokens), F32),
        pltpu.VMEM((8, LANES), F32),
        pltpu.VMEM((s - 1, 8, LANES), F32),
        pltpu.VMEM((bc_rows, tokens), F32),
        *[pltpu.VMEM(a.shape, a.dtype) for a in results],
        *[pltpu.VMEM(a.shape, a.dtype) for a in (og, x, b, c, raw, states)],
        dma((6,)), dma((4,)), dma((2, n - 1, parts)), dma((2, n - 1, parts)), dma((n,)), dma,
        dma((2, n - 1, splits)), dma((2, n - 1, splits)),
        dma((s - 1,)), dma((s - 1,)),
        dma((2,)), dma((2,)), dma((chips - 1, 2)), dma((chips - 1, 2)), dma((2,)), dma((2,)),
        dma((s - 1,)), dma((s - 1,)),
    ]
    outs = pl.pallas_call(
        functools.partial(layer_kernel, n, s, scale),
        out_shape=results,
        in_specs=[hbm] * 5 + [vmem] * 3 + [hbm] * 3,
        out_specs=(hbm,) * 4,
        scratch_shapes=scratch,
        compiler_params=pltpu.CompilerParams(
            collective_id=0, has_side_effects=True, vmem_limit_bytes=58 * 2**20
        ),
        name="layer",
    )(og, x, b, c, raw, bias[None], alog[None], skip[None], states, w_out, w_in)
    return handed_on(outs)


def solution(mesh):
    return jax.shard_map(
        layer,
        mesh=mesh,
        in_specs=(
            P("seq", "head"),
            P("seq", "head"),
            P("seq", None),
            P("seq", None),
            P("head", "seq"),
            P("head"),
            P("head"),
            P("head"),
            P("seq", "head", None),
            P("head", None),
            P(None, "head"),
        ),
        out_specs=(P("head", "seq"), P("head", "seq"), P("head", "seq"), P(None, "head")),
        check_vma=False,
    )
```

```python
import functools

import jax
import jax.numpy as jnp
from jax import lax
from jax.experimental import pallas as pl
from jax.experimental.pallas import tpu as pltpu
from jax.sharding import PartitionSpec as P

LAST = (((1,), (1,)), ((), ()))
FIRST = (((0,), (0,)), ((), ()))
PLAIN = (((1,), (0,)), ((), ()))
MESH = pl.DeviceIdType.MESH
EXACT = lax.Precision.HIGHEST
F32, BF16 = jnp.float32, jnp.bfloat16
SKEW = 3
LANES = 128


def dot(a, b, dims=PLAIN, precision=None):
    return lax.dot_general(a, b, dims, precision=precision, preferred_element_type=F32)


def pieces_of(extent, unit, most):
    count = most
    while extent % (count * unit):
        count //= 2
    return count


def remote(src, dst, send, recv, axis, target):
    return pltpu.make_async_remote_copy(
        src_ref=src, dst_ref=dst, send_sem=send, recv_sem=recv,
        device_id={axis: target}, device_id_type=MESH,
    )


def layer_kernel(
    n, s, scale,
    og_hbm, x_hbm, b_hbm, c_hbm, raw_hbm, bias_ref, alog_ref, skip_ref, states_hbm, w_out, w_in,
    o_hbm, obc_hbm, odt_hbm, opar_hbm,
    wo, wi, held, acc, dy, dyd, xt, mask, km, intra, ysta, back, xend, xg,
    going, coming, own_bc, lf, lb, lin, sb, sin, tf, tb, tin, carried,
    et_own, et_in, reach, rows_step, rows_cum, rows_r, rows_xi, rows_st, rows_dx, rows_xs, rows_tail,
    cols, shared, par, par_in, acc_bc, gbc, cbc, wh, xe, hbc, o_ref, obc_ref, odt_ref, opar_ref, og, x_ref, b_ref, c_ref, raw_ref, states,
    in_sem, out_sem, g_send, g_recv, wo_sem, wi_sem, s_send, s_recv, et_send, et_recv,
    l_send, l_recv, st_send, st_recv, t_send, t_recv, p_send, p_recv,
    b_send, b_recv, w1_send, w1_recv, w2_send, w2_recv, w3_send, w3_recv, x_send, x_recv, h_send, h_recv,
):
    me = lax.axis_index("head")
    mine = lax.axis_index("seq")
    tokens, depth = og.shape
    heads = raw_ref.shape[0]
    inner = x_ref.shape[1]
    hdim = inner // heads
    state = b_ref.shape[1]
    per = LANES // hdim
    chips = s // 2
    chip = mine // 2
    odd = lax.rem(mine, 2) == 1
    even = jnp.logical_not(odd)
    right, left = lax.rem(me + 1, n), lax.rem(me + n - 1, n)
    has_right, has_left = me < n - 1, me > 0
    tile = min(256, inner)

    def w_copy(offset):
        where = pl.ds(pl.multiple_of(lax.rem(me + offset, n) * depth, depth), depth)
        return pltpu.make_async_copy(w_out.at[:, where], wo.at[:, where], wo_sem.at[offset])

    wi_copy = pltpu.make_async_copy(w_in, wi, wi_sem)
    w_order = [0]
    for d in range(n - 1):
        for offset in (n - 1 - d, d + 1):
            if offset not in w_order:
                w_order.append(offset)
    barrier = pltpu.get_barrier_semaphore()
    for neighbour in (left, right):
        pl.semaphore_signal(barrier, inc=1, device_id={"head": neighbour}, device_id_type=MESH)
    for away in range(1, s):
        pl.semaphore_signal(
            barrier, inc=1, device_id={"seq": lax.rem(mine + away, s)}, device_id_type=MESH
        )
    loads = [
        pltpu.make_async_copy(src, dst, in_sem.at[k])
        for k, (src, dst) in enumerate((
            (raw_hbm, raw_ref), (b_hbm, b_ref), (c_hbm, c_ref), (x_hbm, x_ref),
            (states_hbm, states), (og_hbm, og),
        ))
    ]
    for load in loads:
        load.start()

    pl.semaphore_wait(barrier, 2 + s - 1)

    leans = n >= 4
    out_rows, bc_rows = o_ref.shape[0], obc_ref.shape[0]
    is_end = leans & ((me == 0) | (me == n - 1))
    is_helper = leans & ((me == 1) | (me == n - 2))
    helper = jnp.where(me == 0, 1, n - 2)
    sibling = mine + 1 - 2 * lax.rem(mine, 2)

    def end_of(side):
        return leans & (me == (0 if side == 0 else n - 1))

    def helper_of(side):
        return leans & (me == (1 if side == 0 else n - 2))

    share = wh.shape[0] // s
    cuts = w1_send.shape[0]
    cut = share // cuts

    def lent(place, q):
        return pl.ds(pl.multiple_of(lax.rem(place + s, s) * share + q * cut, cut), cut)

    def w1_copy(q):
        start = jnp.where(me == 0, 2 * out_rows, 0) + mine * share + q * cut
        return remote(
            w_in.at[pl.ds(pl.multiple_of(start, 16), cut)], wh.at[lent(mine, q)],
            w1_send.at[q], w1_recv.at[q], "head", helper,
        )

    def w2_copy(a, q, place):
        return remote(
            wh.at[lent(place, q)], wh.at[lent(place, q)],
            w2_send.at[a - 1, q], w2_recv.at[a - 1, q], "seq", lax.rem(mine + 2 * a, s),
        )

    def w3_copy(a, q, place):
        return remote(
            wh.at[lent(place, q)], wh.at[lent(place, q)],
            w3_send.at[a, q], w3_recv.at[a, q], "seq", sibling,
        )

    parts = pieces_of(depth, LANES, 4)
    width = depth // parts

    def g_copy(side, d, q):
        where = pl.ds(q * width, width)
        src = og_hbm.at[:, where] if d == 0 else held.at[side, d - 1, :, where]
        return remote(
            src, held.at[side, d, :, where], g_send.at[side, d, q], g_recv.at[side, d, q],
            "head", right if side == 0 else left,
        )

    def g_sends(side, d):
        return (has_right & (me >= d)) if side == 0 else (has_left & (me + d <= n - 1))

    def g_gets(side, d):
        return (me > d) if side == 0 else (me + 1 + d <= n - 1)

    for side in (0, 1):
        @pl.when(g_sends(side, 0))
        def _():
            for q in range(parts):
                g_copy(side, 0, q).start()

    for offset in w_order:
        w_copy(offset).start()
    wi_copy.start()
    for load in loads:
        load.wait()

    def column_of(row):
        at = lax.broadcasted_iota(jnp.int32, (heads, heads), 0)
        along = lax.broadcasted_iota(jnp.int32, (heads, heads), 1)
        return jnp.sum(jnp.where(at == along, row, 0.0), axis=1, keepdims=True)

    bias = column_of(bias_ref[...])
    rate = jnp.exp(column_of(alog_ref[...]))
    skip = column_of(skip_ref[...])
    first = lax.broadcasted_iota(jnp.int32, (tokens, tokens), 0)
    second = lax.broadcasted_iota(jnp.int32, (tokens, tokens), 1)
    upto = (first <= second).astype(F32)
    raw = raw_ref[...] + bias
    step = jnp.maximum(raw, 0.0) + jnp.log1p(jnp.exp(-jnp.abs(raw)))
    log_step = -rate * step
    cum = dot(log_step, upto, precision=EXACT)
    total = cum[:, tokens - 1 : tokens]
    end_decay = jnp.exp(total - cum)
    start_decay = jnp.exp(cum)
    end_total = jnp.exp(total)
    end_weight = step * end_decay
    rows_step[...] = step
    rows_cum[...] = cum
    et_own[...] = jnp.broadcast_to(end_total, et_own.shape)

    def et_copy(away):
        return remote(
            et_own, et_in.at[away - 1], et_send.at[away - 1], et_recv.at[away - 1],
            "seq", lax.rem(mine + s - away, s),
        )

    for away in range(1, s):
        et_copy(away).start()

    eye = (first == second).astype(F32)
    cols[0] = dot(eye, cum, LAST, precision=EXACT)
    cols[1] = dot(eye, step, LAST, precision=EXACT)
    shared[0] = dot(b_ref[...], c_ref[...], LAST)
    shared[1] = jnp.zeros((tokens, tokens), F32)
    lane = lax.broadcasted_iota(jnp.int32, (tokens, heads), 1)

    def masks(h, carry):
        col = jnp.sum(jnp.where(lane == h, cols[0], 0.0), axis=1, keepdims=True)
        col_step = jnp.sum(jnp.where(lane == h, cols[1], 0.0), axis=1, keepdims=True)
        gap = rows_cum[pl.ds(h, 1), :] - col
        value = jnp.where(first <= second, jnp.exp(jnp.minimum(gap, 0.0)) * col_step, 0.0)
        mask[h] = value
        km[h] = (shared[0] * value).astype(BF16)
        return carry

    lax.fori_loop(0, heads, masks, 0)
    eye_bf = eye[:tile, :tile].astype(BF16)
    for k in range(inner // tile):
        where = pl.ds(k * tile, tile)
        xt[where, :] = dot(eye_bf, x_ref[:, where], LAST).astype(BF16)
        ysta[where, :] = dot(states[0, where, :], c_ref[...], LAST)
    ct = dot(eye_bf[:state, :state], c_ref[...], LAST).astype(BF16)
    bt = dot(eye_bf[:state, :state], b_ref[...], LAST).astype(BF16)
    sbt = dot(eye_bf[:state, :state], states[0], LAST).astype(BF16)

    def multiply(source, offset, start, extent, fresh):
        if start == 0:
            w_copy(offset).wait()
        base = lax.rem(me + offset, n) * depth + start
        where = pl.ds(pl.multiple_of(base, extent), extent)

        def body(k, carry):
            outs = pl.ds(pl.multiple_of(k * tile, tile), tile)
            part = dot(wo[outs, where], source[:, pl.ds(start, extent)], LAST)
            acc[outs, :] = part if fresh else acc[outs, :] + part
            return carry

        lax.fori_loop(0, inner // tile, body, 0)

    multiply(og, 0, 0, depth, True)
    for side in (0, 1):
        @pl.when(end_of(side))
        def _():
            for q in range(parts):
                g_copy(side, 0, q).wait_send()
            for q in range(cuts):
                w1_copy(q).start()

    for d in range(n - 1):
        for q in range(parts):
            for side in (0, 1):
                @pl.when(g_gets(side, d))
                def _():
                    g_copy(side, d, q).wait_recv()
                if d + 1 < n - 1:
                    @pl.when(g_gets(side, d) & g_sends(side, d + 1))
                    def _():
                        g_copy(side, d + 1, q).start()
            if d == 1 and q < cuts:
                @pl.when(is_helper)
                def _():
                    w1_copy(q).wait_recv()
                    for a in range(1, chips):
                        w2_copy(a, q, mine).start()
                    w3_copy(0, q, mine).start()
            for side in (0, 1):
                @pl.when(g_gets(side, d))
                def _():
                    offset = n - 1 - d if side == 0 else d + 1
                    multiply(held.at[side, d], offset, q * width, width, False)

    shares = 2 if heads % 2 == 0 else 1
    group = heads // shares

    def share_rows(k):
        return pl.ds(k * group * hdim, group * hdim)

    def l_copy(k):
        return remote(
            lb.at[share_rows(k)], lin.at[share_rows(k)], l_send.at[k], l_recv.at[k],
            "seq", sibling,
        )

    def t_copy(k):
        return remote(
            tb.at[share_rows(k)], tin.at[share_rows(k)], t_send.at[k], t_recv.at[k],
            "seq", sibling,
        )

    for k in range(shares):
        for h in range(k * group, (k + 1) * group):
            rows = pl.ds(h * hdim, hdim)
            rounded = acc[rows, :].astype(BF16)
            dy[rows, :] = rounded
            dyd[rows, :] = (rounded.astype(F32) * start_decay[h : h + 1, :]).astype(BF16)
        where = share_rows(k)
        value = dot(dyd[where, :], c_ref[...])
        lf[where, :] = value
        lb[where, :] = value.astype(BF16)

        @pl.when(odd)
        def _():
            l_copy(k).start()

    for away in range(1, s):
        et_copy(away).wait_recv()
    weight = jnp.ones((heads, LANES), F32)
    for a in range(1, chips):
        reach[a - 1] = weight
        weight = weight * et_in[2 * a - 1] * et_in[2 * a]

    half_lane = lax.broadcasted_iota(jnp.int32, (tokens, LANES), 1) // hdim

    def intra_heads(pair, carry):
        block = pl.ds(pl.multiple_of(pair * LANES, LANES), LANES)
        x_pair = x_ref[:, block]
        dy_pair = dy[block, :]
        for sub in range(per):
            h = pair * per + sub
            rows = pl.ds(pl.multiple_of(h * hdim, hdim), hdim)
            dots = dot(jnp.where(half_lane == sub, x_pair, jnp.zeros_like(x_pair)), dy_pair)
            shared[1] += dots * mask[h]
            rows_r[pl.ds(h, 1), :] = jnp.sum(dots * km[h].astype(F32), axis=0, keepdims=True)
            dy_h = dy[rows, :]
            x_h = xt[rows, :].astype(F32)
            inside = dot(dy_h, km[h], LAST)
            intra[rows, :] = inside
            wide = dy_h.astype(F32)
            rows_xi[pl.ds(h, 1), :] = jnp.sum(x_h * inside, axis=0, keepdims=True)
            rows_st[pl.ds(h, 1), :] = jnp.sum(wide * ysta[rows, :], axis=0, keepdims=True)
            rows_dx[pl.ds(h, 1), :] = jnp.sum(wide * x_h, axis=0, keepdims=True)
        return carry

    pairs = heads // per
    early = pairs // 8
    lax.fori_loop(0, early, intra_heads, 0)

    def st_copy(a, k):
        return remote(
            sb.at[share_rows(k)], sin.at[a - 1, share_rows(k)],
            st_send.at[a - 1, k], st_recv.at[a - 1, k], "seq", jnp.maximum(mine - 2 * a, 0),
        )

    def over_heads(k, do):
        def body(h, carry):
            do(h, pl.ds(pl.multiple_of(h * hdim, hdim), hdim))
            return carry

        lax.fori_loop(k * group, (k + 1) * group, body, 0)

    for k in range(shares):
        @pl.when(even)
        def _():
            l_copy(k).wait_recv()

            def join(h, rows):
                sb[rows, :] = (
                    lf[rows, :] + et_own[pl.ds(h, 1), :] * lin[rows, :].astype(F32)
                ).astype(BF16)
                tf[rows, :] = jnp.zeros((hdim, state), F32)

            over_heads(k, join)

        for a in range(chips - 1, 0, -1):
            @pl.when(even & (chip >= a))
            def _():
                st_copy(a, k).start()

    lax.fori_loop(early, pairs, intra_heads, 0)

    for k in range(shares):
        for a in range(1, chips):
            @pl.when(even & (chip + a < chips))
            def _():
                st_copy(a, k).wait_recv()

                def add(h, rows):
                    tf[rows, :] += (
                        reach[a - 1, pl.ds(h, 1), :] * sin[a - 1, rows, :].astype(F32)
                    )

                over_heads(k, add)

        @pl.when(even)
        def _():
            tb[share_rows(k), :] = tf[share_rows(k), :].astype(BF16)
            t_copy(k).start()

            def enter(h, rows):
                carried[rows, :] = (
                    lin[rows, :].astype(F32) + et_in[0, pl.ds(h, 1), :] * tf[rows, :]
                )

            over_heads(k, enter)

        @pl.when(odd)
        def _():
            t_copy(k).wait_recv()
            carried[share_rows(k), :] = tin[share_rows(k), :].astype(F32)

        back[share_rows(k), :] = dot(carried[share_rows(k), :].astype(BF16), b_ref[...], LAST)

    halves = xg.shape[0]
    span = tokens // halves

    def x_copy(k, part):
        rows = pl.ds(part * (inner // 2), inner // 2)
        return remote(
            xg.at[k, rows], xe.at[k, rows], x_send.at[k, part], x_recv.at[k, part], "head", helper
        )

    for k in range(halves):
        where = pl.ds(k * span, span)
        for h in range(heads):
            rows = pl.ds(h * hdim, hdim)
            xg[k, rows, :] = (
                intra[rows, where]
                + end_weight[h : h + 1, k * span : (k + 1) * span] * back[rows, where]
                + skip[h : h + 1, :] * dy[rows, where].astype(F32)
            ).astype(BF16)

        if k == 0:
            @pl.when(is_end)
            def _():
                for part in (0, 1):
                    x_copy(0, part).start()

    wi_copy.wait()

    @pl.when(is_helper)
    def _():
        for q in range(cuts):
            for a in range(1, chips):
                w2_copy(a, q, mine - 2 * a).wait_recv()
                w3_copy(a, q, mine - 2 * a).start()
        for q in range(cuts):
            for a in range(chips):
                w3_copy(a, q, sibling - 2 * a).wait_recv()

    strips = s_send.shape[2] // halves
    splits = strips * halves
    piece = out_rows // strips

    def s_copy(side, e, k, strip):
        rows = pl.ds(pl.multiple_of(strip * piece, piece), piece)
        q = k * strips + strip
        return remote(
            going.at[side, e, k, rows], coming.at[side, e, k, rows],
            s_send.at[side, e, q], s_recv.at[side, e, q], "head", right if side == 0 else left,
        )

    def b_copy(side, e):
        return remote(
            gbc.at[side, e], cbc.at[side, e], b_send.at[side, e], b_recv.at[side, e],
            "head", right if side == 0 else left,
        )

    leant = (n - 2) * bc_rows

    def h_copy():
        start = pl.multiple_of(jnp.where(me == 0, 2 * bc_rows, 0), bc_rows)
        return remote(own_bc.at[pl.ds(start, leant)], hbc, h_send, h_recv, "head", helper)

    def owner_of(side, e):
        return n - 1 - e if side == 0 else e

    def s_sends(side, e):
        return (me < owner_of(side, e)) if side == 0 else (me > owner_of(side, e))

    def s_gets(side, e):
        return (s_sends(side, e) | (me == owner_of(side, e))) & (has_left if side == 0 else has_right)

    def term(owner, k, strip):
        start = pl.multiple_of(owner * out_rows + strip * piece, piece)
        return dot(wi[pl.ds(start, piece), :], xg[k])

    count = (n - 1) * splits

    def bc_of(owner):
        return own_bc[pl.ds(pl.multiple_of(owner * bc_rows, bc_rows), bc_rows), :]

    def slot(index, carry):
        for side in (0, 1):
            place = index - SKEW * (me if side == 0 else n - 1 - me)
            held_at = jnp.clip(place, 0, count - 1)
            e, q = lax.div(held_at, splits), lax.rem(held_at, splits)
            k, strip = lax.div(q, strips), lax.rem(q, strips)
            owner = owner_of(side, e)
            live = (place >= 0) & (place < count)
            rows = pl.ds(pl.multiple_of(strip * piece, piece), piece)
            sends = live & s_sends(side, e)
            aided = helper_of(side) & (e < n - 2)
            far = owner - 2 if side == 0 else owner
            passes = jnp.logical_not(end_of(side) & (e < n - 2))
            gets = s_gets(side, e) & jnp.logical_not(aided)
            closes = q == splits - 1

            for one in range(halves):
                @pl.when(helper_of(side) & (place == one * strips))
                def _():
                    for part in (0, 1):
                        x_copy(one, part).wait_recv()

            @pl.when(helper_of(side) & (place == splits - 1))
            def _():
                h_copy().wait_recv()

            @pl.when(sends & passes)
            def _():
                going[side, e, k, rows, :] = term(owner, k, strip).astype(BF16)

                @pl.when(aided)
                def _():
                    start = pl.multiple_of(far * out_rows + strip * piece, piece)
                    aid = dot(wh[pl.ds(start, piece), :], xe[k])
                    going[side, e, k, rows, :] = (
                        going[side, e, k, rows, :].astype(F32) + aid
                    ).astype(BF16)

                @pl.when(gets)
                def _():
                    s_copy(side, e, k, strip).wait_recv()
                    going[side, e, k, rows, :] = (
                        going[side, e, k, rows, :].astype(F32)
                        + coming[side, e, k, rows, :].astype(F32)
                    ).astype(BF16)

                s_copy(side, e, k, strip).start()

            @pl.when(sends & passes & closes)
            def _():
                gbc[side, e] = bc_of(owner)

                @pl.when(aided)
                def _():
                    start = pl.multiple_of(far * bc_rows, bc_rows)
                    gbc[side, e] = (
                        gbc[side, e].astype(F32) + hbc[pl.ds(start, bc_rows), :].astype(F32)
                    ).astype(BF16)

                @pl.when(gets)
                def _():
                    b_copy(side, e).wait_recv()
                    gbc[side, e] = (
                        gbc[side, e].astype(F32) + cbc[side, e].astype(F32)
                    ).astype(BF16)

                b_copy(side, e).start()

            @pl.when(live & (me == owner) & gets)
            def _():
                s_copy(side, e, k, strip).wait_recv()
                where = pl.ds(pl.multiple_of(k * span, span), span)
                acc[rows, where] += coming[side, e, k, rows, :].astype(F32)

                @pl.when(closes)
                def _():
                    b_copy(side, e).wait_recv()
                    acc_bc[...] += cbc[side, e].astype(F32)

        return carry

    lax.fori_loop(0, SKEW, slot, 0)

    for h in range(heads):
        rows = pl.ds(h * hdim, hdim)
        x_h = xt[rows, :].astype(F32)
        xend[rows, :] = (x_h * end_weight[h : h + 1, :]).astype(BF16)
        rows_xs[h : h + 1, :] = jnp.sum(x_h * back[rows, :], axis=0, keepdims=True)
        rows_tail[h : h + 1, :] = jnp.sum(
            states[0, rows, :].astype(F32) * carried[rows, :], axis=0, keepdims=True
        )
    sums = shared[1].astype(BF16)
    carried_t = dot(eye_bf[:state, :state], carried[...].astype(BF16), LAST).astype(BF16)
    own_bc[:state, :] = (dot(ct, sums, LAST) + dot(carried_t, xend[...])).astype(BF16)
    own_bc[state:, :] = (dot(bt, sums) + dot(sbt, dyd[...])).astype(BF16)

    @pl.when(is_end)
    def _():
        for part in (0, 1):
            x_copy(0, part).wait_send()
            for k in range(1, halves):
                x_copy(k, part).start()
        h_copy().start()

    acc_bc[...] = bc_of(me).astype(F32)
    for k in range(halves):
        for strip in range(strips):
            acc[pl.ds(strip * piece, piece), pl.ds(k * span, span)] = term(me, k, strip)
    slots = max((n - k) * splits + SKEW * k for k in range(1, n))
    first_part = min(slots, SKEW + 3)
    lax.fori_loop(SKEW, first_part, slot, 0)

    end_terms = end_weight * rows_xs[...]
    cum_grad = rows_r[...] - rows_xi[...] + start_decay * rows_st[...] - end_terms
    tail = jnp.sum(end_terms, axis=1, keepdims=True) + end_total * jnp.sum(
        rows_tail[...], axis=1, keepdims=True
    )
    token = lax.broadcasted_iota(jnp.int32, (heads, tokens), 1)
    cum_grad = cum_grad + jnp.where(token == tokens - 1, tail, 0.0)
    step_grad = dot(cum_grad, upto, LAST, precision=EXACT)
    dt_sum = -rate * step_grad + (rows_xi[...] + end_terms) / step
    dt_grad = dt_sum / (1.0 + jnp.exp(-raw))
    odt_ref[...] = dt_grad
    writes = [
        pltpu.make_async_copy(src, dst, out_sem.at[k])
        for k, (src, dst) in enumerate((
            (o_ref, o_hbm), (obc_ref, obc_hbm), (odt_ref, odt_hbm), (opar_ref, opar_hbm),
        ))
    ]
    writes[2].start()

    def row_of(column):
        at = lax.broadcasted_iota(jnp.int32, (heads, LANES), 0)
        along = lax.broadcasted_iota(jnp.int32, (heads, LANES), 1)
        return jnp.sum(jnp.where(at == along, column, 0.0), axis=0, keepdims=True)

    line = lax.broadcasted_iota(jnp.int32, (8, LANES), 0)
    packet = jnp.zeros((8, LANES), F32)
    for index, terms in enumerate((step_grad * log_step, rows_dx[...], dt_grad)):
        packet = jnp.where(line == index, row_of(jnp.sum(terms, axis=1, keepdims=True)), packet)
    par[...] = packet

    def p_copy(away):
        return remote(
            par, par_in.at[away - 1], p_send.at[away - 1], p_recv.at[away - 1],
            "seq", lax.rem(mine + s - away, s),
        )

    for away in range(1, s):
        p_copy(away).start()

    @pl.when(is_end)
    def _():
        for k in range(1, halves):
            for part in (0, 1):
                x_copy(k, part).wait_send()

    lax.fori_loop(first_part, slots, slot, 0)

    o_ref[...] = acc[:out_rows, :].astype(BF16)
    writes[0].start()
    obc_ref[...] = acc_bc[...].astype(BF16)
    writes[1].start()
    value = packet
    for away in range(1, s):
        p_copy(away).wait_recv()
        value = value + par_in[away - 1]
    opar_ref[...] = value[: opar_ref.shape[0], :heads] * scale
    writes[3].start()

    for side in (0, 1):
        for d in range(n - 1):
            @pl.when(g_sends(side, d) & (jnp.logical_not(end_of(side)) if d == 0 else True))
            def _():
                for q in range(parts):
                    g_copy(side, d, q).wait_send()

            skipped = end_of(side) if d < n - 2 else False

            @pl.when(s_sends(side, d) & jnp.logical_not(skipped))
            def _():
                for k in range(halves):
                    for strip in range(strips):
                        s_copy(side, d, k, strip).wait_send()
                b_copy(side, d).wait_send()

    @pl.when(is_end)
    def _():
        for q in range(cuts):
            w1_copy(q).wait_send()
        h_copy().wait_send()

    @pl.when(is_helper)
    def _():
        for q in range(cuts):
            for a in range(chips):
                if a > 0:
                    w2_copy(a, q, mine).wait_send()
                w3_copy(a, q, mine - 2 * a).wait_send()

    for away in range(1, s):
        et_copy(away).wait_send()
        p_copy(away).wait_send()

    for k in range(shares):
        @pl.when(odd)
        def _():
            l_copy(k).wait_send()

        for a in range(1, chips):
            @pl.when(even & (chip >= a))
            def _():
                st_copy(a, k).wait_send()

        @pl.when(even)
        def _():
            t_copy(k).wait_send()
    for write in writes:
        write.wait()


def hand_on_kernel(*refs):
    count = len(refs) // 2
    for k in range(count):
        refs[count + k][...] = refs[k][...]


def handed_on(arrays):
    vmem = pl.BlockSpec(memory_space=pltpu.VMEM)
    return pl.pallas_call(
        hand_on_kernel,
        out_shape=tuple(jax.ShapeDtypeStruct(a.shape, a.dtype) for a in arrays),
        in_specs=[vmem] * len(arrays),
        out_specs=(vmem,) * len(arrays),
        name="hand_on",
    )(*arrays)


def layer(og, x, b, c, raw, bias, alog, skip, states, w_out, w_in):
    n, s = lax.axis_size("head"), lax.axis_size("seq")
    tokens, depth = og.shape
    inner = x.shape[1]
    heads = raw.shape[0]
    hdim = inner // heads
    state = b.shape[1]
    out_rows = w_in.shape[0] // n
    bc_rows = 2 * state // n
    chips = s // 2
    scale = (s * tokens * hdim) ** (-0.5)
    vmem = pl.BlockSpec(memory_space=pltpu.VMEM)
    hbm = pl.BlockSpec(memory_space=pltpu.HBM)
    dma = pltpu.SemaphoreType.DMA
    parts = pieces_of(depth, LANES, 4)
    halves = 2 if tokens % (2 * LANES) == 0 else 1
    splits = pieces_of(out_rows, 16, 2) * halves
    lent = max(n - 2, 1) * out_rows
    cuts = pieces_of(lent // s, 16, parts)
    leant = max(n - 2, 1) * bc_rows

    def wide(dtype):
        return pltpu.VMEM((inner, tokens), dtype)

    def slim(dtype, *lead):
        return pltpu.VMEM((*lead, inner, state), dtype)

    results = (
        jax.ShapeDtypeStruct((out_rows, tokens), BF16),
        jax.ShapeDtypeStruct((bc_rows, tokens), BF16),
        jax.ShapeDtypeStruct((heads, tokens), F32),
        jax.ShapeDtypeStruct((3, heads), F32),
    )
    rows = pltpu.VMEM((heads, tokens), F32)
    packet = pltpu.VMEM((2, n - 1, halves, out_rows, tokens // halves), BF16)
    bc_packet = pltpu.VMEM((2, n - 1, bc_rows, tokens), BF16)
    shared_x = pltpu.VMEM((halves, inner, tokens // halves), BF16)
    scratch = [
        pltpu.VMEM(w_out.shape, BF16),
        pltpu.VMEM(w_in.shape, BF16),
        pltpu.VMEM((2, n - 1, tokens, depth), BF16),
        wide(F32), wide(BF16), wide(BF16), wide(BF16),
        pltpu.VMEM((heads, tokens, tokens), F32),
        pltpu.VMEM((heads, tokens, tokens), BF16),
        wide(F32), wide(F32), wide(F32), wide(BF16), shared_x,
        packet, packet,
        pltpu.VMEM((2 * state, tokens), BF16),
        slim(F32), slim(BF16), slim(BF16), slim(BF16), slim(BF16, chips - 1),
        slim(F32), slim(BF16), slim(BF16), slim(F32),
        pltpu.VMEM((heads, LANES), F32),
        pltpu.VMEM((s - 1, heads, LANES), F32),
        pltpu.VMEM((chips - 1, heads, LANES), F32),
        rows, rows, rows, rows, rows, rows, rows, pltpu.VMEM((heads, state), F32),
        pltpu.VMEM((2, tokens, heads), F32),
        pltpu.VMEM((2, tokens, tokens), F32),
        pltpu.VMEM((8, LANES), F32),
        pltpu.VMEM((s - 1, 8, LANES), F32),
        pltpu.VMEM((bc_rows, tokens), F32), bc_packet, bc_packet,
        pltpu.VMEM((lent, inner), BF16), shared_x, pltpu.VMEM((leant, tokens), BF16),
        *[pltpu.VMEM(a.shape, a.dtype) for a in results],
        *[pltpu.VMEM(a.shape, a.dtype) for a in (og, x, b, c, raw, states)],
        dma((6,)), dma((4,)), dma((2, n - 1, parts)), dma((2, n - 1, parts)), dma((n,)), dma,
        dma((2, n - 1, splits)), dma((2, n - 1, splits)),
        dma((s - 1,)), dma((s - 1,)),
        dma((2,)), dma((2,)), dma((chips - 1, 2)), dma((chips - 1, 2)), dma((2,)), dma((2,)),
        dma((s - 1,)), dma((s - 1,)),
        dma((2, n - 1)), dma((2, n - 1)), dma((cuts,)), dma((cuts,)),
        dma((chips - 1, cuts)), dma((chips - 1, cuts)), dma((chips, cuts)), dma((chips, cuts)),
        dma((halves, 2)), dma((halves, 2)), dma, dma,
    ]
    outs = pl.pallas_call(
        functools.partial(layer_kernel, n, s, scale),
        out_shape=results,
        in_specs=[hbm] * 5 + [vmem] * 3 + [hbm] * 3,
        out_specs=(hbm,) * 4,
        scratch_shapes=scratch,
        compiler_params=pltpu.CompilerParams(
            collective_id=0, has_side_effects=True, vmem_limit_bytes=58 * 2**20
        ),
        name="layer",
    )(og, x, b, c, raw, bias[None], alog[None], skip[None], states, w_out, w_in)
    return handed_on(outs)


def solution(mesh):
    return jax.shard_map(
        layer,
        mesh=mesh,
        in_specs=(
            P("seq", "head"),
            P("seq", "head"),
            P("seq", None),
            P("seq", None),
            P("head", "seq"),
            P("head"),
            P("head"),
            P("head"),
            P("seq", "head", None),
            P("head", None),
            P(None, "head"),
        ),
        out_specs=(P("head", "seq"), P("head", "seq"), P("head", "seq"), P(None, "head")),
        check_vma=False,
    )
```

```python
import functools

import jax
import jax.numpy as jnp
from jax import lax
from jax.experimental import pallas as pl
from jax.experimental.pallas import tpu as pltpu
from jax.sharding import PartitionSpec as P

LAST = (((1,), (1,)), ((), ()))
FIRST = (((0,), (0,)), ((), ()))
PLAIN = (((1,), (0,)), ((), ()))
MESH = pl.DeviceIdType.MESH
EXACT = lax.Precision.HIGHEST
F32, BF16 = jnp.float32, jnp.bfloat16
SKEW = 3
LANES = 128


def dot(a, b, dims=PLAIN, precision=None):
    return lax.dot_general(a, b, dims, precision=precision, preferred_element_type=F32)


def pieces_of(extent, unit, most):
    count = most
    while extent % (count * unit):
        count //= 2
    return count


def remote(src, dst, send, recv, axis, target):
    return pltpu.make_async_remote_copy(
        src_ref=src, dst_ref=dst, send_sem=send, recv_sem=recv,
        device_id={axis: target}, device_id_type=MESH,
    )


def layer_kernel(
    n, s, scale,
    og_hbm, x_hbm, b_hbm, c_hbm, raw_hbm, bias_ref, alog_ref, skip_ref, states_hbm, w_out, w_in,
    o_hbm, obc_hbm, odt_hbm, opar_hbm,
    wo, wi, held, acc, dy, dyd, xt, mask, km, intra, ysta, back, xend, xg,
    going, coming, own_bc, lf, lb, lin, sb, sin, tf, tb, tin, carried,
    et_own, et_in, reach, rows_step, rows_cum, rows_r, rows_xi, rows_st, rows_dx, rows_xs, rows_tail,
    cols, shared, par, par_in, acc_bc, gbc, cbc, wh, xe, hbc, o_ref, obc_ref, odt_ref, opar_ref, og, x_ref, b_ref, c_ref, raw_ref, states,
    in_sem, out_sem, g_send, g_recv, wo_sem, wi_sem, s_send, s_recv, et_send, et_recv,
    l_send, l_recv, st_send, st_recv, t_send, t_recv, p_send, p_recv,
    b_send, b_recv, w1_send, w1_recv, w2_send, w2_recv, w3_send, w3_recv, x_send, x_recv, h_send, h_recv,
):
    me = lax.axis_index("head")
    mine = lax.axis_index("seq")
    tokens, depth = og.shape
    heads = raw_ref.shape[0]
    inner = x_ref.shape[1]
    hdim = inner // heads
    state = b_ref.shape[1]
    per = LANES // hdim
    chips = s // 2
    chip = mine // 2
    odd = lax.rem(mine, 2) == 1
    even = jnp.logical_not(odd)
    right, left = lax.rem(me + 1, n), lax.rem(me + n - 1, n)
    has_right, has_left = me < n - 1, me > 0
    tile = min(256, inner)

    def w_copy(offset):
        where = pl.ds(pl.multiple_of(lax.rem(me + offset, n) * depth, depth), depth)
        return pltpu.make_async_copy(w_out.at[:, where], wo.at[:, where], wo_sem.at[offset])

    wi_copy = pltpu.make_async_copy(w_in, wi, wi_sem)
    w_order = [0]
    for d in range(n - 1):
        for offset in (n - 1 - d, d + 1):
            if offset not in w_order:
                w_order.append(offset)
    barrier = pltpu.get_barrier_semaphore()
    for neighbour in (left, right):
        pl.semaphore_signal(barrier, inc=1, device_id={"head": neighbour}, device_id_type=MESH)
    for away in range(1, s):
        pl.semaphore_signal(
            barrier, inc=1, device_id={"seq": lax.rem(mine + away, s)}, device_id_type=MESH
        )
    loads = [
        pltpu.make_async_copy(src, dst, in_sem.at[k])
        for k, (src, dst) in enumerate((
            (raw_hbm, raw_ref), (b_hbm, b_ref), (c_hbm, c_ref), (x_hbm, x_ref),
            (states_hbm, states), (og_hbm, og),
        ))
    ]
    for load in loads:
        load.start()

    pl.semaphore_wait(barrier, 2 + s - 1)

    leans = n >= 4
    out_rows, bc_rows = o_ref.shape[0], obc_ref.shape[0]
    is_end = leans & ((me == 0) | (me == n - 1))
    is_helper = leans & ((me == 1) | (me == n - 2))
    helper = jnp.where(me == 0, 1, n - 2)
    sibling = mine + 1 - 2 * lax.rem(mine, 2)

    def end_of(side):
        return leans & (me == (0 if side == 0 else n - 1))

    def helper_of(side):
        return leans & (me == (1 if side == 0 else n - 2))

    share = wh.shape[0] // s
    cuts = w1_send.shape[0]
    cut = share // cuts

    def lent(place, q):
        return pl.ds(pl.multiple_of(lax.rem(place + s, s) * share + q * cut, cut), cut)

    def w1_copy(q):
        start = jnp.where(me == 0, 2 * out_rows, 0) + mine * share + q * cut
        return remote(
            w_in.at[pl.ds(pl.multiple_of(start, 16), cut)], wh.at[lent(mine, q)],
            w1_send.at[q], w1_recv.at[q], "head", helper,
        )

    def w2_copy(a, q, place):
        return remote(
            wh.at[lent(place, q)], wh.at[lent(place, q)],
            w2_send.at[a - 1, q], w2_recv.at[a - 1, q], "seq", lax.rem(mine + 2 * a, s),
        )

    def w3_copy(a, q, place):
        return remote(
            wh.at[lent(place, q)], wh.at[lent(place, q)],
            w3_send.at[a, q], w3_recv.at[a, q], "seq", sibling,
        )

    parts = pieces_of(depth, LANES, 4)
    width = depth // parts

    def g_copy(side, d, q):
        where = pl.ds(q * width, width)
        src = og_hbm.at[:, where] if d == 0 else held.at[side, d - 1, :, where]
        return remote(
            src, held.at[side, d, :, where], g_send.at[side, d, q], g_recv.at[side, d, q],
            "head", right if side == 0 else left,
        )

    def g_sends(side, d):
        return (has_right & (me >= d)) if side == 0 else (has_left & (me + d <= n - 1))

    def g_gets(side, d):
        return (me > d) if side == 0 else (me + 1 + d <= n - 1)

    for side in (0, 1):
        @pl.when(g_sends(side, 0))
        def _():
            for q in range(parts):
                g_copy(side, 0, q).start()

    for offset in w_order:
        w_copy(offset).start()
    wi_copy.start()
    for load in loads:
        load.wait()

    def column_of(row):
        at = lax.broadcasted_iota(jnp.int32, (heads, heads), 0)
        along = lax.broadcasted_iota(jnp.int32, (heads, heads), 1)
        return jnp.sum(jnp.where(at == along, row, 0.0), axis=1, keepdims=True)

    bias = column_of(bias_ref[...])
    rate = jnp.exp(column_of(alog_ref[...]))
    skip = column_of(skip_ref[...])
    first = lax.broadcasted_iota(jnp.int32, (tokens, tokens), 0)
    second = lax.broadcasted_iota(jnp.int32, (tokens, tokens), 1)
    upto = (first <= second).astype(F32)
    raw = raw_ref[...] + bias
    step = jnp.maximum(raw, 0.0) + jnp.log1p(jnp.exp(-jnp.abs(raw)))
    log_step = -rate * step
    cum = dot(log_step, upto, precision=EXACT)
    total = cum[:, tokens - 1 : tokens]
    end_decay = jnp.exp(total - cum)
    start_decay = jnp.exp(cum)
    end_total = jnp.exp(total)
    end_weight = step * end_decay
    rows_step[...] = step
    rows_cum[...] = cum
    et_own[...] = jnp.broadcast_to(end_total, et_own.shape)

    def et_copy(away):
        return remote(
            et_own, et_in.at[away - 1], et_send.at[away - 1], et_recv.at[away - 1],
            "seq", lax.rem(mine + s - away, s),
        )

    for away in range(1, s):
        et_copy(away).start()

    eye = (first == second).astype(F32)
    cols[0] = dot(eye, cum, LAST, precision=EXACT)
    cols[1] = dot(eye, step, LAST, precision=EXACT)
    shared[0] = dot(b_ref[...], c_ref[...], LAST)
    shared[1] = jnp.zeros((tokens, tokens), F32)
    lane = lax.broadcasted_iota(jnp.int32, (tokens, heads), 1)

    def masks(h, carry):
        col = jnp.sum(jnp.where(lane == h, cols[0], 0.0), axis=1, keepdims=True)
        col_step = jnp.sum(jnp.where(lane == h, cols[1], 0.0), axis=1, keepdims=True)
        gap = rows_cum[pl.ds(h, 1), :] - col
        value = jnp.where(first <= second, jnp.exp(jnp.minimum(gap, 0.0)) * col_step, 0.0)
        mask[h] = value
        km[h] = (shared[0] * value).astype(BF16)
        return carry

    lax.fori_loop(0, heads, masks, 0)
    eye_bf = eye[:tile, :tile].astype(BF16)
    for k in range(inner // tile):
        where = pl.ds(k * tile, tile)
        xt[where, :] = dot(eye_bf, x_ref[:, where], LAST).astype(BF16)
        ysta[where, :] = dot(states[0, where, :], c_ref[...], LAST)
    ct = dot(eye_bf[:state, :state], c_ref[...], LAST).astype(BF16)
    bt = dot(eye_bf[:state, :state], b_ref[...], LAST).astype(BF16)
    sbt = dot(eye_bf[:state, :state], states[0], LAST).astype(BF16)

    def multiply(source, offset, start, extent, fresh):
        if start == 0:
            w_copy(offset).wait()
        base = lax.rem(me + offset, n) * depth + start
        where = pl.ds(pl.multiple_of(base, extent), extent)

        def body(k, carry):
            outs = pl.ds(pl.multiple_of(k * tile, tile), tile)
            part = dot(wo[outs, where], source[:, pl.ds(start, extent)], LAST)
            acc[outs, :] = part if fresh else acc[outs, :] + part
            return carry

        lax.fori_loop(0, inner // tile, body, 0)

    multiply(og, 0, 0, depth, True)
    for side in (0, 1):
        @pl.when(end_of(side))
        def _():
            for q in range(parts):
                g_copy(side, 0, q).wait_send()
            for q in range(cuts):
                w1_copy(q).start()

    for d in range(n - 1):
        for q in range(parts):
            for side in (0, 1):
                @pl.when(g_gets(side, d))
                def _():
                    g_copy(side, d, q).wait_recv()
                if d + 1 < n - 1:
                    @pl.when(g_gets(side, d) & g_sends(side, d + 1))
                    def _():
                        g_copy(side, d + 1, q).start()
            if d == 1 and q < cuts:
                @pl.when(is_helper)
                def _():
                    w1_copy(q).wait_recv()
                    for a in range(1, chips):
                        w2_copy(a, q, mine).start()
                    w3_copy(0, q, mine).start()
            for side in (0, 1):
                @pl.when(g_gets(side, d))
                def _():
                    offset = n - 1 - d if side == 0 else d + 1
                    multiply(held.at[side, d], offset, q * width, width, False)

    shares = 4 if heads % 4 == 0 else 1
    group = heads // shares

    def share_rows(k):
        return pl.ds(k * group * hdim, group * hdim)

    def l_copy(k):
        return remote(
            lb.at[share_rows(k)], lin.at[share_rows(k)], l_send.at[k], l_recv.at[k],
            "seq", sibling,
        )

    def t_copy(k):
        return remote(
            tb.at[share_rows(k)], tin.at[share_rows(k)], t_send.at[k], t_recv.at[k],
            "seq", sibling,
        )

    for k in range(shares):
        for h in range(k * group, (k + 1) * group):
            rows = pl.ds(h * hdim, hdim)
            rounded = acc[rows, :].astype(BF16)
            dy[rows, :] = rounded
            dyd[rows, :] = (rounded.astype(F32) * start_decay[h : h + 1, :]).astype(BF16)
        where = share_rows(k)
        value = dot(dyd[where, :], c_ref[...])
        lf[where, :] = value
        lb[where, :] = value.astype(BF16)

        @pl.when(odd)
        def _():
            l_copy(k).start()

    for away in range(1, s):
        et_copy(away).wait_recv()
    weight = jnp.ones((heads, LANES), F32)
    for a in range(1, chips):
        reach[a - 1] = weight
        weight = weight * et_in[2 * a - 1] * et_in[2 * a]

    half_lane = lax.broadcasted_iota(jnp.int32, (tokens, LANES), 1) // hdim

    def intra_heads(pair, carry):
        block = pl.ds(pl.multiple_of(pair * LANES, LANES), LANES)
        x_pair = x_ref[:, block]
        dy_pair = dy[block, :]
        for sub in range(per):
            h = pair * per + sub
            rows = pl.ds(pl.multiple_of(h * hdim, hdim), hdim)
            dots = dot(jnp.where(half_lane == sub, x_pair, jnp.zeros_like(x_pair)), dy_pair)
            shared[1] += dots * mask[h]
            rows_r[pl.ds(h, 1), :] = jnp.sum(dots * km[h].astype(F32), axis=0, keepdims=True)
            dy_h = dy[rows, :]
            x_h = xt[rows, :].astype(F32)
            inside = dot(dy_h, km[h], LAST)
            intra[rows, :] = inside
            wide = dy_h.astype(F32)
            rows_xi[pl.ds(h, 1), :] = jnp.sum(x_h * inside, axis=0, keepdims=True)
            rows_st[pl.ds(h, 1), :] = jnp.sum(wide * ysta[rows, :], axis=0, keepdims=True)
            rows_dx[pl.ds(h, 1), :] = jnp.sum(wide * x_h, axis=0, keepdims=True)
        return carry

    pairs = heads // per
    early = pairs // 8
    lax.fori_loop(0, early, intra_heads, 0)

    def st_copy(a, k):
        return remote(
            sb.at[share_rows(k)], sin.at[a - 1, share_rows(k)],
            st_send.at[a - 1, k], st_recv.at[a - 1, k], "seq", jnp.maximum(mine - 2 * a, 0),
        )

    def over_heads(k, do):
        def body(h, carry):
            do(h, pl.ds(pl.multiple_of(h * hdim, hdim), hdim))
            return carry

        lax.fori_loop(k * group, (k + 1) * group, body, 0)

    for k in range(shares):
        @pl.when(even)
        def _():
            l_copy(k).wait_recv()

            def join(h, rows):
                sb[rows, :] = (
                    lf[rows, :] + et_own[pl.ds(h, 1), :] * lin[rows, :].astype(F32)
                ).astype(BF16)
                tf[rows, :] = jnp.zeros((hdim, state), F32)

            over_heads(k, join)

        for a in range(chips - 1, 0, -1):
            @pl.when(even & (chip >= a))
            def _():
                st_copy(a, k).start()

        middle = pairs if k == shares - 1 else (early + pairs) // 2
        lax.fori_loop(early, middle, intra_heads, 0)
        early = middle

    halves = xg.shape[0]
    span = tokens // halves

    def x_copy(half, k):
        return remote(
            xg.at[half, share_rows(k)], xe.at[half, share_rows(k)],
            x_send.at[half, k], x_recv.at[half, k], "head", helper,
        )

    def x_grads(half, k):
        where = pl.ds(half * span, span)
        for h in range(k * group, (k + 1) * group):
            rows = pl.ds(h * hdim, hdim)
            xg[half, rows, :] = (
                intra[rows, where]
                + end_weight[h : h + 1, half * span : (half + 1) * span] * back[rows, where]
                + skip[h : h + 1, :] * dy[rows, where].astype(F32)
            ).astype(BF16)

    for k in range(shares):
        for a in range(1, chips):
            @pl.when(even & (chip + a < chips))
            def _():
                st_copy(a, k).wait_recv()

                def add(h, rows):
                    tf[rows, :] += (
                        reach[a - 1, pl.ds(h, 1), :] * sin[a - 1, rows, :].astype(F32)
                    )

                over_heads(k, add)

        @pl.when(even)
        def _():
            tb[share_rows(k), :] = tf[share_rows(k), :].astype(BF16)
            t_copy(k).start()

            def enter(h, rows):
                carried[rows, :] = (
                    lin[rows, :].astype(F32) + et_in[0, pl.ds(h, 1), :] * tf[rows, :]
                )

            over_heads(k, enter)

        @pl.when(odd)
        def _():
            t_copy(k).wait_recv()
            carried[share_rows(k), :] = tin[share_rows(k), :].astype(F32)

        back[share_rows(k), :] = dot(carried[share_rows(k), :].astype(BF16), b_ref[...], LAST)
        x_grads(0, k)

        @pl.when(is_end)
        def _():
            x_copy(0, k).start()

    for half in range(1, halves):
        for k in range(shares):
            x_grads(half, k)

    wi_copy.wait()

    @pl.when(is_helper)
    def _():
        for q in range(cuts):
            for a in range(1, chips):
                w2_copy(a, q, mine - 2 * a).wait_recv()
                w3_copy(a, q, mine - 2 * a).start()
        for q in range(cuts):
            for a in range(chips):
                w3_copy(a, q, sibling - 2 * a).wait_recv()

    strips = s_send.shape[2] // halves
    splits = strips * halves
    piece = out_rows // strips

    def s_copy(side, e, k, strip):
        rows = pl.ds(pl.multiple_of(strip * piece, piece), piece)
        q = k * strips + strip
        return remote(
            going.at[side, e, k, rows], coming.at[side, e, k, rows],
            s_send.at[side, e, q], s_recv.at[side, e, q], "head", right if side == 0 else left,
        )

    def b_copy(side, e):
        return remote(
            gbc.at[side, e], cbc.at[side, e], b_send.at[side, e], b_recv.at[side, e],
            "head", right if side == 0 else left,
        )

    leant = (n - 2) * bc_rows

    def h_copy():
        start = pl.multiple_of(jnp.where(me == 0, 2 * bc_rows, 0), bc_rows)
        return remote(own_bc.at[pl.ds(start, leant)], hbc, h_send, h_recv, "head", helper)

    def owner_of(side, e):
        return n - 1 - e if side == 0 else e

    def s_sends(side, e):
        return (me < owner_of(side, e)) if side == 0 else (me > owner_of(side, e))

    def s_gets(side, e):
        return (s_sends(side, e) | (me == owner_of(side, e))) & (has_left if side == 0 else has_right)

    def term(owner, k, strip):
        start = pl.multiple_of(owner * out_rows + strip * piece, piece)
        return dot(wi[pl.ds(start, piece), :], xg[k])

    count = (n - 1) * splits

    def bc_of(owner):
        return own_bc[pl.ds(pl.multiple_of(owner * bc_rows, bc_rows), bc_rows), :]

    def slot(index, carry):
        for side in (0, 1):
            place = index - SKEW * (me if side == 0 else n - 1 - me)
            held_at = jnp.clip(place, 0, count - 1)
            e, q = lax.div(held_at, splits), lax.rem(held_at, splits)
            k, strip = lax.div(q, strips), lax.rem(q, strips)
            owner = owner_of(side, e)
            live = (place >= 0) & (place < count)
            rows = pl.ds(pl.multiple_of(strip * piece, piece), piece)
            sends = live & s_sends(side, e)
            aided = helper_of(side) & (e < n - 2)
            far = owner - 2 if side == 0 else owner
            passes = jnp.logical_not(end_of(side) & (e < n - 2))
            gets = s_gets(side, e) & jnp.logical_not(aided)
            closes = q == splits - 1

            for one in range(halves):
                @pl.when(helper_of(side) & (place == one * strips))
                def _():
                    for part in range(shares):
                        x_copy(one, part).wait_recv()

            @pl.when(helper_of(side) & (place == splits - 1))
            def _():
                h_copy().wait_recv()

            @pl.when(sends & passes)
            def _():
                going[side, e, k, rows, :] = term(owner, k, strip).astype(BF16)

                @pl.when(aided)
                def _():
                    start = pl.multiple_of(far * out_rows + strip * piece, piece)
                    aid = dot(wh[pl.ds(start, piece), :], xe[k])
                    going[side, e, k, rows, :] = (
                        going[side, e, k, rows, :].astype(F32) + aid
                    ).astype(BF16)

                @pl.when(gets)
                def _():
                    s_copy(side, e, k, strip).wait_recv()
                    going[side, e, k, rows, :] = (
                        going[side, e, k, rows, :].astype(F32)
                        + coming[side, e, k, rows, :].astype(F32)
                    ).astype(BF16)

                s_copy(side, e, k, strip).start()

            @pl.when(sends & passes & closes)
            def _():
                gbc[side, e] = bc_of(owner)

                @pl.when(aided)
                def _():
                    start = pl.multiple_of(far * bc_rows, bc_rows)
                    gbc[side, e] = (
                        gbc[side, e].astype(F32) + hbc[pl.ds(start, bc_rows), :].astype(F32)
                    ).astype(BF16)

                @pl.when(gets)
                def _():
                    b_copy(side, e).wait_recv()
                    gbc[side, e] = (
                        gbc[side, e].astype(F32) + cbc[side, e].astype(F32)
                    ).astype(BF16)

                b_copy(side, e).start()

            @pl.when(live & (me == owner) & gets)
            def _():
                s_copy(side, e, k, strip).wait_recv()
                where = pl.ds(pl.multiple_of(k * span, span), span)
                acc[rows, where] += coming[side, e, k, rows, :].astype(F32)

                @pl.when(closes)
                def _():
                    b_copy(side, e).wait_recv()
                    acc_bc[...] += cbc[side, e].astype(F32)

        return carry

    lax.fori_loop(0, SKEW, slot, 0)

    for h in range(heads):
        rows = pl.ds(h * hdim, hdim)
        x_h = xt[rows, :].astype(F32)
        xend[rows, :] = (x_h * end_weight[h : h + 1, :]).astype(BF16)
        rows_xs[h : h + 1, :] = jnp.sum(x_h * back[rows, :], axis=0, keepdims=True)
        rows_tail[h : h + 1, :] = jnp.sum(
            states[0, rows, :].astype(F32) * carried[rows, :], axis=0, keepdims=True
        )
    sums = shared[1].astype(BF16)
    carried_t = dot(eye_bf[:state, :state], carried[...].astype(BF16), LAST).astype(BF16)
    own_bc[:state, :] = (dot(ct, sums, LAST) + dot(carried_t, xend[...])).astype(BF16)
    own_bc[state:, :] = (dot(bt, sums) + dot(sbt, dyd[...])).astype(BF16)

    @pl.when(is_end)
    def _():
        for part in range(shares):
            x_copy(0, part).wait_send()
            for half in range(1, halves):
                x_copy(half, part).start()
        h_copy().start()

    acc_bc[...] = bc_of(me).astype(F32)
    for k in range(halves):
        for strip in range(strips):
            acc[pl.ds(strip * piece, piece), pl.ds(k * span, span)] = term(me, k, strip)
    slots = max((n - k) * splits + SKEW * k for k in range(1, n))
    first_part = min(slots, SKEW + 3)
    lax.fori_loop(SKEW, first_part, slot, 0)

    end_terms = end_weight * rows_xs[...]
    cum_grad = rows_r[...] - rows_xi[...] + start_decay * rows_st[...] - end_terms
    tail = jnp.sum(end_terms, axis=1, keepdims=True) + end_total * jnp.sum(
        rows_tail[...], axis=1, keepdims=True
    )
    token = lax.broadcasted_iota(jnp.int32, (heads, tokens), 1)
    cum_grad = cum_grad + jnp.where(token == tokens - 1, tail, 0.0)
    step_grad = dot(cum_grad, upto, LAST, precision=EXACT)
    dt_sum = -rate * step_grad + (rows_xi[...] + end_terms) / step
    dt_grad = dt_sum / (1.0 + jnp.exp(-raw))
    odt_ref[...] = dt_grad
    writes = [
        pltpu.make_async_copy(src, dst, out_sem.at[k])
        for k, (src, dst) in enumerate((
            (o_ref, o_hbm), (obc_ref, obc_hbm), (odt_ref, odt_hbm), (opar_ref, opar_hbm),
        ))
    ]
    writes[2].start()

    def row_of(column):
        at = lax.broadcasted_iota(jnp.int32, (heads, LANES), 0)
        along = lax.broadcasted_iota(jnp.int32, (heads, LANES), 1)
        return jnp.sum(jnp.where(at == along, column, 0.0), axis=0, keepdims=True)

    line = lax.broadcasted_iota(jnp.int32, (8, LANES), 0)
    packet = jnp.zeros((8, LANES), F32)
    for index, terms in enumerate((step_grad * log_step, rows_dx[...], dt_grad)):
        packet = jnp.where(line == index, row_of(jnp.sum(terms, axis=1, keepdims=True)), packet)
    par[...] = packet

    def p_copy(away):
        return remote(
            par, par_in.at[away - 1], p_send.at[away - 1], p_recv.at[away - 1],
            "seq", lax.rem(mine + s - away, s),
        )

    for away in range(1, s):
        p_copy(away).start()

    @pl.when(is_end)
    def _():
        for half in range(1, halves):
            for part in range(shares):
                x_copy(half, part).wait_send()

    lax.fori_loop(first_part, slots, slot, 0)

    o_ref[...] = acc[:out_rows, :].astype(BF16)
    writes[0].start()
    obc_ref[...] = acc_bc[...].astype(BF16)
    writes[1].start()
    value = packet
    for away in range(1, s):
        p_copy(away).wait_recv()
        value = value + par_in[away - 1]
    opar_ref[...] = value[: opar_ref.shape[0], :heads] * scale
    writes[3].start()

    for side in (0, 1):
        for d in range(n - 1):
            @pl.when(g_sends(side, d) & (jnp.logical_not(end_of(side)) if d == 0 else True))
            def _():
                for q in range(parts):
                    g_copy(side, d, q).wait_send()

            skipped = end_of(side) if d < n - 2 else False

            @pl.when(s_sends(side, d) & jnp.logical_not(skipped))
            def _():
                for k in range(halves):
                    for strip in range(strips):
                        s_copy(side, d, k, strip).wait_send()
                b_copy(side, d).wait_send()

    @pl.when(is_end)
    def _():
        for q in range(cuts):
            w1_copy(q).wait_send()
        h_copy().wait_send()

    @pl.when(is_helper)
    def _():
        for q in range(cuts):
            for a in range(chips):
                if a > 0:
                    w2_copy(a, q, mine).wait_send()
                w3_copy(a, q, mine - 2 * a).wait_send()

    for away in range(1, s):
        et_copy(away).wait_send()
        p_copy(away).wait_send()

    for k in range(shares):
        @pl.when(odd)
        def _():
            l_copy(k).wait_send()

        for a in range(1, chips):
            @pl.when(even & (chip >= a))
            def _():
                st_copy(a, k).wait_send()

        @pl.when(even)
        def _():
            t_copy(k).wait_send()
    for write in writes:
        write.wait()


def hand_on_kernel(*refs):
    count = len(refs) // 2
    for k in range(count):
        refs[count + k][...] = refs[k][...]


def handed_on(arrays):
    vmem = pl.BlockSpec(memory_space=pltpu.VMEM)
    return pl.pallas_call(
        hand_on_kernel,
        out_shape=tuple(jax.ShapeDtypeStruct(a.shape, a.dtype) for a in arrays),
        in_specs=[vmem] * len(arrays),
        out_specs=(vmem,) * len(arrays),
        name="hand_on",
    )(*arrays)


def layer(og, x, b, c, raw, bias, alog, skip, states, w_out, w_in):
    n, s = lax.axis_size("head"), lax.axis_size("seq")
    tokens, depth = og.shape
    inner = x.shape[1]
    heads = raw.shape[0]
    hdim = inner // heads
    state = b.shape[1]
    out_rows = w_in.shape[0] // n
    bc_rows = 2 * state // n
    chips = s // 2
    scale = (s * tokens * hdim) ** (-0.5)
    vmem = pl.BlockSpec(memory_space=pltpu.VMEM)
    hbm = pl.BlockSpec(memory_space=pltpu.HBM)
    dma = pltpu.SemaphoreType.DMA
    parts = pieces_of(depth, LANES, 4)
    halves = 2 if tokens % (2 * LANES) == 0 else 1
    splits = pieces_of(out_rows, 16, 2) * halves
    lent = max(n - 2, 1) * out_rows
    cuts = pieces_of(lent // s, 16, parts)
    leant = max(n - 2, 1) * bc_rows

    def wide(dtype):
        return pltpu.VMEM((inner, tokens), dtype)

    def slim(dtype, *lead):
        return pltpu.VMEM((*lead, inner, state), dtype)

    results = (
        jax.ShapeDtypeStruct((out_rows, tokens), BF16),
        jax.ShapeDtypeStruct((bc_rows, tokens), BF16),
        jax.ShapeDtypeStruct((heads, tokens), F32),
        jax.ShapeDtypeStruct((3, heads), F32),
    )
    rows = pltpu.VMEM((heads, tokens), F32)
    packet = pltpu.VMEM((2, n - 1, halves, out_rows, tokens // halves), BF16)
    bc_packet = pltpu.VMEM((2, n - 1, bc_rows, tokens), BF16)
    shared_x = pltpu.VMEM((halves, inner, tokens // halves), BF16)
    scratch = [
        pltpu.VMEM(w_out.shape, BF16),
        pltpu.VMEM(w_in.shape, BF16),
        pltpu.VMEM((2, n - 1, tokens, depth), BF16),
        wide(F32), wide(BF16), wide(BF16), wide(BF16),
        pltpu.VMEM((heads, tokens, tokens), F32),
        pltpu.VMEM((heads, tokens, tokens), BF16),
        wide(F32), wide(F32), wide(F32), wide(BF16), shared_x,
        packet, packet,
        pltpu.VMEM((2 * state, tokens), BF16),
        slim(F32), slim(BF16), slim(BF16), slim(BF16), slim(BF16, chips - 1),
        slim(F32), slim(BF16), slim(BF16), slim(F32),
        pltpu.VMEM((heads, LANES), F32),
        pltpu.VMEM((s - 1, heads, LANES), F32),
        pltpu.VMEM((chips - 1, heads, LANES), F32),
        rows, rows, rows, rows, rows, rows, rows, pltpu.VMEM((heads, state), F32),
        pltpu.VMEM((2, tokens, heads), F32),
        pltpu.VMEM((2, tokens, tokens), F32),
        pltpu.VMEM((8, LANES), F32),
        pltpu.VMEM((s - 1, 8, LANES), F32),
        pltpu.VMEM((bc_rows, tokens), F32), bc_packet, bc_packet,
        pltpu.VMEM((lent, inner), BF16), shared_x, pltpu.VMEM((leant, tokens), BF16),
        *[pltpu.VMEM(a.shape, a.dtype) for a in results],
        *[pltpu.VMEM(a.shape, a.dtype) for a in (og, x, b, c, raw, states)],
        dma((6,)), dma((4,)), dma((2, n - 1, parts)), dma((2, n - 1, parts)), dma((n,)), dma,
        dma((2, n - 1, splits)), dma((2, n - 1, splits)),
        dma((s - 1,)), dma((s - 1,)),
        dma((4,)), dma((4,)), dma((chips - 1, 4)), dma((chips - 1, 4)), dma((4,)), dma((4,)),
        dma((s - 1,)), dma((s - 1,)),
        dma((2, n - 1)), dma((2, n - 1)), dma((cuts,)), dma((cuts,)),
        dma((chips - 1, cuts)), dma((chips - 1, cuts)), dma((chips, cuts)), dma((chips, cuts)),
        dma((halves, 4)), dma((halves, 4)), dma, dma,
    ]
    outs = pl.pallas_call(
        functools.partial(layer_kernel, n, s, scale),
        out_shape=results,
        in_specs=[hbm] * 5 + [vmem] * 3 + [hbm] * 3,
        out_specs=(hbm,) * 4,
        scratch_shapes=scratch,
        compiler_params=pltpu.CompilerParams(
            collective_id=0, has_side_effects=True, vmem_limit_bytes=58 * 2**20
        ),
        name="layer",
    )(og, x, b, c, raw, bias[None], alog[None], skip[None], states, w_out, w_in)
    return handed_on(outs)


def solution(mesh):
    return jax.shard_map(
        layer,
        mesh=mesh,
        in_specs=(
            P("seq", "head"),
            P("seq", "head"),
            P("seq", None),
            P("seq", None),
            P("head", "seq"),
            P("head"),
            P("head"),
            P("head"),
            P("seq", "head", None),
            P("head", None),
            P(None, "head"),
        ),
        out_specs=(P("head", "seq"), P("head", "seq"), P("head", "seq"), P(None, "head")),
        check_vma=False,
    )
```

```python
import functools

import jax
import jax.numpy as jnp
from jax import lax
from jax.experimental import pallas as pl
from jax.experimental.pallas import tpu as pltpu
from jax.sharding import PartitionSpec as P

LAST = (((1,), (1,)), ((), ()))
FIRST = (((0,), (0,)), ((), ()))
PLAIN = (((1,), (0,)), ((), ()))
MESH = pl.DeviceIdType.MESH
EXACT = lax.Precision.HIGHEST
F32, BF16 = jnp.float32, jnp.bfloat16
SKEW = 3
LANES = 128


def dot(a, b, dims=PLAIN, precision=None):
    return lax.dot_general(a, b, dims, precision=precision, preferred_element_type=F32)


def pieces_of(extent, unit, most):
    count = most
    while extent % (count * unit):
        count //= 2
    return count


def remote(src, dst, send, recv, axis, target):
    return pltpu.make_async_remote_copy(
        src_ref=src, dst_ref=dst, send_sem=send, recv_sem=recv,
        device_id={axis: target}, device_id_type=MESH,
    )


def layer_kernel(
    n, s, scale,
    og_hbm, x_hbm, b_hbm, c_hbm, raw_hbm, bias_ref, alog_ref, skip_ref, states_hbm, w_out, w_in,
    o_hbm, obc_hbm, odt_hbm, opar_hbm,
    wo, wi, held, acc, dy, dyd, xt, mask, km, intra, ysta, back, xend, xg,
    going, coming, own_bc, lf, lb, lin, sb, sin, tf, tb, tin, carried,
    et_own, et_in, reach, rows_step, rows_cum, rows_r, rows_xi, rows_st, rows_dx, rows_xs, rows_tail,
    cols, shared, par, par_in, acc_bc, gbc, cbc, wh, xe, hbc, o_ref, obc_ref, odt_ref, opar_ref, og, x_ref, b_ref, c_ref, raw_ref, states,
    in_sem, out_sem, g_send, g_recv, wo_sem, wi_sem, s_send, s_recv, et_send, et_recv,
    l_send, l_recv, st_send, st_recv, t_send, t_recv, p_send, p_recv,
    b_send, b_recv, w1_send, w1_recv, w2_send, w2_recv, w3_send, w3_recv, x_send, x_recv, h_send, h_recv,
):
    me = lax.axis_index("head")
    mine = lax.axis_index("seq")
    tokens, depth = og.shape
    heads = raw_ref.shape[0]
    inner = x_ref.shape[1]
    hdim = inner // heads
    state = b_ref.shape[1]
    per = LANES // hdim
    chips = s // 2
    chip = mine // 2
    odd = lax.rem(mine, 2) == 1
    even = jnp.logical_not(odd)
    right, left = lax.rem(me + 1, n), lax.rem(me + n - 1, n)
    has_right, has_left = me < n - 1, me > 0
    tile = min(256, inner)

    def w_copy(offset):
        where = pl.ds(pl.multiple_of(lax.rem(me + offset, n) * depth, depth), depth)
        return pltpu.make_async_copy(w_out.at[:, where], wo.at[:, where], wo_sem.at[offset])

    wi_copy = pltpu.make_async_copy(w_in, wi, wi_sem)
    w_order = [0]
    for d in range(n - 1):
        for offset in (n - 1 - d, d + 1):
            if offset not in w_order:
                w_order.append(offset)
    barrier = pltpu.get_barrier_semaphore()
    for neighbour in (left, right):
        pl.semaphore_signal(barrier, inc=1, device_id={"head": neighbour}, device_id_type=MESH)
    for away in range(1, s):
        pl.semaphore_signal(
            barrier, inc=1, device_id={"seq": lax.rem(mine + away, s)}, device_id_type=MESH
        )
    loads = [
        pltpu.make_async_copy(src, dst, in_sem.at[k])
        for k, (src, dst) in enumerate((
            (raw_hbm, raw_ref), (b_hbm, b_ref), (c_hbm, c_ref), (x_hbm, x_ref),
            (states_hbm, states), (og_hbm, og),
        ))
    ]
    for load in loads:
        load.start()

    pl.semaphore_wait(barrier, 2 + s - 1)

    leans = n >= 4
    out_rows, bc_rows = o_ref.shape[0], obc_ref.shape[0]
    is_end = leans & ((me == 0) | (me == n - 1))
    is_helper = leans & ((me == 1) | (me == n - 2))
    helper = jnp.where(me == 0, 1, n - 2)
    sibling = mine + 1 - 2 * lax.rem(mine, 2)

    def end_of(side):
        return leans & (me == (0 if side == 0 else n - 1))

    def helper_of(side):
        return leans & (me == (1 if side == 0 else n - 2))

    share = wh.shape[0] // s
    cuts = w1_send.shape[0]
    cut = share // cuts

    def lent(place, q):
        return pl.ds(pl.multiple_of(lax.rem(place + s, s) * share + q * cut, cut), cut)

    def w1_copy(q):
        start = jnp.where(me == 0, 2 * out_rows, 0) + mine * share + q * cut
        return remote(
            w_in.at[pl.ds(pl.multiple_of(start, 16), cut)], wh.at[lent(mine, q)],
            w1_send.at[q], w1_recv.at[q], "head", helper,
        )

    def w2_copy(a, q, place):
        return remote(
            wh.at[lent(place, q)], wh.at[lent(place, q)],
            w2_send.at[a - 1, q], w2_recv.at[a - 1, q], "seq", lax.rem(mine + 2 * a, s),
        )

    def w3_copy(a, q, place):
        return remote(
            wh.at[lent(place, q)], wh.at[lent(place, q)],
            w3_send.at[a, q], w3_recv.at[a, q], "seq", sibling,
        )

    parts = pieces_of(depth, LANES, 4)
    width = depth // parts

    def g_copy(side, d, q):
        where = pl.ds(q * width, width)
        src = og_hbm.at[:, where] if d == 0 else held.at[side, d - 1, :, where]
        return remote(
            src, held.at[side, d, :, where], g_send.at[side, d, q], g_recv.at[side, d, q],
            "head", right if side == 0 else left,
        )

    def g_sends(side, d):
        return (has_right & (me >= d)) if side == 0 else (has_left & (me + d <= n - 1))

    def g_gets(side, d):
        return (me > d) if side == 0 else (me + 1 + d <= n - 1)

    for side in (0, 1):
        @pl.when(g_sends(side, 0))
        def _():
            for q in range(parts):
                g_copy(side, 0, q).start()

    for offset in w_order:
        w_copy(offset).start()
    wi_copy.start()
    for load in loads:
        load.wait()

    def column_of(row):
        at = lax.broadcasted_iota(jnp.int32, (heads, heads), 0)
        along = lax.broadcasted_iota(jnp.int32, (heads, heads), 1)
        return jnp.sum(jnp.where(at == along, row, 0.0), axis=1, keepdims=True)

    bias = column_of(bias_ref[...])
    rate = jnp.exp(column_of(alog_ref[...]))
    skip = column_of(skip_ref[...])
    first = lax.broadcasted_iota(jnp.int32, (tokens, tokens), 0)
    second = lax.broadcasted_iota(jnp.int32, (tokens, tokens), 1)
    upto = (first <= second).astype(F32)
    raw = raw_ref[...] + bias
    step = jnp.maximum(raw, 0.0) + jnp.log1p(jnp.exp(-jnp.abs(raw)))
    log_step = -rate * step
    cum = dot(log_step, upto, precision=EXACT)
    total = cum[:, tokens - 1 : tokens]
    end_decay = jnp.exp(total - cum)
    start_decay = jnp.exp(cum)
    end_total = jnp.exp(total)
    end_weight = step * end_decay
    rows_step[...] = step
    rows_cum[...] = cum
    et_own[...] = jnp.broadcast_to(end_total, et_own.shape)

    def et_copy(away):
        return remote(
            et_own, et_in.at[away - 1], et_send.at[away - 1], et_recv.at[away - 1],
            "seq", lax.rem(mine + s - away, s),
        )

    for away in range(1, s):
        et_copy(away).start()

    eye = (first == second).astype(F32)
    cols[0] = dot(eye, cum, LAST, precision=EXACT)
    cols[1] = dot(eye, step, LAST, precision=EXACT)
    shared[0] = dot(b_ref[...], c_ref[...], LAST)
    shared[1] = jnp.zeros((tokens, tokens), F32)
    lane = lax.broadcasted_iota(jnp.int32, (tokens, heads), 1)

    def masks(h, carry):
        col = jnp.sum(jnp.where(lane == h, cols[0], 0.0), axis=1, keepdims=True)
        col_step = jnp.sum(jnp.where(lane == h, cols[1], 0.0), axis=1, keepdims=True)
        gap = rows_cum[pl.ds(h, 1), :] - col
        value = jnp.where(first <= second, jnp.exp(jnp.minimum(gap, 0.0)) * col_step, 0.0)
        mask[h] = value
        km[h] = (shared[0] * value).astype(BF16)
        return carry

    lax.fori_loop(0, heads, masks, 0)
    eye_bf = eye[:tile, :tile].astype(BF16)
    for k in range(inner // tile):
        where = pl.ds(k * tile, tile)
        xt[where, :] = dot(eye_bf, x_ref[:, where], LAST).astype(BF16)
        ysta[where, :] = dot(states[0, where, :], c_ref[...], LAST)
    ct = dot(eye_bf[:state, :state], c_ref[...], LAST).astype(BF16)
    bt = dot(eye_bf[:state, :state], b_ref[...], LAST).astype(BF16)
    sbt = dot(eye_bf[:state, :state], states[0], LAST).astype(BF16)

    def multiply(source, offset, start, extent, fresh):
        if start == 0:
            w_copy(offset).wait()
        base = lax.rem(me + offset, n) * depth + start
        where = pl.ds(pl.multiple_of(base, extent), extent)

        def body(k, carry):
            outs = pl.ds(pl.multiple_of(k * tile, tile), tile)
            part = dot(wo[outs, where], source[:, pl.ds(start, extent)], LAST)
            acc[outs, :] = part if fresh else acc[outs, :] + part
            return carry

        lax.fori_loop(0, inner // tile, body, 0)

    multiply(og, 0, 0, depth, True)
    for side in (0, 1):
        @pl.when(end_of(side))
        def _():
            for q in range(parts):
                g_copy(side, 0, q).wait_send()
            for q in range(cuts):
                w1_copy(q).start()

    for d in range(n - 1):
        for q in range(parts):
            for side in (0, 1):
                @pl.when(g_gets(side, d))
                def _():
                    g_copy(side, d, q).wait_recv()
                if d + 1 < n - 1:
                    @pl.when(g_gets(side, d) & g_sends(side, d + 1))
                    def _():
                        g_copy(side, d + 1, q).start()
            if d == 1 and q < cuts:
                @pl.when(is_helper)
                def _():
                    w1_copy(q).wait_recv()
                    for a in range(1, chips):
                        w2_copy(a, q, mine).start()
                    w3_copy(0, q, mine).start()
            for side in (0, 1):
                @pl.when(g_gets(side, d))
                def _():
                    offset = n - 1 - d if side == 0 else d + 1
                    multiply(held.at[side, d], offset, q * width, width, False)

    shares = 4 if heads % 4 == 0 else 1
    group = heads // shares

    def share_rows(k):
        return pl.ds(k * group * hdim, group * hdim)

    def l_copy(k):
        return remote(
            lb.at[share_rows(k)], lin.at[share_rows(k)], l_send.at[k], l_recv.at[k],
            "seq", sibling,
        )

    def t_copy(k):
        return remote(
            tb.at[share_rows(k)], tin.at[share_rows(k)], t_send.at[k], t_recv.at[k],
            "seq", sibling,
        )

    for k in range(shares):
        for h in range(k * group, (k + 1) * group):
            rows = pl.ds(h * hdim, hdim)
            rounded = acc[rows, :].astype(BF16)
            dy[rows, :] = rounded
            dyd[rows, :] = (rounded.astype(F32) * start_decay[h : h + 1, :]).astype(BF16)
        where = share_rows(k)
        value = dot(dyd[where, :], c_ref[...])
        lf[where, :] = value
        lb[where, :] = value.astype(BF16)

        @pl.when(odd)
        def _():
            l_copy(k).start()

    def hand_over(low, high):
        @pl.when(is_helper)
        def _():
            for q in range(low, high):
                for a in range(1, chips):
                    w2_copy(a, q, mine - 2 * a).wait_recv()
                    w3_copy(a, q, mine - 2 * a).start()

    for away in range(1, s):
        et_copy(away).wait_recv()
    weight = jnp.ones((heads, LANES), F32)
    for a in range(1, chips):
        reach[a - 1] = weight
        weight = weight * et_in[2 * a - 1] * et_in[2 * a]

    half_lane = lax.broadcasted_iota(jnp.int32, (tokens, LANES), 1) // hdim

    def intra_heads(pair, carry):
        block = pl.ds(pl.multiple_of(pair * LANES, LANES), LANES)
        x_pair = x_ref[:, block]
        dy_pair = dy[block, :]
        for sub in range(per):
            h = pair * per + sub
            rows = pl.ds(pl.multiple_of(h * hdim, hdim), hdim)
            dots = dot(jnp.where(half_lane == sub, x_pair, jnp.zeros_like(x_pair)), dy_pair)
            shared[1] += dots * mask[h]
            rows_r[pl.ds(h, 1), :] = jnp.sum(dots * km[h].astype(F32), axis=0, keepdims=True)
            dy_h = dy[rows, :]
            x_h = xt[rows, :].astype(F32)
            inside = dot(dy_h, km[h], LAST)
            intra[rows, :] = inside
            wide = dy_h.astype(F32)
            rows_xi[pl.ds(h, 1), :] = jnp.sum(x_h * inside, axis=0, keepdims=True)
            rows_st[pl.ds(h, 1), :] = jnp.sum(wide * ysta[rows, :], axis=0, keepdims=True)
            rows_dx[pl.ds(h, 1), :] = jnp.sum(wide * x_h, axis=0, keepdims=True)
        return carry

    pairs = heads // per
    early = 0
    lax.fori_loop(0, early, intra_heads, 0)

    def st_copy(a, k):
        return remote(
            sb.at[share_rows(k)], sin.at[a - 1, share_rows(k)],
            st_send.at[a - 1, k], st_recv.at[a - 1, k], "seq", jnp.maximum(mine - 2 * a, 0),
        )

    def over_heads(k, do):
        def body(h, carry):
            do(h, pl.ds(pl.multiple_of(h * hdim, hdim), hdim))
            return carry

        lax.fori_loop(k * group, (k + 1) * group, body, 0)

    for k in range(shares):
        @pl.when(even)
        def _():
            l_copy(k).wait_recv()

            def join(h, rows):
                sb[rows, :] = (
                    lf[rows, :] + et_own[pl.ds(h, 1), :] * lin[rows, :].astype(F32)
                ).astype(BF16)
                tf[rows, :] = jnp.zeros((hdim, state), F32)

            over_heads(k, join)

        for a in range(chips - 1, 0, -1):
            @pl.when(even & (chip >= a))
            def _():
                st_copy(a, k).start()

        middle = pairs if k == shares - 1 else (early + pairs) // 2
        lax.fori_loop(early, middle, intra_heads, 0)
        early = middle

    hand_over(0, cuts // 2)

    halves = xg.shape[0]
    span = tokens // halves

    def x_copy(half, k):
        return remote(
            xg.at[half, share_rows(k)], xe.at[half, share_rows(k)],
            x_send.at[half, k], x_recv.at[half, k], "head", helper,
        )

    def x_grads(half, k):
        where = pl.ds(half * span, span)
        for h in range(k * group, (k + 1) * group):
            rows = pl.ds(h * hdim, hdim)
            xg[half, rows, :] = (
                intra[rows, where]
                + end_weight[h : h + 1, half * span : (half + 1) * span] * back[rows, where]
                + skip[h : h + 1, :] * dy[rows, where].astype(F32)
            ).astype(BF16)

    for k in range(shares):
        for a in range(1, chips):
            @pl.when(even & (chip + a < chips))
            def _():
                st_copy(a, k).wait_recv()

                def add(h, rows):
                    tf[rows, :] += (
                        reach[a - 1, pl.ds(h, 1), :] * sin[a - 1, rows, :].astype(F32)
                    )

                over_heads(k, add)

        @pl.when(even)
        def _():
            tb[share_rows(k), :] = tf[share_rows(k), :].astype(BF16)
            t_copy(k).start()

            def enter(h, rows):
                carried[rows, :] = (
                    lin[rows, :].astype(F32) + et_in[0, pl.ds(h, 1), :] * tf[rows, :]
                )

            over_heads(k, enter)

        @pl.when(odd)
        def _():
            t_copy(k).wait_recv()
            carried[share_rows(k), :] = tin[share_rows(k), :].astype(F32)

        back[share_rows(k), :] = dot(carried[share_rows(k), :].astype(BF16), b_ref[...], LAST)
        x_grads(0, k)

        @pl.when(is_end)
        def _():
            x_copy(0, k).start()

    for half in range(1, halves):
        for k in range(shares):
            x_grads(half, k)

    wi_copy.wait()

    hand_over(cuts // 2, cuts)

    @pl.when(is_helper)
    def _():
        for q in range(cuts):
            for a in range(chips):
                w3_copy(a, q, sibling - 2 * a).wait_recv()

    strips = s_send.shape[2] // halves
    splits = strips * halves
    piece = out_rows // strips

    def s_copy(side, e, k, strip):
        rows = pl.ds(pl.multiple_of(strip * piece, piece), piece)
        q = k * strips + strip
        return remote(
            going.at[side, e, k, rows], coming.at[side, e, k, rows],
            s_send.at[side, e, q], s_recv.at[side, e, q], "head", right if side == 0 else left,
        )

    def b_copy(side, e):
        return remote(
            gbc.at[side, e], cbc.at[side, e], b_send.at[side, e], b_recv.at[side, e],
            "head", right if side == 0 else left,
        )

    leant = (n - 2) * bc_rows

    def h_copy():
        start = pl.multiple_of(jnp.where(me == 0, 2 * bc_rows, 0), bc_rows)
        return remote(own_bc.at[pl.ds(start, leant)], hbc, h_send, h_recv, "head", helper)

    def owner_of(side, e):
        return n - 1 - e if side == 0 else e

    def s_sends(side, e):
        return (me < owner_of(side, e)) if side == 0 else (me > owner_of(side, e))

    def s_gets(side, e):
        return (s_sends(side, e) | (me == owner_of(side, e))) & (has_left if side == 0 else has_right)

    def term(owner, k, strip):
        start = pl.multiple_of(owner * out_rows + strip * piece, piece)
        return dot(wi[pl.ds(start, piece), :], xg[k])

    count = (n - 1) * splits

    def bc_of(owner):
        return own_bc[pl.ds(pl.multiple_of(owner * bc_rows, bc_rows), bc_rows), :]

    def slot(index, carry):
        for side in (0, 1):
            place = index - SKEW * (me if side == 0 else n - 1 - me)
            held_at = jnp.clip(place, 0, count - 1)
            e, q = lax.div(held_at, splits), lax.rem(held_at, splits)
            k, strip = lax.div(q, strips), lax.rem(q, strips)
            owner = owner_of(side, e)
            live = (place >= 0) & (place < count)
            rows = pl.ds(pl.multiple_of(strip * piece, piece), piece)
            sends = live & s_sends(side, e)
            aided = helper_of(side) & (e < n - 2)
            far = owner - 2 if side == 0 else owner
            passes = jnp.logical_not(end_of(side) & (e < n - 2))
            gets = s_gets(side, e) & jnp.logical_not(aided)
            closes = q == splits - 1

            @pl.when(sends & passes)
            def _():
                going[side, e, k, rows, :] = term(owner, k, strip).astype(BF16)

                for one in range(halves):
                    @pl.when(helper_of(side) & (place == one * strips))
                    def _():
                        for part in range(shares):
                            x_copy(one, part).wait_recv()

                @pl.when(aided)
                def _():
                    start = pl.multiple_of(far * out_rows + strip * piece, piece)
                    aid = dot(wh[pl.ds(start, piece), :], xe[k])
                    going[side, e, k, rows, :] = (
                        going[side, e, k, rows, :].astype(F32) + aid
                    ).astype(BF16)

                @pl.when(gets)
                def _():
                    s_copy(side, e, k, strip).wait_recv()
                    going[side, e, k, rows, :] = (
                        going[side, e, k, rows, :].astype(F32)
                        + coming[side, e, k, rows, :].astype(F32)
                    ).astype(BF16)

                s_copy(side, e, k, strip).start()

            @pl.when(sends & passes & closes)
            def _():
                gbc[side, e] = bc_of(owner)

                @pl.when(helper_of(side) & (place == splits - 1))
                def _():
                    h_copy().wait_recv()

                @pl.when(aided)
                def _():
                    start = pl.multiple_of(far * bc_rows, bc_rows)
                    gbc[side, e] = (
                        gbc[side, e].astype(F32) + hbc[pl.ds(start, bc_rows), :].astype(F32)
                    ).astype(BF16)

                @pl.when(gets)
                def _():
                    b_copy(side, e).wait_recv()
                    gbc[side, e] = (
                        gbc[side, e].astype(F32) + cbc[side, e].astype(F32)
                    ).astype(BF16)

                b_copy(side, e).start()

            @pl.when(live & (me == owner) & gets)
            def _():
                s_copy(side, e, k, strip).wait_recv()
                where = pl.ds(pl.multiple_of(k * span, span), span)
                acc[rows, where] += coming[side, e, k, rows, :].astype(F32)

                @pl.when(closes)
                def _():
                    b_copy(side, e).wait_recv()
                    acc_bc[...] += cbc[side, e].astype(F32)

        return carry

    lax.fori_loop(0, SKEW, slot, 0)

    for h in range(heads):
        rows = pl.ds(h * hdim, hdim)
        x_h = xt[rows, :].astype(F32)
        xend[rows, :] = (x_h * end_weight[h : h + 1, :]).astype(BF16)
        rows_xs[h : h + 1, :] = jnp.sum(x_h * back[rows, :], axis=0, keepdims=True)
        rows_tail[h : h + 1, :] = jnp.sum(
            states[0, rows, :].astype(F32) * carried[rows, :], axis=0, keepdims=True
        )
    sums = shared[1].astype(BF16)
    carried_t = dot(eye_bf[:state, :state], carried[...].astype(BF16), LAST).astype(BF16)
    own_bc[:state, :] = (dot(ct, sums, LAST) + dot(carried_t, xend[...])).astype(BF16)
    own_bc[state:, :] = (dot(bt, sums) + dot(sbt, dyd[...])).astype(BF16)

    @pl.when(is_end)
    def _():
        for part in range(shares):
            x_copy(0, part).wait_send()
            for half in range(1, halves):
                x_copy(half, part).start()
        h_copy().start()

    acc_bc[...] = bc_of(me).astype(F32)
    for k in range(halves):
        for strip in range(strips):
            acc[pl.ds(strip * piece, piece), pl.ds(k * span, span)] = term(me, k, strip)
    slots = max((n - k) * splits + SKEW * k for k in range(1, n))
    first_part = min(slots, SKEW + 3)
    lax.fori_loop(SKEW, first_part, slot, 0)

    end_terms = end_weight * rows_xs[...]
    cum_grad = rows_r[...] - rows_xi[...] + start_decay * rows_st[...] - end_terms
    tail = jnp.sum(end_terms, axis=1, keepdims=True) + end_total * jnp.sum(
        rows_tail[...], axis=1, keepdims=True
    )
    token = lax.broadcasted_iota(jnp.int32, (heads, tokens), 1)
    cum_grad = cum_grad + jnp.where(token == tokens - 1, tail, 0.0)
    step_grad = dot(cum_grad, upto, LAST, precision=EXACT)
    dt_sum = -rate * step_grad + (rows_xi[...] + end_terms) / step
    dt_grad = dt_sum / (1.0 + jnp.exp(-raw))
    odt_ref[...] = dt_grad
    writes = [
        pltpu.make_async_copy(src, dst, out_sem.at[k])
        for k, (src, dst) in enumerate((
            (o_ref, o_hbm), (obc_ref, obc_hbm), (odt_ref, odt_hbm), (opar_ref, opar_hbm),
        ))
    ]
    writes[2].start()

    def row_of(column):
        at = lax.broadcasted_iota(jnp.int32, (heads, LANES), 0)
        along = lax.broadcasted_iota(jnp.int32, (heads, LANES), 1)
        return jnp.sum(jnp.where(at == along, column, 0.0), axis=0, keepdims=True)

    line = lax.broadcasted_iota(jnp.int32, (8, LANES), 0)
    packet = jnp.zeros((8, LANES), F32)
    for index, terms in enumerate((step_grad * log_step, rows_dx[...], dt_grad)):
        packet = jnp.where(line == index, row_of(jnp.sum(terms, axis=1, keepdims=True)), packet)
    par[...] = packet

    def p_copy(away):
        return remote(
            par, par_in.at[away - 1], p_send.at[away - 1], p_recv.at[away - 1],
            "seq", lax.rem(mine + s - away, s),
        )

    for away in range(1, s):
        p_copy(away).start()

    @pl.when(is_end)
    def _():
        for half in range(1, halves):
            for part in range(shares):
                x_copy(half, part).wait_send()

    lax.fori_loop(first_part, slots, slot, 0)

    o_ref[...] = acc[:out_rows, :].astype(BF16)
    writes[0].start()
    obc_ref[...] = acc_bc[...].astype(BF16)
    writes[1].start()
    value = packet
    for away in range(1, s):
        p_copy(away).wait_recv()
        value = value + par_in[away - 1]
    opar_ref[...] = value[: opar_ref.shape[0], :heads] * scale
    writes[3].start()

    for side in (0, 1):
        for d in range(n - 1):
            @pl.when(g_sends(side, d) & (jnp.logical_not(end_of(side)) if d == 0 else True))
            def _():
                for q in range(parts):
                    g_copy(side, d, q).wait_send()

            skipped = end_of(side) if d < n - 2 else False

            @pl.when(s_sends(side, d) & jnp.logical_not(skipped))
            def _():
                for k in range(halves):
                    for strip in range(strips):
                        s_copy(side, d, k, strip).wait_send()
                b_copy(side, d).wait_send()

    @pl.when(is_end)
    def _():
        for q in range(cuts):
            w1_copy(q).wait_send()
        h_copy().wait_send()

    @pl.when(is_helper)
    def _():
        for q in range(cuts):
            for a in range(chips):
                if a > 0:
                    w2_copy(a, q, mine).wait_send()
                w3_copy(a, q, mine - 2 * a).wait_send()

    for away in range(1, s):
        et_copy(away).wait_send()
        p_copy(away).wait_send()

    for k in range(shares):
        @pl.when(odd)
        def _():
            l_copy(k).wait_send()

        for a in range(1, chips):
            @pl.when(even & (chip >= a))
            def _():
                st_copy(a, k).wait_send()

        @pl.when(even)
        def _():
            t_copy(k).wait_send()
    for write in writes:
        write.wait()


def hand_on_kernel(*refs):
    count = len(refs) // 2
    for k in range(count):
        refs[count + k][...] = refs[k][...]


def handed_on(arrays):
    vmem = pl.BlockSpec(memory_space=pltpu.VMEM)
    return pl.pallas_call(
        hand_on_kernel,
        out_shape=tuple(jax.ShapeDtypeStruct(a.shape, a.dtype) for a in arrays),
        in_specs=[vmem] * len(arrays),
        out_specs=(vmem,) * len(arrays),
        name="hand_on",
    )(*arrays)


def layer(og, x, b, c, raw, bias, alog, skip, states, w_out, w_in):
    n, s = lax.axis_size("head"), lax.axis_size("seq")
    tokens, depth = og.shape
    inner = x.shape[1]
    heads = raw.shape[0]
    hdim = inner // heads
    state = b.shape[1]
    out_rows = w_in.shape[0] // n
    bc_rows = 2 * state // n
    chips = s // 2
    scale = (s * tokens * hdim) ** (-0.5)
    vmem = pl.BlockSpec(memory_space=pltpu.VMEM)
    hbm = pl.BlockSpec(memory_space=pltpu.HBM)
    dma = pltpu.SemaphoreType.DMA
    parts = pieces_of(depth, LANES, 4)
    halves = 2 if tokens % (2 * LANES) == 0 else 1
    splits = pieces_of(out_rows, 16, 2) * halves
    lent = max(n - 2, 1) * out_rows
    cuts = pieces_of(lent // s, 16, parts)
    leant = max(n - 2, 1) * bc_rows

    def wide(dtype):
        return pltpu.VMEM((inner, tokens), dtype)

    def slim(dtype, *lead):
        return pltpu.VMEM((*lead, inner, state), dtype)

    results = (
        jax.ShapeDtypeStruct((out_rows, tokens), BF16),
        jax.ShapeDtypeStruct((bc_rows, tokens), BF16),
        jax.ShapeDtypeStruct((heads, tokens), F32),
        jax.ShapeDtypeStruct((3, heads), F32),
    )
    rows = pltpu.VMEM((heads, tokens), F32)
    packet = pltpu.VMEM((2, n - 1, halves, out_rows, tokens // halves), BF16)
    bc_packet = pltpu.VMEM((2, n - 1, bc_rows, tokens), BF16)
    shared_x = pltpu.VMEM((halves, inner, tokens // halves), BF16)
    scratch = [
        pltpu.VMEM(w_out.shape, BF16),
        pltpu.VMEM(w_in.shape, BF16),
        pltpu.VMEM((2, n - 1, tokens, depth), BF16),
        wide(F32), wide(BF16), wide(BF16), wide(BF16),
        pltpu.VMEM((heads, tokens, tokens), F32),
        pltpu.VMEM((heads, tokens, tokens), BF16),
        wide(F32), wide(F32), wide(F32), wide(BF16), shared_x,
        packet, packet,
        pltpu.VMEM((2 * state, tokens), BF16),
        slim(F32), slim(BF16), slim(BF16), slim(BF16), slim(BF16, chips - 1),
        slim(F32), slim(BF16), slim(BF16), slim(F32),
        pltpu.VMEM((heads, LANES), F32),
        pltpu.VMEM((s - 1, heads, LANES), F32),
        pltpu.VMEM((chips - 1, heads, LANES), F32),
        rows, rows, rows, rows, rows, rows, rows, pltpu.VMEM((heads, state), F32),
        pltpu.VMEM((2, tokens, heads), F32),
        pltpu.VMEM((2, tokens, tokens), F32),
        pltpu.VMEM((8, LANES), F32),
        pltpu.VMEM((s - 1, 8, LANES), F32),
        pltpu.VMEM((bc_rows, tokens), F32), bc_packet, bc_packet,
        pltpu.VMEM((lent, inner), BF16), shared_x, pltpu.VMEM((leant, tokens), BF16),
        *[pltpu.VMEM(a.shape, a.dtype) for a in results],
        *[pltpu.VMEM(a.shape, a.dtype) for a in (og, x, b, c, raw, states)],
        dma((6,)), dma((4,)), dma((2, n - 1, parts)), dma((2, n - 1, parts)), dma((n,)), dma,
        dma((2, n - 1, splits)), dma((2, n - 1, splits)),
        dma((s - 1,)), dma((s - 1,)),
        dma((4,)), dma((4,)), dma((chips - 1, 4)), dma((chips - 1, 4)), dma((4,)), dma((4,)),
        dma((s - 1,)), dma((s - 1,)),
        dma((2, n - 1)), dma((2, n - 1)), dma((cuts,)), dma((cuts,)),
        dma((chips - 1, cuts)), dma((chips - 1, cuts)), dma((chips, cuts)), dma((chips, cuts)),
        dma((halves, 4)), dma((halves, 4)), dma, dma,
    ]
    outs = pl.pallas_call(
        functools.partial(layer_kernel, n, s, scale),
        out_shape=results,
        in_specs=[hbm] * 5 + [vmem] * 3 + [hbm] * 3,
        out_specs=(hbm,) * 4,
        scratch_shapes=scratch,
        compiler_params=pltpu.CompilerParams(
            collective_id=0, has_side_effects=True, vmem_limit_bytes=58 * 2**20
        ),
        name="layer",
    )(og, x, b, c, raw, bias[None], alog[None], skip[None], states, w_out, w_in)
    return handed_on(outs)


def solution(mesh):
    return jax.shard_map(
        layer,
        mesh=mesh,
        in_specs=(
            P("seq", "head"),
            P("seq", "head"),
            P("seq", None),
            P("seq", None),
            P("head", "seq"),
            P("head"),
            P("head"),
            P("head"),
            P("seq", "head", None),
            P("head", None),
            P(None, "head"),
        ),
        out_specs=(P("head", "seq"), P("head", "seq"), P("head", "seq"), P(None, "head")),
        check_vma=False,
    )
```

```python
import functools

import jax
import jax.numpy as jnp
from jax import lax
from jax.experimental import pallas as pl
from jax.experimental.pallas import tpu as pltpu
from jax.sharding import PartitionSpec as P

LAST = (((1,), (1,)), ((), ()))
FIRST = (((0,), (0,)), ((), ()))
PLAIN = (((1,), (0,)), ((), ()))
MESH = pl.DeviceIdType.MESH
EXACT = lax.Precision.HIGHEST
F32, BF16 = jnp.float32, jnp.bfloat16
SKEW = 3
LANES = 128


def dot(a, b, dims=PLAIN, precision=None):
    return lax.dot_general(a, b, dims, precision=precision, preferred_element_type=F32)


def pieces_of(extent, unit, most):
    count = most
    while extent % (count * unit):
        count //= 2
    return count


def remote(src, dst, send, recv, axis, target):
    return pltpu.make_async_remote_copy(
        src_ref=src, dst_ref=dst, send_sem=send, recv_sem=recv,
        device_id={axis: target}, device_id_type=MESH,
    )


def layer_kernel(
    n, s, scale,
    og_hbm, x_hbm, b_hbm, c_hbm, raw_hbm, bias_ref, alog_ref, skip_ref, states_hbm, w_out, w_in,
    o_hbm, obc_hbm, odt_hbm, opar_hbm,
    wo, wi, held, acc, dy, dyd, xt, mask, km, intra, ysta, back, xend, xg,
    going, coming, own_bc, lf, lb, lin, sb, sin, tf, tb, tin, carried,
    et_own, et_in, reach, rows_step, rows_cum, rows_r, rows_xi, rows_st, rows_dx, rows_xs, rows_tail,
    cols, shared, par, par_in, acc_bc, gbc, cbc, wh, xe, hbc, o_ref, obc_ref, odt_ref, opar_ref, og, x_ref, b_ref, c_ref, raw_ref, states,
    in_sem, out_sem, g_send, g_recv, wo_sem, wi_sem, s_send, s_recv, et_send, et_recv,
    l_send, l_recv, st_send, st_recv, t_send, t_recv, p_send, p_recv,
    b_send, b_recv, w1_send, w1_recv, w2_send, w2_recv, w3_send, w3_recv, x_send, x_recv, h_send, h_recv,
):
    me = lax.axis_index("head")
    mine = lax.axis_index("seq")
    tokens, depth = og.shape
    heads = raw_ref.shape[0]
    inner = x_ref.shape[1]
    hdim = inner // heads
    state = b_ref.shape[1]
    per = LANES // hdim
    chips = s // 2
    chip = mine // 2
    odd = lax.rem(mine, 2) == 1
    even = jnp.logical_not(odd)
    right, left = lax.rem(me + 1, n), lax.rem(me + n - 1, n)
    has_right, has_left = me < n - 1, me > 0
    tile = min(256, inner)

    def w_copy(offset):
        where = pl.ds(pl.multiple_of(lax.rem(me + offset, n) * depth, depth), depth)
        return pltpu.make_async_copy(w_out.at[:, where], wo.at[:, where], wo_sem.at[offset])

    wi_copy = pltpu.make_async_copy(w_in, wi, wi_sem)
    w_order = [0]
    for d in range(n - 1):
        for offset in (n - 1 - d, d + 1):
            if offset not in w_order:
                w_order.append(offset)
    barrier = pltpu.get_barrier_semaphore()
    for neighbour in (left, right):
        pl.semaphore_signal(barrier, inc=1, device_id={"head": neighbour}, device_id_type=MESH)
    for away in range(1, s):
        pl.semaphore_signal(
            barrier, inc=1, device_id={"seq": lax.rem(mine + away, s)}, device_id_type=MESH
        )
    loads = [
        pltpu.make_async_copy(src, dst, in_sem.at[k])
        for k, (src, dst) in enumerate((
            (raw_hbm, raw_ref), (b_hbm, b_ref), (c_hbm, c_ref), (x_hbm, x_ref),
            (states_hbm, states), (og_hbm, og),
        ))
    ]
    for load in loads:
        load.start()

    pl.semaphore_wait(barrier, 2 + s - 1)

    leans = n >= 4
    out_rows, bc_rows = o_ref.shape[0], obc_ref.shape[0]
    is_end = leans & ((me == 0) | (me == n - 1))
    is_helper = leans & ((me == 1) | (me == n - 2))
    helper = jnp.where(me == 0, 1, n - 2)
    sibling = mine + 1 - 2 * lax.rem(mine, 2)

    def end_of(side):
        return leans & (me == (0 if side == 0 else n - 1))

    def helper_of(side):
        return leans & (me == (1 if side == 0 else n - 2))

    share = wh.shape[0] // s
    cuts = w1_send.shape[0]
    cut = share // cuts

    def lent(place, q):
        return pl.ds(pl.multiple_of(lax.rem(place + s, s) * share + q * cut, cut), cut)

    def w1_copy(q):
        start = jnp.where(me == 0, 2 * out_rows, 0) + mine * share + q * cut
        return remote(
            w_in.at[pl.ds(pl.multiple_of(start, 16), cut)], wh.at[lent(mine, q)],
            w1_send.at[q], w1_recv.at[q], "head", helper,
        )

    def w2_copy(a, q, place):
        return remote(
            wh.at[lent(place, q)], wh.at[lent(place, q)],
            w2_send.at[a - 1, q], w2_recv.at[a - 1, q], "seq", lax.rem(mine + 2 * a, s),
        )

    def w3_copy(a, q, place):
        return remote(
            wh.at[lent(place, q)], wh.at[lent(place, q)],
            w3_send.at[a, q], w3_recv.at[a, q], "seq", sibling,
        )

    parts = pieces_of(depth, LANES, 4)
    width = depth // parts

    def g_copy(side, d, q):
        where = pl.ds(q * width, width)
        src = og_hbm.at[:, where] if d == 0 else held.at[side, d - 1, :, where]
        return remote(
            src, held.at[side, d, :, where], g_send.at[side, d, q], g_recv.at[side, d, q],
            "head", right if side == 0 else left,
        )

    def g_sends(side, d):
        return (has_right & (me >= d)) if side == 0 else (has_left & (me + d <= n - 1))

    def g_gets(side, d):
        return (me > d) if side == 0 else (me + 1 + d <= n - 1)

    for side in (0, 1):
        @pl.when(g_sends(side, 0))
        def _():
            for q in range(parts):
                g_copy(side, 0, q).start()

    for offset in w_order:
        w_copy(offset).start()
    wi_copy.start()
    for load in loads:
        load.wait()

    def column_of(row):
        at = lax.broadcasted_iota(jnp.int32, (heads, heads), 0)
        along = lax.broadcasted_iota(jnp.int32, (heads, heads), 1)
        return jnp.sum(jnp.where(at == along, row, 0.0), axis=1, keepdims=True)

    bias = column_of(bias_ref[...])
    rate = jnp.exp(column_of(alog_ref[...]))
    skip = column_of(skip_ref[...])
    first = lax.broadcasted_iota(jnp.int32, (tokens, tokens), 0)
    second = lax.broadcasted_iota(jnp.int32, (tokens, tokens), 1)
    upto = (first <= second).astype(F32)
    raw = raw_ref[...] + bias
    step = jnp.maximum(raw, 0.0) + jnp.log1p(jnp.exp(-jnp.abs(raw)))
    log_step = -rate * step
    cum = dot(log_step, upto, precision=EXACT)
    total = cum[:, tokens - 1 : tokens]
    end_decay = jnp.exp(total - cum)
    start_decay = jnp.exp(cum)
    end_total = jnp.exp(total)
    end_weight = step * end_decay
    rows_step[...] = step
    rows_cum[...] = cum
    et_own[...] = jnp.broadcast_to(end_total, et_own.shape)

    def et_copy(away):
        return remote(
            et_own, et_in.at[away - 1], et_send.at[away - 1], et_recv.at[away - 1],
            "seq", lax.rem(mine + s - away, s),
        )

    for away in range(1, s):
        et_copy(away).start()

    eye = (first == second).astype(F32)
    cols[0] = dot(eye, cum, LAST, precision=EXACT)
    cols[1] = dot(eye, step, LAST, precision=EXACT)
    shared[0] = dot(b_ref[...], c_ref[...], LAST)
    shared[1] = jnp.zeros((tokens, tokens), F32)
    lane = lax.broadcasted_iota(jnp.int32, (tokens, heads), 1)

    def masks(h, carry):
        col = jnp.sum(jnp.where(lane == h, cols[0], 0.0), axis=1, keepdims=True)
        col_step = jnp.sum(jnp.where(lane == h, cols[1], 0.0), axis=1, keepdims=True)
        gap = rows_cum[pl.ds(h, 1), :] - col
        value = jnp.where(first <= second, jnp.exp(jnp.minimum(gap, 0.0)) * col_step, 0.0)
        mask[h] = value
        km[h] = (shared[0] * value).astype(BF16)
        return carry

    lax.fori_loop(0, heads, masks, 0)
    eye_bf = eye[:tile, :tile].astype(BF16)
    for k in range(inner // tile):
        where = pl.ds(k * tile, tile)
        xt[where, :] = dot(eye_bf, x_ref[:, where], LAST).astype(BF16)
        ysta[where, :] = dot(states[0, where, :], c_ref[...], LAST)
    ct = dot(eye_bf[:state, :state], c_ref[...], LAST).astype(BF16)
    bt = dot(eye_bf[:state, :state], b_ref[...], LAST).astype(BF16)
    sbt = dot(eye_bf[:state, :state], states[0], LAST).astype(BF16)

    def multiply(source, offset, start, extent, fresh):
        if start == 0:
            w_copy(offset).wait()
        base = lax.rem(me + offset, n) * depth + start
        where = pl.ds(pl.multiple_of(base, extent), extent)

        def body(k, carry):
            outs = pl.ds(pl.multiple_of(k * tile, tile), tile)
            part = dot(wo[outs, where], source[:, pl.ds(start, extent)], LAST)
            acc[outs, :] = part if fresh else acc[outs, :] + part
            return carry

        lax.fori_loop(0, inner // tile, body, 0)

    multiply(og, 0, 0, depth, True)
    for side in (0, 1):
        @pl.when(end_of(side))
        def _():
            for q in range(parts):
                g_copy(side, 0, q).wait_send()
            for q in range(cuts):
                w1_copy(q).start()

    for d in range(n - 1):
        for q in range(parts):
            for side in (0, 1):
                @pl.when(g_gets(side, d))
                def _():
                    g_copy(side, d, q).wait_recv()
                if d + 1 < n - 1:
                    @pl.when(g_gets(side, d) & g_sends(side, d + 1))
                    def _():
                        g_copy(side, d + 1, q).start()
            if d == 1 and q < cuts:
                @pl.when(is_helper)
                def _():
                    w1_copy(q).wait_recv()
                    for a in range(1, chips):
                        w2_copy(a, q, mine).start()
                    w3_copy(0, q, mine).start()
            for side in (0, 1):
                @pl.when(g_gets(side, d))
                def _():
                    offset = n - 1 - d if side == 0 else d + 1
                    multiply(held.at[side, d], offset, q * width, width, False)

    shares = 4 if heads % 4 == 0 else 1
    group = heads // shares

    def share_rows(k):
        return pl.ds(k * group * hdim, group * hdim)

    def l_copy(k):
        return remote(
            lb.at[share_rows(k)], lin.at[share_rows(k)], l_send.at[k], l_recv.at[k],
            "seq", sibling,
        )

    def t_copy(k):
        return remote(
            tb.at[share_rows(k)], tin.at[share_rows(k)], t_send.at[k], t_recv.at[k],
            "seq", sibling,
        )

    for k in range(shares):
        for h in range(k * group, (k + 1) * group):
            rows = pl.ds(h * hdim, hdim)
            rounded = acc[rows, :].astype(BF16)
            dy[rows, :] = rounded
            dyd[rows, :] = (rounded.astype(F32) * start_decay[h : h + 1, :]).astype(BF16)
        where = share_rows(k)
        value = dot(dyd[where, :], c_ref[...])
        lf[where, :] = value
        lb[where, :] = value.astype(BF16)

        @pl.when(odd)
        def _():
            l_copy(k).start()

    def hand_over(low, high):
        @pl.when(is_helper)
        def _():
            for q in range(low, high):
                for a in range(1, chips):
                    w2_copy(a, q, mine - 2 * a).wait_recv()
                    w3_copy(a, q, mine - 2 * a).start()

    for away in range(1, s):
        et_copy(away).wait_recv()
    weight = jnp.ones((heads, LANES), F32)
    for a in range(1, chips):
        reach[a - 1] = weight
        weight = weight * et_in[2 * a - 1] * et_in[2 * a]

    half_lane = lax.broadcasted_iota(jnp.int32, (tokens, LANES), 1) // hdim

    def intra_heads(pair, carry):
        block = pl.ds(pl.multiple_of(pair * LANES, LANES), LANES)
        x_pair = x_ref[:, block]
        dy_pair = dy[block, :]
        for sub in range(per):
            h = pair * per + sub
            rows = pl.ds(pl.multiple_of(h * hdim, hdim), hdim)
            dots = dot(jnp.where(half_lane == sub, x_pair, jnp.zeros_like(x_pair)), dy_pair)
            shared[1] += dots * mask[h]
            rows_r[pl.ds(h, 1), :] = jnp.sum(dots * km[h].astype(F32), axis=0, keepdims=True)
            dy_h = dy[rows, :]
            x_h = xt[rows, :].astype(F32)
            inside = dot(dy_h, km[h], LAST)
            intra[rows, :] = inside
            wide = dy_h.astype(F32)
            rows_xi[pl.ds(h, 1), :] = jnp.sum(x_h * inside, axis=0, keepdims=True)
            rows_st[pl.ds(h, 1), :] = jnp.sum(wide * ysta[rows, :], axis=0, keepdims=True)
            rows_dx[pl.ds(h, 1), :] = jnp.sum(wide * x_h, axis=0, keepdims=True)
        return carry

    pairs = heads // per
    early = 0
    lax.fori_loop(0, early, intra_heads, 0)

    def st_copy(a, k):
        return remote(
            sb.at[share_rows(k)], sin.at[a - 1, share_rows(k)],
            st_send.at[a - 1, k], st_recv.at[a - 1, k], "seq", jnp.maximum(mine - 2 * a, 0),
        )

    def over_heads(k, do):
        def body(h, carry):
            do(h, pl.ds(pl.multiple_of(h * hdim, hdim), hdim))
            return carry

        lax.fori_loop(k * group, (k + 1) * group, body, 0)

    for k in range(shares):
        @pl.when(even)
        def _():
            l_copy(k).wait_recv()

            def join(h, rows):
                sb[rows, :] = (
                    lf[rows, :] + et_own[pl.ds(h, 1), :] * lin[rows, :].astype(F32)
                ).astype(BF16)
                tf[rows, :] = jnp.zeros((hdim, state), F32)

            over_heads(k, join)

        for a in range(chips - 1, 0, -1):
            @pl.when(even & (chip >= a))
            def _():
                st_copy(a, k).start()

        middle = pairs if k == shares - 1 else (early + pairs) // 2
        lax.fori_loop(early, middle, intra_heads, 0)
        early = middle

    hand_over(0, cuts // 2)

    halves = xg.shape[0]
    span = tokens // halves

    def x_copy(half, k):
        return remote(
            xg.at[half, share_rows(k)], xe.at[half, share_rows(k)],
            x_send.at[half, k], x_recv.at[half, k], "head", helper,
        )

    def x_grads(half, k):
        where = pl.ds(half * span, span)
        for h in range(k * group, (k + 1) * group):
            rows = pl.ds(h * hdim, hdim)
            xg[half, rows, :] = (
                intra[rows, where]
                + end_weight[h : h + 1, half * span : (half + 1) * span] * back[rows, where]
                + skip[h : h + 1, :] * dy[rows, where].astype(F32)
            ).astype(BF16)

    for k in range(shares):
        for a in range(1, chips):
            @pl.when(even & (chip + a < chips))
            def _():
                st_copy(a, k).wait_recv()

                def add(h, rows):
                    tf[rows, :] += (
                        reach[a - 1, pl.ds(h, 1), :] * sin[a - 1, rows, :].astype(F32)
                    )

                over_heads(k, add)

        @pl.when(even)
        def _():
            tb[share_rows(k), :] = tf[share_rows(k), :].astype(BF16)
            t_copy(k).start()

            def enter(h, rows):
                carried[rows, :] = (
                    lin[rows, :].astype(F32) + et_in[0, pl.ds(h, 1), :] * tf[rows, :]
                )

            over_heads(k, enter)

        @pl.when(odd)
        def _():
            t_copy(k).wait_recv()
            carried[share_rows(k), :] = tin[share_rows(k), :].astype(F32)

        back[share_rows(k), :] = dot(carried[share_rows(k), :].astype(BF16), b_ref[...], LAST)
        x_grads(0, k)

        @pl.when(is_end)
        def _():
            x_copy(0, k).start()

    for half in range(1, halves):
        for k in range(shares):
            x_grads(half, k)

            @pl.when(is_end)
            def _():
                x_copy(half, k).start()

    wi_copy.wait()

    hand_over(cuts // 2, cuts)

    @pl.when(is_helper)
    def _():
        for q in range(cuts):
            for a in range(chips):
                w3_copy(a, q, sibling - 2 * a).wait_recv()

    strips = s_send.shape[2] // halves
    splits = strips * halves
    piece = out_rows // strips

    def s_copy(side, e, k, strip):
        rows = pl.ds(pl.multiple_of(strip * piece, piece), piece)
        q = k * strips + strip
        return remote(
            going.at[side, e, k, rows], coming.at[side, e, k, rows],
            s_send.at[side, e, q], s_recv.at[side, e, q], "head", right if side == 0 else left,
        )

    def b_copy(side, e):
        return remote(
            gbc.at[side, e], cbc.at[side, e], b_send.at[side, e], b_recv.at[side, e],
            "head", right if side == 0 else left,
        )

    leant = (n - 2) * bc_rows

    def h_copy():
        start = pl.multiple_of(jnp.where(me == 0, 2 * bc_rows, 0), bc_rows)
        return remote(own_bc.at[pl.ds(start, leant)], hbc, h_send, h_recv, "head", helper)

    def owner_of(side, e):
        return n - 1 - e if side == 0 else e

    def s_sends(side, e):
        return (me < owner_of(side, e)) if side == 0 else (me > owner_of(side, e))

    def s_gets(side, e):
        return (s_sends(side, e) | (me == owner_of(side, e))) & (has_left if side == 0 else has_right)

    def term(owner, k, strip):
        start = pl.multiple_of(owner * out_rows + strip * piece, piece)
        return dot(wi[pl.ds(start, piece), :], xg[k])

    count = (n - 1) * splits

    def bc_of(owner):
        return own_bc[pl.ds(pl.multiple_of(owner * bc_rows, bc_rows), bc_rows), :]

    def slot(index, carry):
        for side in (0, 1):
            place = index - SKEW * (me if side == 0 else n - 1 - me)
            held_at = jnp.clip(place, 0, count - 1)
            e, q = lax.div(held_at, splits), lax.rem(held_at, splits)
            k, strip = lax.div(q, strips), lax.rem(q, strips)
            owner = owner_of(side, e)
            live = (place >= 0) & (place < count)
            rows = pl.ds(pl.multiple_of(strip * piece, piece), piece)
            sends = live & s_sends(side, e)
            aided = helper_of(side) & (e < n - 2)
            far = owner - 2 if side == 0 else owner
            passes = jnp.logical_not(end_of(side) & (e < n - 2))
            gets = s_gets(side, e) & jnp.logical_not(aided)
            closes = q == splits - 1

            @pl.when(sends & passes)
            def _():
                going[side, e, k, rows, :] = term(owner, k, strip).astype(BF16)

                for one in range(halves):
                    @pl.when(helper_of(side) & (place == one * strips))
                    def _():
                        for part in range(shares):
                            x_copy(one, part).wait_recv()

                @pl.when(aided)
                def _():
                    start = pl.multiple_of(far * out_rows + strip * piece, piece)
                    aid = dot(wh[pl.ds(start, piece), :], xe[k])
                    going[side, e, k, rows, :] = (
                        going[side, e, k, rows, :].astype(F32) + aid
                    ).astype(BF16)

                @pl.when(gets)
                def _():
                    s_copy(side, e, k, strip).wait_recv()
                    going[side, e, k, rows, :] = (
                        going[side, e, k, rows, :].astype(F32)
                        + coming[side, e, k, rows, :].astype(F32)
                    ).astype(BF16)

                s_copy(side, e, k, strip).start()

            @pl.when(sends & passes & closes)
            def _():
                gbc[side, e] = bc_of(owner)

                @pl.when(helper_of(side) & (place == splits - 1))
                def _():
                    h_copy().wait_recv()

                @pl.when(aided)
                def _():
                    start = pl.multiple_of(far * bc_rows, bc_rows)
                    gbc[side, e] = (
                        gbc[side, e].astype(F32) + hbc[pl.ds(start, bc_rows), :].astype(F32)
                    ).astype(BF16)

                @pl.when(gets)
                def _():
                    b_copy(side, e).wait_recv()
                    gbc[side, e] = (
                        gbc[side, e].astype(F32) + cbc[side, e].astype(F32)
                    ).astype(BF16)

                b_copy(side, e).start()

            @pl.when(live & (me == owner) & gets)
            def _():
                s_copy(side, e, k, strip).wait_recv()
                where = pl.ds(pl.multiple_of(k * span, span), span)
                acc[rows, where] += coming[side, e, k, rows, :].astype(F32)

                @pl.when(closes)
                def _():
                    b_copy(side, e).wait_recv()
                    acc_bc[...] += cbc[side, e].astype(F32)

        return carry

    lax.fori_loop(0, SKEW, slot, 0)

    for h in range(heads):
        rows = pl.ds(h * hdim, hdim)
        x_h = xt[rows, :].astype(F32)
        xend[rows, :] = (x_h * end_weight[h : h + 1, :]).astype(BF16)
        rows_xs[h : h + 1, :] = jnp.sum(x_h * back[rows, :], axis=0, keepdims=True)
        rows_tail[h : h + 1, :] = jnp.sum(
            states[0, rows, :].astype(F32) * carried[rows, :], axis=0, keepdims=True
        )
    sums = shared[1].astype(BF16)
    carried_t = dot(eye_bf[:state, :state], carried[...].astype(BF16), LAST).astype(BF16)
    own_bc[:state, :] = (dot(ct, sums, LAST) + dot(carried_t, xend[...])).astype(BF16)
    own_bc[state:, :] = (dot(bt, sums) + dot(sbt, dyd[...])).astype(BF16)

    @pl.when(is_end)
    def _():
        for part in range(shares):
            x_copy(0, part).wait_send()
        h_copy().start()

    acc_bc[...] = bc_of(me).astype(F32)
    for k in range(halves):
        for strip in range(strips):
            acc[pl.ds(strip * piece, piece), pl.ds(k * span, span)] = term(me, k, strip)
    slots = max((n - k) * splits + SKEW * k for k in range(1, n))
    first_part = min(slots, SKEW + 3)
    lax.fori_loop(SKEW, first_part, slot, 0)

    end_terms = end_weight * rows_xs[...]
    cum_grad = rows_r[...] - rows_xi[...] + start_decay * rows_st[...] - end_terms
    tail = jnp.sum(end_terms, axis=1, keepdims=True) + end_total * jnp.sum(
        rows_tail[...], axis=1, keepdims=True
    )
    token = lax.broadcasted_iota(jnp.int32, (heads, tokens), 1)
    cum_grad = cum_grad + jnp.where(token == tokens - 1, tail, 0.0)
    step_grad = dot(cum_grad, upto, LAST, precision=EXACT)
    dt_sum = -rate * step_grad + (rows_xi[...] + end_terms) / step
    dt_grad = dt_sum / (1.0 + jnp.exp(-raw))
    odt_ref[...] = dt_grad
    writes = [
        pltpu.make_async_copy(src, dst, out_sem.at[k])
        for k, (src, dst) in enumerate((
            (o_ref, o_hbm), (obc_ref, obc_hbm), (odt_ref, odt_hbm), (opar_ref, opar_hbm),
        ))
    ]
    writes[2].start()

    def row_of(column):
        at = lax.broadcasted_iota(jnp.int32, (heads, LANES), 0)
        along = lax.broadcasted_iota(jnp.int32, (heads, LANES), 1)
        return jnp.sum(jnp.where(at == along, column, 0.0), axis=0, keepdims=True)

    line = lax.broadcasted_iota(jnp.int32, (8, LANES), 0)
    packet = jnp.zeros((8, LANES), F32)
    for index, terms in enumerate((step_grad * log_step, rows_dx[...], dt_grad)):
        packet = jnp.where(line == index, row_of(jnp.sum(terms, axis=1, keepdims=True)), packet)
    par[...] = packet

    def p_copy(away):
        return remote(
            par, par_in.at[away - 1], p_send.at[away - 1], p_recv.at[away - 1],
            "seq", lax.rem(mine + s - away, s),
        )

    for away in range(1, s):
        p_copy(away).start()

    @pl.when(is_end)
    def _():
        for half in range(1, halves):
            for part in range(shares):
                x_copy(half, part).wait_send()

    lax.fori_loop(first_part, slots, slot, 0)

    o_ref[...] = acc[:out_rows, :].astype(BF16)
    writes[0].start()
    obc_ref[...] = acc_bc[...].astype(BF16)
    writes[1].start()
    value = packet
    for away in range(1, s):
        p_copy(away).wait_recv()
        value = value + par_in[away - 1]
    opar_ref[...] = value[: opar_ref.shape[0], :heads] * scale
    writes[3].start()

    for side in (0, 1):
        for d in range(n - 1):
            @pl.when(g_sends(side, d) & (jnp.logical_not(end_of(side)) if d == 0 else True))
            def _():
                for q in range(parts):
                    g_copy(side, d, q).wait_send()

            skipped = end_of(side) if d < n - 2 else False

            @pl.when(s_sends(side, d) & jnp.logical_not(skipped))
            def _():
                for k in range(halves):
                    for strip in range(strips):
                        s_copy(side, d, k, strip).wait_send()
                b_copy(side, d).wait_send()

    @pl.when(is_end)
    def _():
        for q in range(cuts):
            w1_copy(q).wait_send()
        h_copy().wait_send()

    @pl.when(is_helper)
    def _():
        for q in range(cuts):
            for a in range(chips):
                if a > 0:
                    w2_copy(a, q, mine).wait_send()
                w3_copy(a, q, mine - 2 * a).wait_send()

    for away in range(1, s):
        et_copy(away).wait_send()
        p_copy(away).wait_send()

    for k in range(shares):
        @pl.when(odd)
        def _():
            l_copy(k).wait_send()

        for a in range(1, chips):
            @pl.when(even & (chip >= a))
            def _():
                st_copy(a, k).wait_send()

        @pl.when(even)
        def _():
            t_copy(k).wait_send()
    for write in writes:
        write.wait()


def hand_on_kernel(*refs):
    count = len(refs) // 2
    for k in range(count):
        refs[count + k][...] = refs[k][...]


def handed_on(arrays):
    vmem = pl.BlockSpec(memory_space=pltpu.VMEM)
    return pl.pallas_call(
        hand_on_kernel,
        out_shape=tuple(jax.ShapeDtypeStruct(a.shape, a.dtype) for a in arrays),
        in_specs=[vmem] * len(arrays),
        out_specs=(vmem,) * len(arrays),
        name="hand_on",
    )(*arrays)


def layer(og, x, b, c, raw, bias, alog, skip, states, w_out, w_in):
    n, s = lax.axis_size("head"), lax.axis_size("seq")
    tokens, depth = og.shape
    inner = x.shape[1]
    heads = raw.shape[0]
    hdim = inner // heads
    state = b.shape[1]
    out_rows = w_in.shape[0] // n
    bc_rows = 2 * state // n
    chips = s // 2
    scale = (s * tokens * hdim) ** (-0.5)
    vmem = pl.BlockSpec(memory_space=pltpu.VMEM)
    hbm = pl.BlockSpec(memory_space=pltpu.HBM)
    dma = pltpu.SemaphoreType.DMA
    parts = pieces_of(depth, LANES, 4)
    halves = 2 if tokens % (2 * LANES) == 0 else 1
    splits = pieces_of(out_rows, 16, 2) * halves
    lent = max(n - 2, 1) * out_rows
    cuts = pieces_of(lent // s, 16, parts)
    leant = max(n - 2, 1) * bc_rows

    def wide(dtype):
        return pltpu.VMEM((inner, tokens), dtype)

    def slim(dtype, *lead):
        return pltpu.VMEM((*lead, inner, state), dtype)

    results = (
        jax.ShapeDtypeStruct((out_rows, tokens), BF16),
        jax.ShapeDtypeStruct((bc_rows, tokens), BF16),
        jax.ShapeDtypeStruct((heads, tokens), F32),
        jax.ShapeDtypeStruct((3, heads), F32),
    )
    rows = pltpu.VMEM((heads, tokens), F32)
    packet = pltpu.VMEM((2, n - 1, halves, out_rows, tokens // halves), BF16)
    bc_packet = pltpu.VMEM((2, n - 1, bc_rows, tokens), BF16)
    shared_x = pltpu.VMEM((halves, inner, tokens // halves), BF16)
    scratch = [
        pltpu.VMEM(w_out.shape, BF16),
        pltpu.VMEM(w_in.shape, BF16),
        pltpu.VMEM((2, n - 1, tokens, depth), BF16),
        wide(F32), wide(BF16), wide(BF16), wide(BF16),
        pltpu.VMEM((heads, tokens, tokens), F32),
        pltpu.VMEM((heads, tokens, tokens), BF16),
        wide(F32), wide(F32), wide(F32), wide(BF16), shared_x,
        packet, packet,
        pltpu.VMEM((2 * state, tokens), BF16),
        slim(F32), slim(BF16), slim(BF16), slim(BF16), slim(BF16, chips - 1),
        slim(F32), slim(BF16), slim(BF16), slim(F32),
        pltpu.VMEM((heads, LANES), F32),
        pltpu.VMEM((s - 1, heads, LANES), F32),
        pltpu.VMEM((chips - 1, heads, LANES), F32),
        rows, rows, rows, rows, rows, rows, rows, pltpu.VMEM((heads, state), F32),
        pltpu.VMEM((2, tokens, heads), F32),
        pltpu.VMEM((2, tokens, tokens), F32),
        pltpu.VMEM((8, LANES), F32),
        pltpu.VMEM((s - 1, 8, LANES), F32),
        pltpu.VMEM((bc_rows, tokens), F32), bc_packet, bc_packet,
        pltpu.VMEM((lent, inner), BF16), shared_x, pltpu.VMEM((leant, tokens), BF16),
        *[pltpu.VMEM(a.shape, a.dtype) for a in results],
        *[pltpu.VMEM(a.shape, a.dtype) for a in (og, x, b, c, raw, states)],
        dma((6,)), dma((4,)), dma((2, n - 1, parts)), dma((2, n - 1, parts)), dma((n,)), dma,
        dma((2, n - 1, splits)), dma((2, n - 1, splits)),
        dma((s - 1,)), dma((s - 1,)),
        dma((4,)), dma((4,)), dma((chips - 1, 4)), dma((chips - 1, 4)), dma((4,)), dma((4,)),
        dma((s - 1,)), dma((s - 1,)),
        dma((2, n - 1)), dma((2, n - 1)), dma((cuts,)), dma((cuts,)),
        dma((chips - 1, cuts)), dma((chips - 1, cuts)), dma((chips, cuts)), dma((chips, cuts)),
        dma((halves, 4)), dma((halves, 4)), dma, dma,
    ]
    outs = pl.pallas_call(
        functools.partial(layer_kernel, n, s, scale),
        out_shape=results,
        in_specs=[hbm] * 5 + [vmem] * 3 + [hbm] * 3,
        out_specs=(hbm,) * 4,
        scratch_shapes=scratch,
        compiler_params=pltpu.CompilerParams(
            collective_id=0, has_side_effects=True, vmem_limit_bytes=58 * 2**20
        ),
        name="layer",
    )(og, x, b, c, raw, bias[None], alog[None], skip[None], states, w_out, w_in)
    return handed_on(outs)


def solution(mesh):
    return jax.shard_map(
        layer,
        mesh=mesh,
        in_specs=(
            P("seq", "head"),
            P("seq", "head"),
            P("seq", None),
            P("seq", None),
            P("head", "seq"),
            P("head"),
            P("head"),
            P("head"),
            P("seq", "head", None),
            P("head", None),
            P(None, "head"),
        ),
        out_specs=(P("head", "seq"), P("head", "seq"), P("head", "seq"), P(None, "head")),
        check_vma=False,
    )
```

```python
import functools

import jax
import jax.numpy as jnp
from jax import lax
from jax.experimental import pallas as pl
from jax.experimental.pallas import tpu as pltpu
from jax.sharding import PartitionSpec as P

LAST = (((1,), (1,)), ((), ()))
FIRST = (((0,), (0,)), ((), ()))
PLAIN = (((1,), (0,)), ((), ()))
MESH = pl.DeviceIdType.MESH
EXACT = lax.Precision.HIGHEST
F32, BF16 = jnp.float32, jnp.bfloat16
SKEW = 3
LANES = 128


def dot(a, b, dims=PLAIN, precision=None):
    return lax.dot_general(a, b, dims, precision=precision, preferred_element_type=F32)


def pieces_of(extent, unit, most):
    count = most
    while extent % (count * unit):
        count //= 2
    return count


def remote(src, dst, send, recv, axis, target):
    return pltpu.make_async_remote_copy(
        src_ref=src, dst_ref=dst, send_sem=send, recv_sem=recv,
        device_id={axis: target}, device_id_type=MESH,
    )


def layer_kernel(
    n, s, scale,
    og_hbm, x_hbm, b_hbm, c_hbm, raw_hbm, bias_ref, alog_ref, skip_ref, states_hbm, w_out, w_in,
    o_hbm, obc_hbm, odt_hbm, opar_hbm,
    wo, wi, held, acc, dy, dyd, xt, mask, km, intra, ysta, back, xend, xg,
    going, coming, own_bc, lf, lb, lin, sb, sin, tf, tb, tin, carried,
    et_own, et_in, reach, rows_step, rows_cum, rows_r, rows_xi, rows_st, rows_dx, rows_xs, rows_tail,
    cols, shared, par, par_in, acc_bc, gbc, cbc, wh, xe, hbc, o_ref, obc_ref, odt_ref, opar_ref, og, x_ref, b_ref, c_ref, raw_ref, states,
    in_sem, out_sem, g_send, g_recv, wo_sem, wi_sem, s_send, s_recv, et_send, et_recv,
    l_send, l_recv, st_send, st_recv, t_send, t_recv, p_send, p_recv,
    b_send, b_recv, w1_send, w1_recv, w2_send, w2_recv, w3_send, w3_recv, x_send, x_recv, h_send, h_recv,
):
    me = lax.axis_index("head")
    mine = lax.axis_index("seq")
    tokens, depth = og.shape
    heads = raw_ref.shape[0]
    inner = x_ref.shape[1]
    hdim = inner // heads
    state = b_ref.shape[1]
    per = LANES // hdim
    chips = s // 2
    chip = mine // 2
    odd = lax.rem(mine, 2) == 1
    even = jnp.logical_not(odd)
    right, left = lax.rem(me + 1, n), lax.rem(me + n - 1, n)
    has_right, has_left = me < n - 1, me > 0
    tile = min(256, inner)

    def w_copy(offset):
        where = pl.ds(pl.multiple_of(lax.rem(me + offset, n) * depth, depth), depth)
        return pltpu.make_async_copy(w_out.at[:, where], wo.at[:, where], wo_sem.at[offset])

    wi_copy = pltpu.make_async_copy(w_in, wi, wi_sem)
    w_order = [0]
    for d in range(n - 1):
        for offset in (n - 1 - d, d + 1):
            if offset not in w_order:
                w_order.append(offset)
    barrier = pltpu.get_barrier_semaphore()
    for neighbour in (left, right):
        pl.semaphore_signal(barrier, inc=1, device_id={"head": neighbour}, device_id_type=MESH)
    for away in range(1, s):
        pl.semaphore_signal(
            barrier, inc=1, device_id={"seq": lax.rem(mine + away, s)}, device_id_type=MESH
        )
    loads = [
        pltpu.make_async_copy(src, dst, in_sem.at[k])
        for k, (src, dst) in enumerate((
            (raw_hbm, raw_ref), (b_hbm, b_ref), (c_hbm, c_ref), (x_hbm, x_ref),
            (states_hbm, states), (og_hbm, og),
        ))
    ]
    for load in loads:
        load.start()

    pl.semaphore_wait(barrier, 2 + s - 1)

    leans = n >= 4
    out_rows, bc_rows = o_ref.shape[0], obc_ref.shape[0]
    is_end = leans & ((me == 0) | (me == n - 1))
    is_helper = leans & ((me == 1) | (me == n - 2))
    helper = jnp.where(me == 0, 1, n - 2)
    sibling = mine + 1 - 2 * lax.rem(mine, 2)

    def end_of(side):
        return leans & (me == (0 if side == 0 else n - 1))

    def helper_of(side):
        return leans & (me == (1 if side == 0 else n - 2))

    share = wh.shape[0] // s
    cuts = w1_send.shape[0]
    cut = share // cuts

    def lent(place, q):
        return pl.ds(pl.multiple_of(lax.rem(place + s, s) * share + q * cut, cut), cut)

    def w1_copy(q):
        start = jnp.where(me == 0, 2 * out_rows, 0) + mine * share + q * cut
        return remote(
            w_in.at[pl.ds(pl.multiple_of(start, 16), cut)], wh.at[lent(mine, q)],
            w1_send.at[q], w1_recv.at[q], "head", helper,
        )

    def w2_copy(a, q, place):
        return remote(
            wh.at[lent(place, q)], wh.at[lent(place, q)],
            w2_send.at[a - 1, q], w2_recv.at[a - 1, q], "seq", lax.rem(mine + 2 * a, s),
        )

    def w3_copy(a, q, place):
        return remote(
            wh.at[lent(place, q)], wh.at[lent(place, q)],
            w3_send.at[a, q], w3_recv.at[a, q], "seq", sibling,
        )

    parts = pieces_of(depth, LANES, 4)
    width = depth // parts

    def g_copy(side, d, q):
        where = pl.ds(q * width, width)
        src = og_hbm.at[:, where] if d == 0 else held.at[side, d - 1, :, where]
        return remote(
            src, held.at[side, d, :, where], g_send.at[side, d, q], g_recv.at[side, d, q],
            "head", right if side == 0 else left,
        )

    def g_sends(side, d):
        return (has_right & (me >= d)) if side == 0 else (has_left & (me + d <= n - 1))

    def g_gets(side, d):
        return (me > d) if side == 0 else (me + 1 + d <= n - 1)

    for side in (0, 1):
        @pl.when(g_sends(side, 0))
        def _():
            for q in range(parts):
                g_copy(side, 0, q).start()

    for offset in w_order:
        w_copy(offset).start()
    wi_copy.start()
    for load in loads:
        load.wait()

    def column_of(row):
        at = lax.broadcasted_iota(jnp.int32, (heads, heads), 0)
        along = lax.broadcasted_iota(jnp.int32, (heads, heads), 1)
        return jnp.sum(jnp.where(at == along, row, 0.0), axis=1, keepdims=True)

    bias = column_of(bias_ref[...])
    rate = jnp.exp(column_of(alog_ref[...]))
    skip = column_of(skip_ref[...])
    first = lax.broadcasted_iota(jnp.int32, (tokens, tokens), 0)
    second = lax.broadcasted_iota(jnp.int32, (tokens, tokens), 1)
    upto = (first <= second).astype(F32)
    raw = raw_ref[...] + bias
    step = jnp.maximum(raw, 0.0) + jnp.log1p(jnp.exp(-jnp.abs(raw)))
    log_step = -rate * step
    cum = dot(log_step, upto, precision=EXACT)
    total = cum[:, tokens - 1 : tokens]
    end_decay = jnp.exp(total - cum)
    start_decay = jnp.exp(cum)
    end_total = jnp.exp(total)
    end_weight = step * end_decay
    rows_step[...] = step
    rows_cum[...] = cum
    et_own[...] = jnp.broadcast_to(end_total, et_own.shape)

    def et_copy(away):
        return remote(
            et_own, et_in.at[away - 1], et_send.at[away - 1], et_recv.at[away - 1],
            "seq", lax.rem(mine + s - away, s),
        )

    for away in range(1, s):
        et_copy(away).start()

    eye = (first == second).astype(F32)
    cols[0] = dot(eye, cum, LAST, precision=EXACT)
    cols[1] = dot(eye, step, LAST, precision=EXACT)
    shared[0] = dot(b_ref[...], c_ref[...], LAST)
    shared[1] = jnp.zeros((tokens, tokens), F32)
    lane = lax.broadcasted_iota(jnp.int32, (tokens, heads), 1)

    def masks(h, carry):
        col = jnp.sum(jnp.where(lane == h, cols[0], 0.0), axis=1, keepdims=True)
        col_step = jnp.sum(jnp.where(lane == h, cols[1], 0.0), axis=1, keepdims=True)
        gap = rows_cum[pl.ds(h, 1), :] - col
        value = jnp.where(first <= second, jnp.exp(jnp.minimum(gap, 0.0)) * col_step, 0.0)
        mask[h] = value
        km[h] = (shared[0] * value).astype(BF16)
        return carry

    lax.fori_loop(0, heads, masks, 0)
    eye_bf = eye[:tile, :tile].astype(BF16)
    for k in range(inner // tile):
        where = pl.ds(k * tile, tile)
        xt[where, :] = dot(eye_bf, x_ref[:, where], LAST).astype(BF16)
        ysta[where, :] = dot(states[0, where, :], c_ref[...], LAST)
    ct = dot(eye_bf[:state, :state], c_ref[...], LAST).astype(BF16)
    bt = dot(eye_bf[:state, :state], b_ref[...], LAST).astype(BF16)
    sbt = dot(eye_bf[:state, :state], states[0], LAST).astype(BF16)

    def multiply(source, offset, start, extent, fresh):
        if start == 0:
            w_copy(offset).wait()
        base = lax.rem(me + offset, n) * depth + start
        where = pl.ds(pl.multiple_of(base, extent), extent)

        def body(k, carry):
            outs = pl.ds(pl.multiple_of(k * tile, tile), tile)
            part = dot(wo[outs, where], source[:, pl.ds(start, extent)], LAST)
            acc[outs, :] = part if fresh else acc[outs, :] + part
            return carry

        lax.fori_loop(0, inner // tile, body, 0)

    multiply(og, 0, 0, depth, True)
    for side in (0, 1):
        @pl.when(end_of(side))
        def _():
            for q in range(parts):
                g_copy(side, 0, q).wait_send()
            for q in range(cuts):
                w1_copy(q).start()

    for d in range(n - 1):
        for q in range(parts):
            for side in (0, 1):
                @pl.when(g_gets(side, d))
                def _():
                    g_copy(side, d, q).wait_recv()
                if d + 1 < n - 1:
                    @pl.when(g_gets(side, d) & g_sends(side, d + 1))
                    def _():
                        g_copy(side, d + 1, q).start()
            if d == 1 and q < cuts:
                @pl.when(is_helper)
                def _():
                    w1_copy(q).wait_recv()
                    for a in range(1, chips):
                        w2_copy(a, q, mine).start()
                    w3_copy(0, q, mine).start()
            for side in (0, 1):
                @pl.when(g_gets(side, d))
                def _():
                    offset = n - 1 - d if side == 0 else d + 1
                    multiply(held.at[side, d], offset, q * width, width, False)

    shares = 4 if heads % 4 == 0 else 1
    group = heads // shares

    def share_rows(k):
        return pl.ds(k * group * hdim, group * hdim)

    def l_copy(k):
        return remote(
            lb.at[share_rows(k)], lin.at[share_rows(k)], l_send.at[k], l_recv.at[k],
            "seq", sibling,
        )

    def t_copy(k):
        return remote(
            tb.at[share_rows(k)], tin.at[share_rows(k)], t_send.at[k], t_recv.at[k],
            "seq", sibling,
        )

    for k in range(shares):
        for h in range(k * group, (k + 1) * group):
            rows = pl.ds(h * hdim, hdim)
            rounded = acc[rows, :].astype(BF16)
            dy[rows, :] = rounded
            dyd[rows, :] = (rounded.astype(F32) * start_decay[h : h + 1, :]).astype(BF16)
        where = share_rows(k)
        value = dot(dyd[where, :], c_ref[...])
        lf[where, :] = value
        lb[where, :] = value.astype(BF16)

        @pl.when(odd)
        def _():
            l_copy(k).start()

    def hand_over(low, high):
        @pl.when(is_helper)
        def _():
            for q in range(low, high):
                for a in range(1, chips):
                    w2_copy(a, q, mine - 2 * a).wait_recv()
                    w3_copy(a, q, mine - 2 * a).start()

    for away in range(1, s):
        et_copy(away).wait_recv()
    weight = jnp.ones((heads, LANES), F32)
    for a in range(1, chips):
        reach[a - 1] = weight
        weight = weight * et_in[2 * a - 1] * et_in[2 * a]

    half_lane = lax.broadcasted_iota(jnp.int32, (tokens, LANES), 1) // hdim

    def intra_heads(pair, carry):
        block = pl.ds(pl.multiple_of(pair * LANES, LANES), LANES)
        x_pair = x_ref[:, block]
        dy_pair = dy[block, :]
        for sub in range(per):
            h = pair * per + sub
            rows = pl.ds(pl.multiple_of(h * hdim, hdim), hdim)
            dots = dot(jnp.where(half_lane == sub, x_pair, jnp.zeros_like(x_pair)), dy_pair)
            shared[1] += dots * mask[h]
            rows_r[pl.ds(h, 1), :] = jnp.sum(dots * km[h].astype(F32), axis=0, keepdims=True)
            dy_h = dy[rows, :]
            x_h = xt[rows, :].astype(F32)
            inside = dot(dy_h, km[h], LAST)
            intra[rows, :] = inside
            wide = dy_h.astype(F32)
            rows_xi[pl.ds(h, 1), :] = jnp.sum(x_h * inside, axis=0, keepdims=True)
            rows_st[pl.ds(h, 1), :] = jnp.sum(wide * ysta[rows, :], axis=0, keepdims=True)
            rows_dx[pl.ds(h, 1), :] = jnp.sum(wide * x_h, axis=0, keepdims=True)
        return carry

    pairs = heads // per
    early = 0
    lax.fori_loop(0, early, intra_heads, 0)

    def st_copy(a, k):
        return remote(
            sb.at[share_rows(k)], sin.at[a - 1, share_rows(k)],
            st_send.at[a - 1, k], st_recv.at[a - 1, k], "seq", jnp.maximum(mine - 2 * a, 0),
        )

    def over_heads(k, do):
        def body(h, carry):
            do(h, pl.ds(pl.multiple_of(h * hdim, hdim), hdim))
            return carry

        lax.fori_loop(k * group, (k + 1) * group, body, 0)

    for k in range(shares):
        @pl.when(even)
        def _():
            l_copy(k).wait_recv()

            def join(h, rows):
                sb[rows, :] = (
                    lf[rows, :] + et_own[pl.ds(h, 1), :] * lin[rows, :].astype(F32)
                ).astype(BF16)
                tf[rows, :] = jnp.zeros((hdim, state), F32)

            over_heads(k, join)

        for a in range(1, chips):
            @pl.when(even & (chip >= a))
            def _():
                st_copy(a, k).start()

        middle = pairs if k == shares - 1 else (early + pairs) // 2
        lax.fori_loop(early, middle, intra_heads, 0)
        early = middle

    hand_over(0, cuts * 3 // 4)

    halves = xg.shape[0]
    span = tokens // halves

    def x_copy(half, k):
        return remote(
            xg.at[half, share_rows(k)], xe.at[half, share_rows(k)],
            x_send.at[half, k], x_recv.at[half, k], "head", helper,
        )

    def x_grads(half, k):
        where = pl.ds(half * span, span)
        for h in range(k * group, (k + 1) * group):
            rows = pl.ds(h * hdim, hdim)
            xg[half, rows, :] = (
                intra[rows, where]
                + end_weight[h : h + 1, half * span : (half + 1) * span] * back[rows, where]
                + skip[h : h + 1, :] * dy[rows, where].astype(F32)
            ).astype(BF16)

    for k in range(shares):
        for a in range(1, chips):
            @pl.when(even & (chip + a < chips))
            def _():
                st_copy(a, k).wait_recv()

                def add(h, rows):
                    tf[rows, :] += (
                        reach[a - 1, pl.ds(h, 1), :] * sin[a - 1, rows, :].astype(F32)
                    )

                over_heads(k, add)

        @pl.when(even)
        def _():
            tb[share_rows(k), :] = tf[share_rows(k), :].astype(BF16)
            t_copy(k).start()

            def enter(h, rows):
                carried[rows, :] = (
                    lin[rows, :].astype(F32) + et_in[0, pl.ds(h, 1), :] * tf[rows, :]
                )

            over_heads(k, enter)

        @pl.when(odd)
        def _():
            t_copy(k).wait_recv()
            carried[share_rows(k), :] = tin[share_rows(k), :].astype(F32)

        back[share_rows(k), :] = dot(carried[share_rows(k), :].astype(BF16), b_ref[...], LAST)
        x_grads(0, k)

        @pl.when(is_end)
        def _():
            x_copy(0, k).start()

    for half in range(1, halves):
        for k in range(shares):
            x_grads(half, k)

            @pl.when(is_end)
            def _():
                x_copy(half, k).start()

    wi_copy.wait()

    hand_over(cuts * 3 // 4, cuts)

    @pl.when(is_helper)
    def _():
        for q in range(cuts):
            for a in range(chips):
                w3_copy(a, q, sibling - 2 * a).wait_recv()

    strips = s_send.shape[2] // halves
    splits = strips * halves
    piece = out_rows // strips

    def s_copy(side, e, k, strip):
        rows = pl.ds(pl.multiple_of(strip * piece, piece), piece)
        q = k * strips + strip
        return remote(
            going.at[side, e, k, rows], coming.at[side, e, k, rows],
            s_send.at[side, e, q], s_recv.at[side, e, q], "head", right if side == 0 else left,
        )

    def b_copy(side, e):
        return remote(
            gbc.at[side, e], cbc.at[side, e], b_send.at[side, e], b_recv.at[side, e],
            "head", right if side == 0 else left,
        )

    leant = (n - 2) * bc_rows

    def h_copy():
        start = pl.multiple_of(jnp.where(me == 0, 2 * bc_rows, 0), bc_rows)
        return remote(own_bc.at[pl.ds(start, leant)], hbc, h_send, h_recv, "head", helper)

    def owner_of(side, e):
        return n - 1 - e if side == 0 else e

    def s_sends(side, e):
        return (me < owner_of(side, e)) if side == 0 else (me > owner_of(side, e))

    def s_gets(side, e):
        return (s_sends(side, e) | (me == owner_of(side, e))) & (has_left if side == 0 else has_right)

    def term(owner, k, strip):
        start = pl.multiple_of(owner * out_rows + strip * piece, piece)
        return dot(wi[pl.ds(start, piece), :], xg[k])

    count = (n - 1) * splits

    def bc_of(owner):
        return own_bc[pl.ds(pl.multiple_of(owner * bc_rows, bc_rows), bc_rows), :]

    def slot(index, carry):
        for side in (0, 1):
            place = index - SKEW * (me if side == 0 else n - 1 - me)
            held_at = jnp.clip(place, 0, count - 1)
            e, q = lax.div(held_at, splits), lax.rem(held_at, splits)
            k, strip = lax.div(q, strips), lax.rem(q, strips)
            owner = owner_of(side, e)
            live = (place >= 0) & (place < count)
            rows = pl.ds(pl.multiple_of(strip * piece, piece), piece)
            sends = live & s_sends(side, e)
            aided = helper_of(side) & (e < n - 2)
            far = owner - 2 if side == 0 else owner
            passes = jnp.logical_not(end_of(side) & (e < n - 2))
            gets = s_gets(side, e) & jnp.logical_not(aided)
            closes = q == splits - 1

            @pl.when(sends & passes)
            def _():
                going[side, e, k, rows, :] = term(owner, k, strip).astype(BF16)

                for one in range(halves):
                    @pl.when(helper_of(side) & (place == one * strips))
                    def _():
                        for part in range(shares):
                            x_copy(one, part).wait_recv()

                @pl.when(aided)
                def _():
                    start = pl.multiple_of(far * out_rows + strip * piece, piece)
                    aid = dot(wh[pl.ds(start, piece), :], xe[k])
                    going[side, e, k, rows, :] = (
                        going[side, e, k, rows, :].astype(F32) + aid
                    ).astype(BF16)

                @pl.when(gets)
                def _():
                    s_copy(side, e, k, strip).wait_recv()
                    going[side, e, k, rows, :] = (
                        going[side, e, k, rows, :].astype(F32)
                        + coming[side, e, k, rows, :].astype(F32)
                    ).astype(BF16)

                s_copy(side, e, k, strip).start()

            @pl.when(sends & passes & closes)
            def _():
                gbc[side, e] = bc_of(owner)

                @pl.when(helper_of(side) & (place == splits - 1))
                def _():
                    h_copy().wait_recv()

                @pl.when(aided)
                def _():
                    start = pl.multiple_of(far * bc_rows, bc_rows)
                    gbc[side, e] = (
                        gbc[side, e].astype(F32) + hbc[pl.ds(start, bc_rows), :].astype(F32)
                    ).astype(BF16)

                @pl.when(gets)
                def _():
                    b_copy(side, e).wait_recv()
                    gbc[side, e] = (
                        gbc[side, e].astype(F32) + cbc[side, e].astype(F32)
                    ).astype(BF16)

                b_copy(side, e).start()

            @pl.when(live & (me == owner) & gets)
            def _():
                s_copy(side, e, k, strip).wait_recv()
                where = pl.ds(pl.multiple_of(k * span, span), span)
                acc[rows, where] += coming[side, e, k, rows, :].astype(F32)

                @pl.when(closes)
                def _():
                    b_copy(side, e).wait_recv()
                    acc_bc[...] += cbc[side, e].astype(F32)

        return carry

    lax.fori_loop(0, SKEW, slot, 0)

    for h in range(heads):
        rows = pl.ds(h * hdim, hdim)
        x_h = xt[rows, :].astype(F32)
        xend[rows, :] = (x_h * end_weight[h : h + 1, :]).astype(BF16)
        rows_xs[h : h + 1, :] = jnp.sum(x_h * back[rows, :], axis=0, keepdims=True)
        rows_tail[h : h + 1, :] = jnp.sum(
            states[0, rows, :].astype(F32) * carried[rows, :], axis=0, keepdims=True
        )
    sums = shared[1].astype(BF16)
    carried_t = dot(eye_bf[:state, :state], carried[...].astype(BF16), LAST).astype(BF16)
    own_bc[:state, :] = (dot(ct, sums, LAST) + dot(carried_t, xend[...])).astype(BF16)
    own_bc[state:, :] = (dot(bt, sums) + dot(sbt, dyd[...])).astype(BF16)

    @pl.when(is_end)
    def _():
        for part in range(shares):
            x_copy(0, part).wait_send()
        h_copy().start()

    acc_bc[...] = bc_of(me).astype(F32)
    for k in range(halves):
        for strip in range(strips):
            acc[pl.ds(strip * piece, piece), pl.ds(k * span, span)] = term(me, k, strip)
    slots = max((n - k) * splits + SKEW * k for k in range(1, n))
    first_part = min(slots, SKEW + 3)
    lax.fori_loop(SKEW, first_part, slot, 0)

    end_terms = end_weight * rows_xs[...]
    cum_grad = rows_r[...] - rows_xi[...] + start_decay * rows_st[...] - end_terms
    tail = jnp.sum(end_terms, axis=1, keepdims=True) + end_total * jnp.sum(
        rows_tail[...], axis=1, keepdims=True
    )
    token = lax.broadcasted_iota(jnp.int32, (heads, tokens), 1)
    cum_grad = cum_grad + jnp.where(token == tokens - 1, tail, 0.0)
    step_grad = dot(cum_grad, upto, LAST, precision=EXACT)
    dt_sum = -rate * step_grad + (rows_xi[...] + end_terms) / step
    dt_grad = dt_sum / (1.0 + jnp.exp(-raw))
    odt_ref[...] = dt_grad
    writes = [
        pltpu.make_async_copy(src, dst, out_sem.at[k])
        for k, (src, dst) in enumerate((
            (o_ref, o_hbm), (obc_ref, obc_hbm), (odt_ref, odt_hbm), (opar_ref, opar_hbm),
        ))
    ]
    writes[2].start()

    def row_of(column):
        at = lax.broadcasted_iota(jnp.int32, (heads, LANES), 0)
        along = lax.broadcasted_iota(jnp.int32, (heads, LANES), 1)
        return jnp.sum(jnp.where(at == along, column, 0.0), axis=0, keepdims=True)

    line = lax.broadcasted_iota(jnp.int32, (8, LANES), 0)
    packet = jnp.zeros((8, LANES), F32)
    for index, terms in enumerate((step_grad * log_step, rows_dx[...], dt_grad)):
        packet = jnp.where(line == index, row_of(jnp.sum(terms, axis=1, keepdims=True)), packet)
    par[...] = packet

    def p_copy(away):
        return remote(
            par, par_in.at[away - 1], p_send.at[away - 1], p_recv.at[away - 1],
            "seq", lax.rem(mine + s - away, s),
        )

    for away in range(1, s):
        p_copy(away).start()

    @pl.when(is_end)
    def _():
        for half in range(1, halves):
            for part in range(shares):
                x_copy(half, part).wait_send()

    lax.fori_loop(first_part, slots, slot, 0)

    o_ref[...] = acc[:out_rows, :].astype(BF16)
    writes[0].start()
    obc_ref[...] = acc_bc[...].astype(BF16)
    writes[1].start()
    value = packet
    for away in range(1, s):
        p_copy(away).wait_recv()
        value = value + par_in[away - 1]
    opar_ref[...] = value[: opar_ref.shape[0], :heads] * scale
    writes[3].start()

    for side in (0, 1):
        for d in range(n - 1):
            @pl.when(g_sends(side, d) & (jnp.logical_not(end_of(side)) if d == 0 else True))
            def _():
                for q in range(parts):
                    g_copy(side, d, q).wait_send()

            skipped = end_of(side) if d < n - 2 else False

            @pl.when(s_sends(side, d) & jnp.logical_not(skipped))
            def _():
                for k in range(halves):
                    for strip in range(strips):
                        s_copy(side, d, k, strip).wait_send()
                b_copy(side, d).wait_send()

    @pl.when(is_end)
    def _():
        for q in range(cuts):
            w1_copy(q).wait_send()
        h_copy().wait_send()

    @pl.when(is_helper)
    def _():
        for q in range(cuts):
            for a in range(chips):
                if a > 0:
                    w2_copy(a, q, mine).wait_send()
                w3_copy(a, q, mine - 2 * a).wait_send()

    for away in range(1, s):
        et_copy(away).wait_send()
        p_copy(away).wait_send()

    for k in range(shares):
        @pl.when(odd)
        def _():
            l_copy(k).wait_send()

        for a in range(1, chips):
            @pl.when(even & (chip >= a))
            def _():
                st_copy(a, k).wait_send()

        @pl.when(even)
        def _():
            t_copy(k).wait_send()
    for write in writes:
        write.wait()


def hand_on_kernel(*refs):
    count = len(refs) // 2
    for k in range(count):
        refs[count + k][...] = refs[k][...]


def handed_on(arrays):
    vmem = pl.BlockSpec(memory_space=pltpu.VMEM)
    return pl.pallas_call(
        hand_on_kernel,
        out_shape=tuple(jax.ShapeDtypeStruct(a.shape, a.dtype) for a in arrays),
        in_specs=[vmem] * len(arrays),
        out_specs=(vmem,) * len(arrays),
        name="hand_on",
    )(*arrays)


def layer(og, x, b, c, raw, bias, alog, skip, states, w_out, w_in):
    n, s = lax.axis_size("head"), lax.axis_size("seq")
    tokens, depth = og.shape
    inner = x.shape[1]
    heads = raw.shape[0]
    hdim = inner // heads
    state = b.shape[1]
    out_rows = w_in.shape[0] // n
    bc_rows = 2 * state // n
    chips = s // 2
    scale = (s * tokens * hdim) ** (-0.5)
    vmem = pl.BlockSpec(memory_space=pltpu.VMEM)
    hbm = pl.BlockSpec(memory_space=pltpu.HBM)
    dma = pltpu.SemaphoreType.DMA
    parts = pieces_of(depth, LANES, 4)
    halves = 2 if tokens % (2 * LANES) == 0 else 1
    splits = pieces_of(out_rows, 16, 2) * halves
    lent = max(n - 2, 1) * out_rows
    cuts = pieces_of(lent // s, 16, parts)
    leant = max(n - 2, 1) * bc_rows

    def wide(dtype):
        return pltpu.VMEM((inner, tokens), dtype)

    def slim(dtype, *lead):
        return pltpu.VMEM((*lead, inner, state), dtype)

    results = (
        jax.ShapeDtypeStruct((out_rows, tokens), BF16),
        jax.ShapeDtypeStruct((bc_rows, tokens), BF16),
        jax.ShapeDtypeStruct((heads, tokens), F32),
        jax.ShapeDtypeStruct((3, heads), F32),
    )
    rows = pltpu.VMEM((heads, tokens), F32)
    packet = pltpu.VMEM((2, n - 1, halves, out_rows, tokens // halves), BF16)
    bc_packet = pltpu.VMEM((2, n - 1, bc_rows, tokens), BF16)
    shared_x = pltpu.VMEM((halves, inner, tokens // halves), BF16)
    scratch = [
        pltpu.VMEM(w_out.shape, BF16),
        pltpu.VMEM(w_in.shape, BF16),
        pltpu.VMEM((2, n - 1, tokens, depth), BF16),
        wide(F32), wide(BF16), wide(BF16), wide(BF16),
        pltpu.VMEM((heads, tokens, tokens), F32),
        pltpu.VMEM((heads, tokens, tokens), BF16),
        wide(F32), wide(F32), wide(F32), wide(BF16), shared_x,
        packet, packet,
        pltpu.VMEM((2 * state, tokens), BF16),
        slim(F32), slim(BF16), slim(BF16), slim(BF16), slim(BF16, chips - 1),
        slim(F32), slim(BF16), slim(BF16), slim(F32),
        pltpu.VMEM((heads, LANES), F32),
        pltpu.VMEM((s - 1, heads, LANES), F32),
        pltpu.VMEM((chips - 1, heads, LANES), F32),
        rows, rows, rows, rows, rows, rows, rows, pltpu.VMEM((heads, state), F32),
        pltpu.VMEM((2, tokens, heads), F32),
        pltpu.VMEM((2, tokens, tokens), F32),
        pltpu.VMEM((8, LANES), F32),
        pltpu.VMEM((s - 1, 8, LANES), F32),
        pltpu.VMEM((bc_rows, tokens), F32), bc_packet, bc_packet,
        pltpu.VMEM((lent, inner), BF16), shared_x, pltpu.VMEM((leant, tokens), BF16),
        *[pltpu.VMEM(a.shape, a.dtype) for a in results],
        *[pltpu.VMEM(a.shape, a.dtype) for a in (og, x, b, c, raw, states)],
        dma((6,)), dma((4,)), dma((2, n - 1, parts)), dma((2, n - 1, parts)), dma((n,)), dma,
        dma((2, n - 1, splits)), dma((2, n - 1, splits)),
        dma((s - 1,)), dma((s - 1,)),
        dma((4,)), dma((4,)), dma((chips - 1, 4)), dma((chips - 1, 4)), dma((4,)), dma((4,)),
        dma((s - 1,)), dma((s - 1,)),
        dma((2, n - 1)), dma((2, n - 1)), dma((cuts,)), dma((cuts,)),
        dma((chips - 1, cuts)), dma((chips - 1, cuts)), dma((chips, cuts)), dma((chips, cuts)),
        dma((halves, 4)), dma((halves, 4)), dma, dma,
    ]
    outs = pl.pallas_call(
        functools.partial(layer_kernel, n, s, scale),
        out_shape=results,
        in_specs=[hbm] * 5 + [vmem] * 3 + [hbm] * 3,
        out_specs=(hbm,) * 4,
        scratch_shapes=scratch,
        compiler_params=pltpu.CompilerParams(
            collective_id=0, has_side_effects=True, vmem_limit_bytes=58 * 2**20
        ),
        name="layer",
    )(og, x, b, c, raw, bias[None], alog[None], skip[None], states, w_out, w_in)
    return handed_on(outs)


def solution(mesh):
    return jax.shard_map(
        layer,
        mesh=mesh,
        in_specs=(
            P("seq", "head"),
            P("seq", "head"),
            P("seq", None),
            P("seq", None),
            P("head", "seq"),
            P("head"),
            P("head"),
            P("head"),
            P("seq", "head", None),
            P("head", None),
            P(None, "head"),
        ),
        out_specs=(P("head", "seq"), P("head", "seq"), P("head", "seq"), P(None, "head")),
        check_vma=False,
    )
```
